256 devices in a mesh: dp: 8 (over y, core), seq: 32 (over x, z).
Axes of the slice: x: 4, y: 4, z: 8, core: 2. Of those that a mesh axis runs over, the one named last changes fastest.
Arguments:
- token_ids: int32 [8, 4096], P('dp', 'seq'), may hold values from 0 to 255
- cotangent: bfloat16 [8, 4096, 768], P('dp', 'seq'), may hold values from -6 to 6
- table: bfloat16 [256, 768], replicated, may hold values from -12 to 12
- w_query: bfloat16 [768, 768], replicated, may hold values from -2 to 2
- w_key: bfloat16 [768, 768], replicated, may hold values from -2 to 2
- w_value: bfloat16 [768, 768], replicated, may hold values from -0.21875 to 0.21875
- w_out: bfloat16 [768, 768], replicated, may hold values from -0.21875 to 0.21875
- window: int32 [12], replicated, may hold values from 64 to 512, as said below
Outputs:
- grad_input: bfloat16 [8, 4096, 768], P('dp', 'seq')
- weight_grads: float32 [3072, 768], P('seq')
The draws below stay inside these ranges and needn't reach their ends.
Inputs may be any that keep to these rules, and one draw needn't show every extreme that they name: Some head's window is exactly 512.
All inputs are finite; a program needn't handle non-finite values.
Results may differ from the reference program's by a relative error of at most 0.025.
Values may be sent and summed in bfloat16 or wider, within the bound.
A program may use at most 128 MiB of HBM per device.

```python
import math
import jax
import jax.numpy as jnp
import numpy as np
from jax import lax

D = 768
HEADS = 12
HEAD_DIM = 64
VOCAB = 256
WINDOW = 512
SEQ = 4096
SEQS = 8


def draw_table(key, part):
    normal_part = jax.random.normal(jax.random.fold_in(key, 11), (VOCAB, D), jnp.float32)
    base_values = normal_part
    log_scale = jax.random.uniform(jax.random.fold_in(key, 12), (VOCAB, 1), jnp.float32, jnp.log(0.3), jnp.log(3.0))
    return jnp.clip(base_values * jnp.exp(log_scale), -12.0, 12.0).astype(jnp.bfloat16)


def paired_weight(key, which):
    own_part = jax.random.normal(jax.random.fold_in(key, 22 + which), (D, D), jnp.float32)
    mixed = own_part
    return jnp.clip(mixed * D ** (-0.5), -2.0, 2.0)


def draw_w_query(key, part):
    return paired_weight(key, 0).astype(jnp.bfloat16)


def draw_w_key(key, part):
    return paired_weight(key, 1).astype(jnp.bfloat16)


def draw_window(key, part):
    widths = jax.random.randint(jax.random.fold_in(key, 31), (HEADS,), WINDOW // 8, WINDOW + 1)
    chosen = jax.random.randint(jax.random.fold_in(key, 32), (), 0, HEADS)
    return jnp.where(jnp.arange(HEADS, dtype=jnp.int32) == chosen, WINDOW, widths).astype(jnp.int32)


def set_ends(result, rng, low, largest):
    longest = result.shape.index(max(result.shape))
    spots = []
    for shift in (0, 1):
        where = [jax.random.randint(jax.random.fold_in(rng, axis), (), 0, length) for axis, length in enumerate(result.shape)]
        where[longest] = (where[longest] + shift) % result.shape[longest]
        spots.append(tuple(where))
    return result.at[spots[0]].set(low).at[spots[1]].set(largest)


def level_of(key, dims, split, least, top_value):
    def one(dim, blocks):
        steps = jax.random.uniform(jax.random.fold_in(jax.random.fold_in(key, 6), dim), (blocks,), jnp.float32, least / len(split), top_value / len(split))
        return jnp.repeat(jnp.exp(steps), dims[dim] // blocks).reshape((-1,) + (1,) * (len(dims) - dim - 1))

    loudness = one(*split[0])
    for cut in split[1:]:
        loudness = loudness * one(*cut)
    return loudness


def rank_table(count, lean):
    weights = [(1 << 20) // math.isqrt(rank ** lean) + 1 for rank in range(1, count + 1)]
    width = 1 + sum(weights) // (1 << 30)
    return np.cumsum(np.array([max(1, weight // width) for weight in weights]))


def skewed_ids(own_key, dims, number_of, lean):
    grid = rank_table(number_of, lean)
    ticket = jax.random.randint(jax.random.fold_in(own_key, 1), dims, 0, int(grid[number_of - 1]))
    standing = jnp.searchsorted(jnp.asarray(grid, jnp.int32), ticket, side="right")
    return jax.random.permutation(jax.random.fold_in(own_key, 2), number_of)[standing].astype(jnp.int32)


def scatter_about(stream_key, shape, scale, most, cuts=(), kind=jnp.bfloat16):
    values = scale * jax.random.normal(stream_key, shape, jnp.float32)
    if cuts:
        values = values * level_of(stream_key, shape, cuts, -0.22, 0.18)
    return jnp.clip(values, -most, most).astype(kind)


def setup_inputs(seed: int = 0) -> dict:
    keys = jax.random.split(jax.random.key(seed), 9)
    token_ids = set_ends(skewed_ids(keys[0], (SEQS, SEQ), VOCAB, 2), jax.random.fold_in(keys[0], 3), 0, VOCAB - 1).astype(jnp.int32)
    cotangent = scatter_about(keys[1], (SEQS, SEQ, D), 1.0, 6.0, ((0, 8), (1, 32)))
    table = draw_table(jax.random.fold_in(keys[8], 71), 0)
    w_query = draw_w_query(jax.random.fold_in(keys[8], 71), 0)
    w_key = draw_w_key(jax.random.fold_in(keys[8], 71), 0)
    w_value = scatter_about(keys[5], (D, D), D ** -0.5, 0.21875)
    w_out = scatter_about(keys[6], (D, D), D ** -0.5, 0.21875)
    window = draw_window(jax.random.fold_in(keys[8], 71), 0)
    return {"token_ids": token_ids, "cotangent": cotangent, "table": table, "w_query": w_query, "w_key": w_key, "w_value": w_value, "w_out": w_out, "window": window}


EPSILON = 1e-05

def rotate(values, positions):
    row_count = values.shape[0]
    shaped = values.reshape(row_count, -1, HEAD_DIM)
    middle = HEAD_DIM // 2
    frequency = 10000.0 ** (-2.0 * jnp.arange(middle, dtype=jnp.float32) / HEAD_DIM)
    angles = positions.astype(jnp.float32)[:, None] * frequency[None, :]
    cosine = jnp.cos(angles)[:, None, :]
    sine_part = jnp.sin(angles)[:, None, :]
    former = shaped[..., :middle]
    latter = shaped[..., middle:]
    turned = jnp.concatenate([former * cosine - latter * sine_part, latter * cosine + former * sine_part], axis=-1)
    return turned.reshape(row_count, -1)

def unrotate(values, positions):
    row_count = values.shape[0]
    shaped = values.reshape(row_count, -1, HEAD_DIM)
    middle = HEAD_DIM // 2
    frequency = 10000.0 ** (-2.0 * jnp.arange(middle, dtype=jnp.float32) / HEAD_DIM)
    angles = positions.astype(jnp.float32)[:, None] * frequency[None, :]
    cosine = jnp.cos(angles)[:, None, :]
    sine_part = jnp.sin(angles)[:, None, :]
    former = shaped[..., :middle]
    latter = shaped[..., middle:]
    turned = jnp.concatenate([former * cosine + latter * sine_part, latter * cosine - former * sine_part], axis=-1)
    return turned.reshape(row_count, -1)

def tdot(left, right):
    return lax.dot_general(left, right, (((0,), (0,)), ((), ())), preferred_element_type=jnp.float32)

def ndot(left, right):
    return lax.dot_general(left, right, (((1,), (1,)), ((), ())), preferred_element_type=jnp.float32)

def reference(token_ids, cotangent, table, w_query, w_key, w_value, w_out, window):
    score_scale = HEAD_DIM ** (-0.5)
    block_rows = min(512, SEQ)
    block_count = SEQ // block_rows
    positions = jnp.arange(SEQ, dtype=jnp.int32)

    def one_sequence(pair):
        byte_ids, grad_out = pair
        embedded = table[byte_ids]
        widened = embedded.astype(jnp.float32)
        inv_rms = lax.rsqrt(lax.optimization_barrier(jnp.mean(widened * widened, axis=1, keepdims=True)) + EPSILON)
        normed = (widened * inv_rms).astype(jnp.bfloat16)
        query = rotate(jnp.dot(normed, w_query, preferred_element_type=jnp.float32), positions).astype(jnp.bfloat16)
        key_rows = rotate(jnp.dot(normed, w_key, preferred_element_type=jnp.float32), positions).astype(jnp.bfloat16)
        value_rows = jnp.dot(normed, w_value, preferred_element_type=jnp.float32).astype(jnp.bfloat16)
        grad_att = ndot(grad_out, w_out).astype(jnp.bfloat16)
        padding = jnp.zeros((WINDOW, D), jnp.bfloat16)
        key_pad = jnp.concatenate([padding, key_rows], axis=0)
        value_pad = jnp.concatenate([padding, value_rows], axis=0)

        def one_block(carry, block_index):
            grad_keys, grad_values = carry
            start = (block_index * block_rows).astype(jnp.int32)
            span_rows = WINDOW + block_rows
            query_heads = lax.dynamic_slice_in_dim(query, start, block_rows, 0).astype(jnp.float32).reshape(block_rows, HEADS, HEAD_DIM)
            key_heads = lax.dynamic_slice_in_dim(key_pad, start, span_rows, 0).astype(jnp.float32).reshape(span_rows, HEADS, HEAD_DIM)
            value_heads = lax.dynamic_slice_in_dim(value_pad, start, span_rows, 0).astype(jnp.float32).reshape(span_rows, HEADS, HEAD_DIM)
            grad_heads = lax.dynamic_slice_in_dim(grad_att, start, block_rows, 0).astype(jnp.float32).reshape(block_rows, HEADS, HEAD_DIM)
            query_pos = start + jnp.arange(block_rows, dtype=jnp.int32)
            key_pos = start - WINDOW + jnp.arange(span_rows, dtype=jnp.int32)
            distance = query_pos[:, None] - key_pos[None, :]
            allowed = (distance[None] >= 0) & (distance[None] < window[:, None, None]) & (key_pos[None, None, :] >= 0)
            scores = jnp.einsum('qhd,khd->hqk', query_heads, key_heads) * score_scale
            masked = jnp.where(allowed, scores, -1e+30)
            row_max = lax.optimization_barrier(jnp.max(masked, axis=-1, keepdims=True))
            weights = jnp.where(allowed, jnp.exp(masked - row_max), 0.0)
            probs = weights / lax.optimization_barrier(jnp.sum(weights, axis=-1, keepdims=True))
            probs_b = probs.astype(jnp.bfloat16)
            probs_wide = probs_b.astype(jnp.float32)
            attended = jnp.einsum('hqk,khd->qhd', probs_wide, value_heads).astype(jnp.bfloat16).reshape(block_rows, D)
            grad_probs = jnp.einsum('qhd,khd->hqk', grad_heads, value_heads)
            row_term = lax.optimization_barrier(jnp.sum(probs * grad_probs, axis=-1, keepdims=True))
            grad_scores = (probs * (grad_probs - row_term) * score_scale).astype(jnp.bfloat16).astype(jnp.float32)
            grad_query = jnp.einsum('hqk,khd->qhd', grad_scores, key_heads).reshape(block_rows, D)
            part_keys = jnp.einsum('hqk,qhd->khd', grad_scores, query_heads).reshape(span_rows, D)
            part_values = jnp.einsum('hqk,qhd->khd', probs_wide, grad_heads).reshape(span_rows, D)
            slab_keys = lax.dynamic_slice_in_dim(grad_keys, start, span_rows, 0) + part_keys
            slab_values = lax.dynamic_slice_in_dim(grad_values, start, span_rows, 0) + part_values
            grad_keys = lax.dynamic_update_slice_in_dim(grad_keys, slab_keys, start, 0)
            grad_values = lax.dynamic_update_slice_in_dim(grad_values, slab_values, start, 0)
            return ((grad_keys, grad_values), (attended, grad_query))
        empty = jnp.zeros((SEQ + WINDOW, D), jnp.float32)
        (grad_keys, grad_values), (attended, grad_query) = lax.scan(one_block, (empty, empty), jnp.arange(block_count, dtype=jnp.int32))
        attended = attended.reshape(SEQ, D)
        grad_query = grad_query.reshape(SEQ, D)
        grad_q_lin = unrotate(grad_query, positions).astype(jnp.bfloat16)
        grad_k_lin = unrotate(grad_keys[WINDOW:], positions).astype(jnp.bfloat16)
        grad_v_lin = grad_values[WINDOW:].astype(jnp.bfloat16)
        grad_normed = ndot(grad_q_lin, w_query) + ndot(grad_k_lin, w_key) + ndot(grad_v_lin, w_value)
        scaled = widened * inv_rms
        grad_input = (inv_rms * (grad_normed - scaled * lax.optimization_barrier(jnp.mean(grad_normed * scaled, axis=1, keepdims=True)))).astype(jnp.bfloat16)
        term = jnp.concatenate([tdot(normed, grad_q_lin), tdot(normed, grad_k_lin), tdot(normed, grad_v_lin), tdot(attended, grad_out)], axis=0)
        return (grad_input, term)

    def accumulate(total, pair):
        grad_input, term = one_sequence(pair)
        return (total + term, grad_input)
    weight_grads, grad_input = lax.scan(accumulate, jnp.zeros((4 * D, D), jnp.float32), (token_ids, cotangent))
    return (grad_input, weight_grads)
```

```python
import functools

import jax
import jax.numpy as jnp
import numpy as np
from jax import lax
from jax.experimental import pallas as pl
from jax.experimental.pallas import tpu as pltpu
from jax.sharding import PartitionSpec as P

D = 768
HEADS = 12
HEAD_DIM = 64
VOCAB = 256
WINDOW = 512
EPSILON = 1e-05
B = 128
SEQ_DEVS = 32
REACH = WINDOW // B
SPAN = (REACH + 1) * B
PAIRS = D // B
MESH = pl.DeviceIdType.MESH
BF = jnp.bfloat16
F32 = jnp.float32
TERM_ROWS = 3 * VOCAB + D


def rope_tables():
    frequency = 10000.0 ** (-2.0 * np.arange(HEAD_DIM // 2) / HEAD_DIM)
    lane_frequency = np.tile(frequency, 4)[None, :]
    inside = np.arange(B)[:, None] * lane_frequency
    blocks = (np.arange(SEQ_DEVS) * B)[:, None] * lane_frequency
    return [
        np.asarray(part, np.float32)
        for part in (np.cos(inside), np.sin(inside), np.cos(blocks), np.sin(blocks))
    ]


def nn(a, b):
    return lax.dot_general(a, b, (((1,), (0,)), ((), ())), preferred_element_type=F32)


def nt(a, b):
    return lax.dot_general(a, b, (((1,), (1,)), ((), ())), preferred_element_type=F32)


def tn(a, b):
    return lax.dot_general(a, b, (((0,), (0,)), ((), ())), preferred_element_type=F32)


def swap_halves(x):
    lane = lax.broadcasted_iota(jnp.int32, x.shape, 1)
    first = (lane // (HEAD_DIM // 2)) % 2 == 0
    return jnp.where(first, pltpu.roll(x, B - HEAD_DIM // 2, 1), pltpu.roll(x, HEAD_DIM // 2, 1))


def rope(x, cosine, sine):
    return x * cosine + swap_halves(x) * sine


def unrope(x, cosine, sine):
    return x * cosine - swap_halves(x) * sine


def kernel(
    ids_ref, cot_hbm, table_hbm, wq_hbm, wk_hbm, wv_hbm, wo_hbm, window_ref, cr_ref, sr_ref, cb_ref, sb_ref,
    gin_ref, wg_ref,
    ids_all, cot_all, table, wq, wk, wv, wo, ntab, normed, emb, cosv, sinv,
    keys, values, query, gatt, att, gq, gk, gv, onehot_t, statc, stats,
    probs_s, ds_s,
    term, r1, s1, r2, s2, r3, a4, r4, r5,
    load_sem, ids_send, ids_recv, cot_send, cot_recv, st_send, st_recv,
    p1_send, p1_recv, p2_send, p2_recv, p3_send, p3_recv, p4_send, p4_recv, p5_send, p5_recv,
):
    dp = lax.axis_index("dp")
    sq = lax.axis_index("seq")
    x, z = sq // 8, sq % 8
    y, c = dp // 2, dp % 2
    base = sq * B

    loads = [
        pltpu.make_async_copy(src, dst, load_sem.at[i])
        for i, (src, dst) in enumerate(
            [(cot_hbm, cot_all.at[0]), (table_hbm, table), (wk_hbm, wk), (wv_hbm, wv), (wq_hbm, wq), (wo_hbm, wo)]
        )
    ]
    for load in loads:
        load.start()

    def at(new_dp, new_sq):
        return (new_dp, new_sq)

    def seq_of(new_x, new_z):
        return new_x * 8 + new_z

    def shift(distance):
        return lax.rem(sq + distance + SEQ_DEVS, SEQ_DEVS)

    def other_dp(step):
        return lax.rem(dp + step, 8)

    def other_y(step):
        return lax.rem(y + step, 4)

    def other_x(step):
        return lax.rem(x + step, 4)

    def other_z(step):
        return lax.rem(z + step, 8)

    barrier = pltpu.get_barrier_semaphore()
    partners = [at(dp, shift(d)) for d in (1, 2, 3, 4, -1, -2, -3, -4)]
    partners += [at(other_dp(d), sq) for d in range(1, 8)]
    partners += [at(dp, seq_of(other_x(d), z)) for d in range(1, 4)]
    partners += [at(dp, seq_of(x, other_z(d))) for d in range(1, 8)]
    for partner in partners:
        pl.semaphore_signal(barrier, inc=1, device_id=partner, device_id_type=MESH)

    lane_row = lax.broadcasted_iota(jnp.int32, (1, B), 1)
    sign = jnp.where((lane_row // (HEAD_DIM // 2)) % 2 == 0, -1.0, 1.0)

    def rope_block(i, carry):
        block = lax.rem(sq + i - REACH + SEQ_DEVS, SEQ_DEVS)
        cb = cb_ref[pl.ds(block, 1), :]
        sb = sb_ref[pl.ds(block, 1), :]
        rows = pl.ds(pl.multiple_of(i * B, B), B)
        cosv[rows, :] = cr_ref[...] * cb - sr_ref[...] * sb
        sinv[rows, :] = (sr_ref[...] * cb + cr_ref[...] * sb) * sign
        return carry

    lax.fori_loop(0, 2 * REACH + 1, rope_block, 0)

    loads[1].wait()
    rows_f = table[...].astype(F32)
    table_inv = lax.rsqrt(jnp.mean(rows_f * rows_f, axis=1, keepdims=True) + EPSILON)
    ntab[...] = (rows_f * table_inv).astype(BF)

    loads[0].wait()
    pl.semaphore_wait(barrier, len(partners))

    def remote(src, dst, send, recv, device):
        return pltpu.make_async_remote_copy(
            src_ref=src, dst_ref=dst, send_sem=send, recv_sem=recv, device_id=device, device_id_type=MESH
        )

    id_copies = []
    for i, d in enumerate((1, 2, 3, 4, -1, -2, -3, -4)):
        id_copies.append(remote(ids_ref, ids_all.at[d + REACH], ids_send.at[i], ids_recv.at[i], at(dp, shift(-d))))

    def relay(step):
        return remote(
            cot_all.at[step], cot_all.at[step + 1], cot_send.at[step], cot_recv.at[step], at(dp, shift(-1))
        )

    relays = [relay(step) for step in range(REACH)]
    for copy in id_copies:
        copy.start()
    relays[0].start()
    ids_all[REACH] = ids_ref[...]
    for copy in id_copies:
        copy.wait_recv()

    token = lax.broadcasted_iota(jnp.int32, (VOCAB, B), 0)
    onehot_t[...] = (token == ids_ref[...]).astype(BF)
    emb[...] = tn(onehot_t[...], table[...])

    def embed_block(i, carry):
        rows = pl.ds(pl.multiple_of(i * B, B), B)
        hot = (token == ids_all[i]).astype(BF)
        normed[rows, :] = tn(hot, ntab[...]).astype(BF)
        return carry

    lax.fori_loop(0, 2 * REACH + 1, embed_block, 0)

    def project(first, w, out, rotated, scale):
        def slab(j, carry):
            lanes = pl.ds(pl.multiple_of(j * B, B), B)
            got = nn(normed[pl.ds(first, SPAN), :], w[:, lanes])
            if rotated:
                got = rope(got, cosv[pl.ds(first, SPAN), :], sinv[pl.ds(first, SPAN), :])
            out[:, lanes] = (got.astype(BF) * scale).astype(BF) if scale != 1.0 else got.astype(BF)
            return carry

        lax.fori_loop(0, PAIRS, slab, 0)

    loads[2].wait()
    project(0, wk, keys, True, 1.0)
    loads[3].wait()
    project(0, wv, values, False, 1.0)
    loads[4].wait()
    project(REACH * B, wq, query, True, HEAD_DIM ** (-0.5))
    loads[5].wait()
    gatt[pl.ds(0, B), :] = nt(cot_all[0], wo[...]).astype(BF)

    relays[0].wait_recv()
    relays[1].start()

    lane_one = lax.broadcasted_iota(jnp.int32, (1, B), 1)
    left = (lane_one < HEAD_DIM).astype(BF)
    right = (lane_one >= HEAD_DIM).astype(BF)

    def stacked(a):
        return jnp.concatenate([a * left, a * right], axis=0)

    def picked(a):
        return jnp.where(lane_one < HEAD_DIM, a[:B], a[B:])

    own_cos = cosv[pl.ds(REACH * B, B), :]
    own_sin = sinv[pl.ds(REACH * B, B), :]
    statc[...] = jnp.zeros_like(statc)

    def pass_one(p, carry):
        lanes = pl.ds(pl.multiple_of(p * B, B), B)
        k, v = keys[:, lanes], values[:, lanes]
        scores = nt(stacked(query[pl.ds(0, B), lanes]), k)
        row = lax.broadcasted_iota(jnp.int32, (2 * B, SPAN), 0)
        col = lax.broadcasted_iota(jnp.int32, (2 * B, SPAN), 1)
        dist = row % B + WINDOW - col
        row_one = lax.broadcasted_iota(jnp.int32, (2 * B, 1), 0)
        width = jnp.where(row_one < B, window_ref[2 * p], window_ref[2 * p + 1])
        allowed = (dist >= 0) & (dist < width) & (col >= WINDOW - base)
        masked = jnp.where(allowed, scores, -1e30)
        top = jnp.max(masked, axis=1, keepdims=True)
        weights = jnp.exp(masked - top)
        scale = 1.0 / jnp.sum(weights, axis=1, keepdims=True)
        probs = weights * scale
        grad_probs = nt(stacked(gatt[pl.ds(0, B), lanes]), v)
        row_term = jnp.sum(probs * grad_probs, axis=1, keepdims=True)
        ds = (probs * (grad_probs - row_term)).astype(BF)
        att[:, lanes] = picked(nn(probs.astype(BF), v)).astype(BF)
        grad_query = picked(nn(ds, k)) * HEAD_DIM ** (-0.5)
        gq[:, lanes] = unrope(grad_query, own_cos, own_sin).astype(BF)
        held = statc[...]
        for j, stat in enumerate((top, scale, row_term)):
            held = jnp.where(lane_one == 16 * j + 2 * p, stat[:B], held)
            held = jnp.where(lane_one == 16 * j + 2 * p + 1, stat[B:], held)
        statc[...] = held
        return carry

    lax.fori_loop(0, PAIRS, pass_one, 0)

    relays[1].wait_recv()
    relays[2].start()

    stats[0] = statc[...].T[: 3 * 16]
    stat_copies = []
    for d in range(1, REACH + 1):
        stat_copies.append(
            remote(stats.at[0], stats.at[d], st_send.at[d - 1], st_recv.at[d - 1], at(dp, shift(-d)))
        )
    for copy in stat_copies:
        copy.start()

    relays[2].wait_recv()
    relays[3].start()
    for d in range(1, REACH):
        gatt[pl.ds(d * B, B), :] = nt(cot_all[d], wo[...]).astype(BF)
    relays[3].wait_recv()
    gatt[pl.ds(REACH * B, B), :] = nt(cot_all[REACH], wo[...]).astype(BF)
    for copy in stat_copies:
        copy.wait_recv()

    def pass_two(p, carry):
        lanes = pl.ds(pl.multiple_of(p * B, B), B)
        k2 = stacked(keys[pl.ds(REACH * B, B), lanes])
        v2 = stacked(values[pl.ds(REACH * B, B), lanes])
        row_one = lax.broadcasted_iota(jnp.int32, (2 * B, 1), 0)
        width = jnp.where(row_one < B, window_ref[2 * p], window_ref[2 * p + 1])
        row = lax.broadcasted_iota(jnp.int32, (2 * B, B), 0) % B
        col = lax.broadcasted_iota(jnp.int32, (2 * B, B), 1)
        for d in range(REACH + 1):
            q, g = query[pl.ds(d * B, B), lanes], gatt[pl.ds(d * B, B), lanes]
            dist = col + d * B - row
            allowed = (dist >= 0) & (dist < width) & (col + d * B < SEQ_DEVS * B - base)

            def spread(j):
                a = jnp.broadcast_to(stats[d, pl.ds(16 * j + 2 * p, 1), :], (B, B))
                b = jnp.broadcast_to(stats[d, pl.ds(16 * j + 2 * p + 1, 1), :], (B, B))
                return jnp.concatenate([a, b], axis=0)

            masked = jnp.where(allowed, nt(k2, q), -1e30)
            weights = jnp.exp(jnp.where(allowed, masked - spread(0), -1e30))
            probs = weights * spread(1)
            ds = probs * (nt(v2, g) - spread(2))
            probs_s[:, pl.ds(d * B, B)] = probs.astype(BF)
            ds_s[:, pl.ds(d * B, B)] = ds.astype(BF)
        grad_value = picked(nn(probs_s[...], gatt[:, lanes]))
        grad_key = picked(nn(ds_s[...], query[:, lanes]))
        gv[:, lanes] = grad_value.astype(BF)
        gk[:, lanes] = unrope(grad_key, own_cos, own_sin).astype(BF)
        return carry

    lax.fori_loop(0, PAIRS, pass_two, 0)

    att_t = att[...].T

    def terms(p, carry):
        lanes = pl.ds(pl.multiple_of(p * B, B), B)
        core, row = p % 2, p // 2
        hot = onehot_t[...]
        term[core, row, pl.ds(0, VOCAB), :] = nn(hot, gq[:, lanes]).astype(BF)
        term[core, row, pl.ds(VOCAB, VOCAB), :] = nn(hot, gk[:, lanes]).astype(BF)
        term[core, row, pl.ds(2 * VOCAB, VOCAB), :] = nn(hot, gv[:, lanes]).astype(BF)
        term[core, row, pl.ds(3 * VOCAB, D), :] = nn(att_t, cot_all[0, :, lanes]).astype(BF)
        return carry

    lax.fori_loop(0, PAIRS, terms, 0)

    p1 = remote(term.at[1 - c], r1, p1_send.at[0], p1_recv.at[0], at(y * 2 + 1 - c, sq))
    p1.start()

    grad_normed = nt(gq[...], wq[...]) + nt(gk[...], wk[...]) + nt(gv[...], wv[...])
    own = emb[...]
    inv = lax.rsqrt(jnp.mean(own * own, axis=1, keepdims=True) + EPSILON)
    scaled = own * inv
    gin_ref[...] = (
        inv * (grad_normed - scaled * jnp.mean(grad_normed * scaled, axis=1, keepdims=True))
    ).astype(BF)

    p1.wait_recv()
    for row in range(3):
        s1[row] = (term[c, row].astype(F32) + r1[row].astype(F32)).astype(BF)

    def p2(step):
        return remote(
            s1.at[lax.min(other_y(step), 2)], r2.at[step - 1], p2_send.at[step - 1], p2_recv.at[step - 1],
            at(other_y(step) * 2 + c, sq),
        )

    for step in range(1, 4):
        @pl.when(other_y(step) < 3)
        def _():
            p2(step).start()

    def p3_token(step, target):
        return remote(
            s2.at[pl.ds(pl.multiple_of(target * VOCAB, VOCAB), VOCAB)], r3.at[step - 1, pl.ds(0, VOCAB)],
            p3_send.at[step - 1], p3_recv.at[step - 1], at(dp, seq_of(target, z)),
        )

    def p3_out(step):
        return remote(
            s2.at[pl.ds(3 * VOCAB, D)], r3.at[step - 1],
            p3_send.at[step - 1], p3_recv.at[step - 1], at(dp, seq_of(3, z)),
        )

    def p4(step):
        return remote(
            a4.at[other_z(step)], r4.at[step - 1], p4_send.at[step - 1], p4_recv.at[step - 1],
            at(dp, seq_of(x, other_z(step))),
        )

    @pl.when(y < 3)
    def _():
        for step in range(1, 4):
            p2(step).wait_recv()
        total = s1[lax.min(y, 2)].astype(F32)
        for step in range(3):
            total += r2[step].astype(F32)
        s2[...] = total.astype(BF)

        for step in range(1, 4):
            @pl.when(other_x(step) < 3)
            def _():
                p3_token(step, lax.min(other_x(step), 2)).start()

            @pl.when(other_x(step) == 3)
            def _():
                p3_out(step).start()

        @pl.when(x < 3)
        def _():
            for step in range(1, 4):
                p3_token(step, lax.min(x, 2)).wait_recv()
            total = s2[pl.ds(pl.multiple_of(lax.min(x, 2) * VOCAB, VOCAB), VOCAB), :].astype(F32)
            for step in range(3):
                total += r3[step, pl.ds(0, VOCAB), :].astype(F32)
            a4[...] = tn(ntab[...], total.astype(BF)).astype(BF).reshape(8, D // 8, B)

        @pl.when(x == 3)
        def _():
            for step in range(1, 4):
                p3_out(step).wait_recv()
            total = s2[pl.ds(3 * VOCAB, D), :].astype(F32)
            for step in range(3):
                total += r3[step].astype(F32)
            a4[...] = total.astype(BF).reshape(8, D // 8, B)

        for step in range(1, 8):
            p4(step).start()
        for step in range(1, 8):
            p4(step).wait_recv()
        total = a4[z].astype(F32)
        for step in range(7):
            total += r4[step].astype(F32)
        r5[dp] = total.astype(BF)

    def p5(step):
        mine = lax.min(dp, 5)
        return remote(r5.at[mine], r5.at[mine], p5_send.at[step - 1], p5_recv.at[step - 1], at(other_dp(step), sq))

    def p5_from(step):
        owner = lax.rem(dp + 8 - step, 8)
        slot = lax.min(owner, 5)
        return owner, remote(
            r5.at[slot], r5.at[slot], p5_send.at[step - 1], p5_recv.at[step - 1], at(other_dp(step), sq)
        )

    @pl.when(dp < 6)
    def _():
        for step in range(1, 8):
            p5(step).start()

    for step in range(1, 8):
        owner, copy = p5_from(step)

        @pl.when(owner < 6)
        def _():
            copy.wait_recv()

    for p in range(PAIRS):
        wg_ref[:, pl.ds(p * B, B)] = r5[p].astype(F32)

    for copy in id_copies + relays + stat_copies + [p1]:
        copy.wait_send()
    for step in range(1, 4):
        @pl.when(other_y(step) < 3)
        def _():
            p2(step).wait_send()

    @pl.when(y < 3)
    def _():
        for step in range(1, 4):
            @pl.when(other_x(step) < 3)
            def _():
                p3_token(step, lax.min(other_x(step), 2)).wait_send()

            @pl.when(other_x(step) == 3)
            def _():
                p3_out(step).wait_send()
        for step in range(1, 8):
            p4(step).wait_send()
            p5(step).wait_send()


def on_device(token_ids, cotangent, table, w_query, w_key, w_value, w_out, window):
    tables = [jnp.asarray(part) for part in rope_tables()]
    vmem = pl.BlockSpec(memory_space=pltpu.VMEM)
    hbm = pl.BlockSpec(memory_space=pl.ANY)
    smem = pl.BlockSpec(memory_space=pltpu.SMEM)
    dma = pltpu.SemaphoreType.DMA
    grad_input, weight_grads = pl.pallas_call(
        kernel,
        out_shape=(
            jax.ShapeDtypeStruct((B, D), BF),
            jax.ShapeDtypeStruct((D // 8, D), F32),
        ),
        in_specs=[vmem] + [hbm] * 6 + [smem] + [vmem] * 4,
        out_specs=(vmem, vmem),
        scratch_shapes=[
            pltpu.VMEM((2 * REACH + 1, 1, B), jnp.int32),
            pltpu.VMEM((REACH + 1, B, D), BF),
            pltpu.VMEM((VOCAB, D), BF),
            pltpu.VMEM((D, D), BF),
            pltpu.VMEM((D, D), BF),
            pltpu.VMEM((D, D), BF),
            pltpu.VMEM((D, D), BF),
            pltpu.VMEM((VOCAB, D), BF),
            pltpu.VMEM(((2 * REACH + 1) * B, D), BF),
            pltpu.VMEM((B, D), F32),
            pltpu.VMEM(((2 * REACH + 1) * B, B), F32),
            pltpu.VMEM(((2 * REACH + 1) * B, B), F32),
            pltpu.VMEM((SPAN, D), BF),
            pltpu.VMEM((SPAN, D), BF),
            pltpu.VMEM((SPAN, D), BF),
            pltpu.VMEM((SPAN, D), BF),
            pltpu.VMEM((B, D), BF),
            pltpu.VMEM((B, D), BF),
            pltpu.VMEM((B, D), BF),
            pltpu.VMEM((B, D), BF),
            pltpu.VMEM((VOCAB, B), BF),
            pltpu.VMEM((B, B), F32),
            pltpu.VMEM((REACH + 1, 48, B), F32),
            pltpu.VMEM((2 * B, SPAN), BF),
            pltpu.VMEM((2 * B, SPAN), BF),
            pltpu.VMEM((2, 3, TERM_ROWS, B), BF),
            pltpu.VMEM((3, TERM_ROWS, B), BF),
            pltpu.VMEM((3, TERM_ROWS, B), BF),
            pltpu.VMEM((3, TERM_ROWS, B), BF),
            pltpu.VMEM((TERM_ROWS, B), BF),
            pltpu.VMEM((3, D, B), BF),
            pltpu.VMEM((8, D // 8, B), BF),
            pltpu.VMEM((7, D // 8, B), BF),
            pltpu.VMEM((PAIRS, D // 8, B), BF),
            dma((6,)), dma((8,)), dma((8,)), dma((4,)), dma((4,)), dma((4,)), dma((4,)),
            dma((1,)), dma((1,)), dma((3,)), dma((3,)), dma((3,)), dma((3,)),
            dma((7,)), dma((7,)), dma((7,)), dma((7,)),
        ],
        compiler_params=pltpu.CompilerParams(collective_id=0, has_side_effects=True),
    )(token_ids, cotangent[0], table, w_query, w_key, w_value, w_out, window, *tables)
    return (grad_input[None], weight_grads)


def solution(mesh):
    return jax.shard_map(
        on_device,
        mesh=mesh,
        in_specs=(P("dp", "seq"), P("dp", "seq", None), P(), P(), P(), P(), P(), P()),
        out_specs=(P("dp", "seq", None), P("seq", None)),
        check_vma=False,
    )
```

```python
import functools

import jax
import jax.numpy as jnp
import numpy as np
from jax import lax
from jax.experimental import pallas as pl
from jax.experimental.pallas import tpu as pltpu
from jax.sharding import PartitionSpec as P

D = 768
HEADS = 12
HEAD_DIM = 64
VOCAB = 256
WINDOW = 512
EPSILON = 1e-05
B = 128
SEQ_DEVS = 32
REACH = WINDOW // B
SPAN = (REACH + 1) * B
PAIRS = D // B
MESH = pl.DeviceIdType.MESH
BF = jnp.bfloat16
F32 = jnp.float32


def rope_tables():
    frequency = 10000.0 ** (-2.0 * np.arange(HEAD_DIM // 2) / HEAD_DIM)
    lane_frequency = np.tile(frequency, 4)[None, :]
    inside = np.arange(B)[:, None] * lane_frequency
    blocks = (np.arange(SEQ_DEVS) * B)[:, None] * lane_frequency
    return [
        np.asarray(part, np.float32)
        for part in (np.cos(inside), np.sin(inside), np.cos(blocks), np.sin(blocks))
    ]


def nn(a, b):
    return lax.dot_general(a, b, (((1,), (0,)), ((), ())), preferred_element_type=F32)


def nt(a, b):
    return lax.dot_general(a, b, (((1,), (1,)), ((), ())), preferred_element_type=F32)


def tn(a, b):
    return lax.dot_general(a, b, (((0,), (0,)), ((), ())), preferred_element_type=F32)


def swap_halves(x):
    lane = lax.broadcasted_iota(jnp.int32, x.shape, 1)
    first = (lane // (HEAD_DIM // 2)) % 2 == 0
    return jnp.where(first, pltpu.roll(x, B - HEAD_DIM // 2, 1), pltpu.roll(x, HEAD_DIM // 2, 1))


def rope(x, cosine, sine):
    return x * cosine + swap_halves(x) * sine


def unrope(x, cosine, sine):
    return x * cosine - swap_halves(x) * sine


def kernel(
    ids_ref, cot_hbm, table_hbm, wq_hbm, wk_hbm, wv_hbm, wo_hbm, window_ref, cr_ref, sr_ref, cb_ref, sb_ref,
    gin_ref, wg_ref,
    ids_all, ids_dp, cot_all, table, wq, wk, wv, wo, ntab, normed, emb, cosv, sinv,
    keys, values, query, gatt, att, gq, gk, gv, statc, stats, probs_s, ds_s, hot_dp,
    q_out, kv_out, q_in, kv_in, tok_sum, tok_in, z_out, z_in, final,
    out_term, out_core, out_x, out_x_in, out_y, out_y_in, out_z, out_z_in, out_final,
    load_sem, ids_send, ids_recv, idp_send, idp_recv, cot_send, cot_recv, st_send, st_recv,
    q_send, q_recv, kv_send, kv_recv, tok_send, tok_recv, z_send, z_recv, fin_send, fin_recv,
    oc_send, oc_recv, ox_send, ox_recv, oy_send, oy_recv, oz_send, oz_recv, of_send,
):
    dp = lax.axis_index("dp")
    sq = lax.axis_index("seq")
    x, z = sq // 8, sq % 8
    y, c = dp // 2, dp % 2
    base = sq * B

    loads = [
        pltpu.make_async_copy(src, dst, load_sem.at[i])
        for i, (src, dst) in enumerate(
            [(cot_hbm, cot_all.at[0]), (table_hbm, table), (wk_hbm, wk), (wv_hbm, wv), (wq_hbm, wq), (wo_hbm, wo)]
        )
    ]
    for load in loads:
        load.start()

    def seq_of(new_x, new_z):
        return new_x * 8 + new_z

    def shift(distance):
        return lax.rem(sq + distance + SEQ_DEVS, SEQ_DEVS)

    def other_dp(step):
        return lax.rem(dp + step, 8)

    def other_y(step):
        return lax.rem(y + step, 4)

    def other_x(step):
        return lax.rem(x + step, 4)

    def other_z(step):
        return lax.rem(z + step, 8)

    barrier = pltpu.get_barrier_semaphore()
    partners = [(dp, shift(d)) for d in (1, 2, 3, 4, -1, -2, -3, -4)]
    partners += [(other_dp(d), sq) for d in range(1, 8)]
    partners += [(dp, seq_of(other_x(d), z)) for d in range(1, 4)]
    partners += [(dp, seq_of(x, other_z(d))) for d in range(1, 8)]
    partners += [(other_dp(e), seq_of(other_x(d), z)) for d in range(1, 4) for e in range(1, 8)]
    for partner in partners:
        pl.semaphore_signal(barrier, inc=1, device_id=partner, device_id_type=MESH)

    lane_row = lax.broadcasted_iota(jnp.int32, (1, B), 1)
    sign = jnp.where((lane_row // (HEAD_DIM // 2)) % 2 == 0, -1.0, 1.0)

    def rope_block(i, carry):
        block = lax.rem(sq + i - REACH + SEQ_DEVS, SEQ_DEVS)
        cb = cb_ref[pl.ds(block, 1), :]
        sb = sb_ref[pl.ds(block, 1), :]
        rows = pl.ds(pl.multiple_of(i * B, B), B)
        cosv[rows, :] = cr_ref[...] * cb - sr_ref[...] * sb
        sinv[rows, :] = (sr_ref[...] * cb + cr_ref[...] * sb) * sign
        return carry

    lax.fori_loop(0, 2 * REACH + 1, rope_block, 0)

    loads[1].wait()
    rows_f = table[...].astype(F32)
    table_inv = lax.rsqrt(jnp.mean(rows_f * rows_f, axis=1, keepdims=True) + EPSILON)
    ntab[...] = (rows_f * table_inv).astype(BF)

    loads[0].wait()
    pl.semaphore_wait(barrier, len(partners))

    def remote(src, dst, send, recv, device):
        return pltpu.make_async_remote_copy(
            src_ref=src, dst_ref=dst, send_sem=send, recv_sem=recv, device_id=device, device_id_type=MESH
        )

    id_copies = []
    for i, d in enumerate((1, 2, 3, 4, -1, -2, -3, -4)):
        id_copies.append(remote(ids_ref, ids_all.at[d + REACH], ids_send.at[i], ids_recv.at[i], (dp, shift(-d))))
    idp_copies = []
    for d in range(1, 8):
        idp_copies.append(
            remote(ids_ref, ids_dp.at[8 - d], idp_send.at[d - 1], idp_recv.at[d - 1], (other_dp(d), sq))
        )
    relays = [
        remote(cot_all.at[step], cot_all.at[step + 1], cot_send.at[step], cot_recv.at[step], (dp, shift(-1)))
        for step in range(REACH)
    ]
    for copy in id_copies:
        copy.start()
    relays[0].start()
    for copy in idp_copies:
        copy.start()
    ids_all[REACH] = ids_ref[...]
    ids_dp[0] = ids_ref[...]

    token = lax.broadcasted_iota(jnp.int32, (VOCAB, B), 0)
    emb[...] = tn((token == ids_ref[...]).astype(BF), table[...])
    loads[5].wait()
    gatt[pl.ds(0, B), :] = nt(cot_all[0], wo[...]).astype(BF)
    for copy in id_copies:
        copy.wait_recv()

    def embed_block(i, carry):
        rows = pl.ds(pl.multiple_of(i * B, B), B)
        hot = (token == ids_all[i]).astype(BF)
        normed[rows, :] = tn(hot, ntab[...]).astype(BF)
        return carry

    lax.fori_loop(0, 2 * REACH + 1, embed_block, 0)

    def project(first, w, out, rotated, scale):
        def slab(j, carry):
            lanes = pl.ds(pl.multiple_of(j * 2 * B, B), 2 * B)
            got = nn(normed[pl.ds(first, SPAN), :], w[:, lanes])
            for half in range(2):
                part = got[:, half * B : (half + 1) * B]
                if rotated:
                    part = rope(part, cosv[pl.ds(first, SPAN), :], sinv[pl.ds(first, SPAN), :])
                out[:, pl.ds(pl.multiple_of((2 * j + half) * B, B), B)] = (
                    (part.astype(BF) * scale).astype(BF) if scale != 1.0 else part.astype(BF)
                )
            return carry

        lax.fori_loop(0, PAIRS // 2, slab, 0)

    loads[2].wait()
    project(0, wk, keys, True, 1.0)
    loads[3].wait()
    project(0, wv, values, False, 1.0)
    relays[0].wait_recv()
    relays[1].start()
    loads[4].wait()
    project(REACH * B, wq, query, True, HEAD_DIM ** (-0.5))

    lane_one = lax.broadcasted_iota(jnp.int32, (1, B), 1)
    left = (lane_one < HEAD_DIM).astype(BF)
    right = (lane_one >= HEAD_DIM).astype(BF)

    def stacked(a):
        return jnp.concatenate([a * left, a * right], axis=0)

    def picked(a):
        return jnp.where(lane_one < HEAD_DIM, a[:B], a[B:])

    own_cos = cosv[pl.ds(REACH * B, B), :]
    own_sin = sinv[pl.ds(REACH * B, B), :]
    statc[...] = jnp.zeros_like(statc)

    def q_copy(p):
        return remote(q_out.at[p], q_in.at[dp], q_send.at[p], q_recv.at[dp], (p, sq))

    def kv_copy(p):
        return remote(kv_out.at[p], kv_in.at[dp], kv_send.at[p], kv_recv.at[dp], (p, sq))

    def pass_one(p, carry):
        lanes = pl.ds(pl.multiple_of(p * B, B), B)
        k, v = keys[:, lanes], values[:, lanes]
        scores = nt(stacked(query[pl.ds(0, B), lanes]), k)
        row = lax.broadcasted_iota(jnp.int32, (2 * B, SPAN), 0)
        col = lax.broadcasted_iota(jnp.int32, (2 * B, SPAN), 1)
        dist = row % B + WINDOW - col
        row_one = lax.broadcasted_iota(jnp.int32, (2 * B, 1), 0)
        width = jnp.where(row_one < B, window_ref[2 * p], window_ref[2 * p + 1])
        allowed = (dist >= 0) & (dist < width) & (col >= WINDOW - base)
        masked = jnp.where(allowed, scores, -1e30)
        top = jnp.max(masked, axis=1, keepdims=True)
        weights = jnp.exp(masked - top)
        scale = 1.0 / jnp.sum(weights, axis=1, keepdims=True)
        probs = weights * scale
        grad_probs = nt(stacked(gatt[pl.ds(0, B), lanes]), v)
        row_term = jnp.sum(probs * grad_probs, axis=1, keepdims=True)
        ds = (probs * (grad_probs - row_term)).astype(BF)
        att[:, lanes] = picked(nn(probs.astype(BF), v)).astype(BF)
        grad_query = picked(nn(ds, k)) * HEAD_DIM ** (-0.5)
        got = unrope(grad_query, own_cos, own_sin).astype(BF)
        gq[:, lanes] = got

        @pl.when(p != dp)
        def _():
            q_out[p] = got
            q_copy(p).start()

        @pl.when(p == dp)
        def _():
            q_in[dp] = got

        held = statc[...]
        for j, stat in enumerate((top, scale, row_term)):
            held = jnp.where(lane_one == 16 * j + 2 * p, stat[:B], held)
            held = jnp.where(lane_one == 16 * j + 2 * p + 1, stat[B:], held)
        statc[...] = held

        @pl.when(p == 2)
        def _():
            relays[1].wait_recv()
            relays[2].start()

        return carry

    lax.fori_loop(0, PAIRS, pass_one, 0)

    stats[0] = statc[...].T[: 3 * 16]
    stat_copies = [
        remote(stats.at[0], stats.at[d], st_send.at[d - 1], st_recv.at[d - 1], (dp, shift(-d)))
        for d in range(1, REACH + 1)
    ]
    for copy in stat_copies:
        copy.start()

    att_t = att[...].T

    def out_terms(p, carry):
        lanes = pl.ds(pl.multiple_of(p * B, B), B)
        got = nn(att_t, cot_all[0, :, lanes]).astype(BF)
        for block in range(4):
            out_term[p % 2, block, p // 2] = got[block * 192 : (block + 1) * 192]
        return carry

    lax.fori_loop(0, PAIRS, out_terms, 0)
    oc = remote(out_term.at[1 - c], out_core, oc_send.at[0], oc_recv.at[0], (y * 2 + 1 - c, sq))
    oc.start()

    for d in range(1, 3):
        gatt[pl.ds(d * B, B), :] = nt(cot_all[d], wo[...]).astype(BF)
    relays[2].wait_recv()
    relays[3].start()
    gatt[pl.ds(3 * B, B), :] = nt(cot_all[3], wo[...]).astype(BF)

    oc.wait_recv()
    for block in range(4):
        out_x[block] = (out_term[c, block].astype(F32) + out_core[block].astype(F32)).astype(BF)

    def ox(step):
        return remote(
            out_x.at[other_x(step)], out_x_in.at[step - 1], ox_send.at[step - 1], ox_recv.at[step - 1],
            (dp, seq_of(other_x(step), z)),
        )

    for step in range(1, 4):
        ox(step).start()

    relays[3].wait_recv()
    gatt[pl.ds(REACH * B, B), :] = nt(cot_all[REACH], wo[...]).astype(BF)
    for copy in stat_copies:
        copy.wait_recv()

    def oy(step):
        return remote(
            out_y.at[lax.min(other_y(step), 2)], out_y_in.at[step - 1], oy_send.at[step - 1], oy_recv.at[step - 1],
            (other_y(step) * 2 + c, sq),
        )

    def pass_two(p, carry):
        lanes = pl.ds(pl.multiple_of(p * B, B), B)
        k2 = stacked(keys[pl.ds(REACH * B, B), lanes])
        v2 = stacked(values[pl.ds(REACH * B, B), lanes])
        row_one = lax.broadcasted_iota(jnp.int32, (2 * B, 1), 0)
        width = jnp.where(row_one < B, window_ref[2 * p], window_ref[2 * p + 1])
        row = lax.broadcasted_iota(jnp.int32, (2 * B, B), 0) % B
        col = lax.broadcasted_iota(jnp.int32, (2 * B, B), 1)
        for d in range(REACH + 1):
            q, g = query[pl.ds(d * B, B), lanes], gatt[pl.ds(d * B, B), lanes]
            dist = col + d * B - row
            allowed = (dist >= 0) & (dist < width) & (col + d * B < SEQ_DEVS * B - base)

            def spread(j):
                a = jnp.broadcast_to(stats[d, pl.ds(16 * j + 2 * p, 1), :], (B, B))
                b = jnp.broadcast_to(stats[d, pl.ds(16 * j + 2 * p + 1, 1), :], (B, B))
                return jnp.concatenate([a, b], axis=0)

            weights = jnp.exp(jnp.where(allowed, nt(k2, q) - spread(0), -1e30))
            probs = weights * spread(1)
            ds = probs * (nt(v2, g) - spread(2))
            probs_s[:, pl.ds(d * B, B)] = probs.astype(BF)
            ds_s[:, pl.ds(d * B, B)] = ds.astype(BF)
        grad_value = picked(nn(probs_s[...], gatt[:, lanes])).astype(BF)
        grad_key = unrope(picked(nn(ds_s[...], query[:, lanes])), own_cos, own_sin).astype(BF)
        gv[:, lanes] = grad_value
        gk[:, lanes] = grad_key

        @pl.when(p != dp)
        def _():
            kv_out[p, 0] = grad_key
            kv_out[p, 1] = grad_value
            kv_copy(p).start()

        @pl.when(p == dp)
        def _():
            kv_in[dp, 0] = grad_key
            kv_in[dp, 1] = grad_value

        @pl.when(p == 4)
        def _():
            for step in range(1, 4):
                ox(step).wait_recv()
            for row in range(3):
                total = out_x[x, row].astype(F32)
                for step in range(3):
                    total += out_x_in[step, row].astype(F32)
                out_y[row] = total.astype(BF)
            for step in range(1, 4):
                @pl.when(other_y(step) < 3)
                def _():
                    oy(step).start()

        return carry

    lax.fori_loop(0, PAIRS, pass_two, 0)

    grad_normed = nt(gq[...], wq[...]) + nt(gk[...], wk[...]) + nt(gv[...], wv[...])
    own = emb[...]
    inv = lax.rsqrt(jnp.mean(own * own, axis=1, keepdims=True) + EPSILON)
    scaled = own * inv
    gin_ref[...] = (
        inv * (grad_normed - scaled * jnp.mean(grad_normed * scaled, axis=1, keepdims=True))
    ).astype(BF)

    def tok(step, target):
        return remote(
            tok_sum.at[target], tok_in.at[step - 1], tok_send.at[step - 1], tok_recv.at[step - 1],
            (dp, seq_of(target, z)),
        )

    def oz_step(i):
        return lax.rem(2 * x + i - z + 8, 8)

    def oz(i):
        step = lax.max(oz_step(i), 1)
        return remote(
            out_z.at[i], out_z_in.at[step - 1], oz_send.at[i], oz_recv.at[step - 1], (dp, seq_of(x, 2 * x + i))
        )

    def oz_in(step):
        return remote(
            out_z.at[0], out_z_in.at[step - 1], oz_send.at[0], oz_recv.at[step - 1], (dp, seq_of(x, z))
        )

    def zs(step):
        return remote(
            z_out.at[other_z(step)], z_in.at[step - 1], z_send.at[step - 1], z_recv.at[step - 1],
            (dp, seq_of(x, other_z(step))),
        )

    mine = lax.min(dp, PAIRS - 1)

    def fin(step):
        return remote(
            final.at[mine], final.at[mine], fin_send.at[step - 1], fin_recv.at[mine], (other_dp(step), sq)
        )

    def out_fin(step):
        return remote(
            out_final, final.at[mine], of_send.at[step], fin_recv.at[mine], (other_dp(step), seq_of(3, z))
        )

    def fin_in(p):
        return remote(final.at[p], final.at[p], fin_send.at[0], fin_recv.at[p], (p, sq))

    for copy in idp_copies:
        copy.wait_recv()

    @pl.when(dp < PAIRS)
    def _():
        def hot_block(i, carry):
            owner = lax.rem(dp + i, 8)
            hot_dp[owner] = (token == ids_dp[i]).astype(BF)
            return carry

        lax.fori_loop(0, 8, hot_block, 0)

        for i in range(8):
            @pl.when(i != dp)
            def _():
                remote(q_out.at[0], q_in.at[i], q_send.at[0], q_recv.at[i], (mine, sq)).wait_recv()

        hot = jnp.concatenate([hot_dp[i] for i in range(8)], axis=1)
        tok_sum[0] = nn(hot, q_in[...].reshape(8 * B, B)).astype(BF)
        for i in range(8):
            @pl.when(i != dp)
            def _():
                remote(kv_out.at[0], kv_in.at[i], kv_send.at[0], kv_recv.at[i], (mine, sq)).wait_recv()
        tok_sum[1] = nn(hot, kv_in[:, 0].reshape(8 * B, B)).astype(BF)
        tok_sum[2] = nn(hot, kv_in[:, 1].reshape(8 * B, B)).astype(BF)
        for step in range(1, 4):
            @pl.when(other_x(step) < 3)
            def _():
                tok(step, lax.min(other_x(step), 2)).start()

        for step in range(1, 4):
            oy(step).wait_recv()
        total = out_y[lax.min(y, 2)].astype(F32)
        for step in range(3):
            total += out_y_in[step].astype(F32)
        out_z[...] = total.astype(BF).reshape(2, D // 8, B)
        for i in range(2):
            @pl.when(oz_step(i) != 0)
            def _():
                oz(i).start()

        @pl.when(x < 3)
        def _():
            for step in range(1, 4):
                tok(step, lax.min(x, 2)).wait_recv()
            total = tok_sum[lax.min(x, 2)].astype(F32)
            for step in range(3):
                total += tok_in[step].astype(F32)
            z_out[...] = tn(ntab[...], total.astype(BF)).astype(BF).reshape(8, D // 8, B)
            for step in range(1, 8):
                zs(step).start()

        @pl.when(z // 2 == x)
        def _():
            for step in range(1, 8):
                oz_in(step).wait_recv()
            total = out_z[z % 2].astype(F32)
            for step in range(7):
                total += out_z_in[step].astype(F32)
            out_final[...] = total.astype(BF)
            for step in range(1, 8):
                out_fin(step).start()

            @pl.when(x < 3)
            def _():
                out_fin(0).start()

            @pl.when(x == 3)
            def _():
                final[mine] = out_final[...]

        @pl.when(x < 3)
        def _():
            for step in range(1, 8):
                zs(step).wait_recv()
            total = z_out[z].astype(F32)
            for step in range(7):
                total += z_in[step].astype(F32)
            final[mine] = total.astype(BF)
            for step in range(1, 8):
                fin(step).start()

    for p in range(PAIRS):
        @pl.when((dp != p) | ((x == 3) & (z < 6)))
        def _():
            fin_in(p).wait_recv()

        wg_ref[:, pl.ds(p * B, B)] = final[p].astype(F32)

    for copy in id_copies + idp_copies + relays + stat_copies + [oc] + [ox(step) for step in range(1, 4)]:
        copy.wait_send()
    for p in range(PAIRS):
        @pl.when(p != dp)
        def _():
            q_copy(p).wait_send()
            kv_copy(p).wait_send()
    for step in range(1, 4):
        @pl.when(other_y(step) < 3)
        def _():
            oy(step).wait_send()

    @pl.when(dp < PAIRS)
    def _():
        for step in range(1, 4):
            @pl.when(other_x(step) < 3)
            def _():
                tok(step, lax.min(other_x(step), 2)).wait_send()
        for i in range(2):
            @pl.when(oz_step(i) != 0)
            def _():
                oz(i).wait_send()

        @pl.when(x < 3)
        def _():
            for step in range(1, 8):
                zs(step).wait_send()
                fin(step).wait_send()

        @pl.when(z // 2 == x)
        def _():
            for step in range(1, 8):
                out_fin(step).wait_send()

            @pl.when(x < 3)
            def _():
                out_fin(0).wait_send()


def on_device(token_ids, cotangent, table, w_query, w_key, w_value, w_out, window):
    tables = [jnp.asarray(part) for part in rope_tables()]
    vmem = pl.BlockSpec(memory_space=pltpu.VMEM)
    hbm = pl.BlockSpec(memory_space=pl.ANY)
    smem = pl.BlockSpec(memory_space=pltpu.SMEM)
    dma = pltpu.SemaphoreType.DMA
    grad_input, weight_grads = pl.pallas_call(
        kernel,
        out_shape=(
            jax.ShapeDtypeStruct((B, D), BF),
            jax.ShapeDtypeStruct((D // 8, D), F32),
        ),
        in_specs=[vmem] + [hbm] * 6 + [smem] + [vmem] * 4,
        out_specs=(vmem, vmem),
        scratch_shapes=[
            pltpu.VMEM((2 * REACH + 1, 1, B), jnp.int32),
            pltpu.VMEM((8, 1, B), jnp.int32),
            pltpu.VMEM((REACH + 1, B, D), BF),
            pltpu.VMEM((VOCAB, D), BF),
            pltpu.VMEM((D, D), BF),
            pltpu.VMEM((D, D), BF),
            pltpu.VMEM((D, D), BF),
            pltpu.VMEM((D, D), BF),
            pltpu.VMEM((VOCAB, D), BF),
            pltpu.VMEM(((2 * REACH + 1) * B, D), BF),
            pltpu.VMEM((B, D), F32),
            pltpu.VMEM(((2 * REACH + 1) * B, B), F32),
            pltpu.VMEM(((2 * REACH + 1) * B, B), F32),
            pltpu.VMEM((SPAN, D), BF),
            pltpu.VMEM((SPAN, D), BF),
            pltpu.VMEM((SPAN, D), BF),
            pltpu.VMEM((SPAN, D), BF),
            pltpu.VMEM((B, D), BF),
            pltpu.VMEM((B, D), BF),
            pltpu.VMEM((B, D), BF),
            pltpu.VMEM((B, D), BF),
            pltpu.VMEM((B, B), F32),
            pltpu.VMEM((REACH + 1, 48, B), F32),
            pltpu.VMEM((2 * B, SPAN), BF),
            pltpu.VMEM((2 * B, SPAN), BF),
            pltpu.VMEM((8, VOCAB, B), BF),
            pltpu.VMEM((PAIRS, B, B), BF),
            pltpu.VMEM((PAIRS, 2, B, B), BF),
            pltpu.VMEM((8, B, B), BF),
            pltpu.VMEM((8, 2, B, B), BF),
            pltpu.VMEM((3, VOCAB, B), BF),
            pltpu.VMEM((3, VOCAB, B), BF),
            pltpu.VMEM((8, D // 8, B), BF),
            pltpu.VMEM((7, D // 8, B), BF),
            pltpu.VMEM((PAIRS, D // 8, B), BF),
            pltpu.VMEM((2, 4, 3, D // 4, B), BF),
            pltpu.VMEM((4, 3, D // 4, B), BF),
            pltpu.VMEM((4, 3, D // 4, B), BF),
            pltpu.VMEM((3, 3, D // 4, B), BF),
            pltpu.VMEM((3, D // 4, B), BF),
            pltpu.VMEM((3, D // 4, B), BF),
            pltpu.VMEM((2, D // 8, B), BF),
            pltpu.VMEM((7, D // 8, B), BF),
            pltpu.VMEM((D // 8, B), BF),
            dma((6,)), dma((8,)), dma((8,)), dma((7,)), dma((7,)), dma((4,)), dma((4,)), dma((4,)), dma((4,)),
            dma((PAIRS,)), dma((8,)), dma((PAIRS,)), dma((8,)), dma((3,)), dma((3,)), dma((7,)), dma((7,)),
            dma((7,)), dma((PAIRS,)),
            dma((1,)), dma((1,)), dma((3,)), dma((3,)), dma((3,)), dma((3,)), dma((2,)), dma((7,)), dma((8,)),
        ],
        compiler_params=pltpu.CompilerParams(collective_id=0, has_side_effects=True),
    )(token_ids, cotangent[0], table, w_query, w_key, w_value, w_out, window, *tables)
    return (grad_input[None], weight_grads)


def solution(mesh):
    return jax.shard_map(
        on_device,
        mesh=mesh,
        in_specs=(P("dp", "seq"), P("dp", "seq", None), P(), P(), P(), P(), P(), P()),
        out_specs=(P("dp", "seq", None), P("seq", None)),
        check_vma=False,
    )
```

```python
import functools

import jax
import jax.numpy as jnp
import numpy as np
from jax import lax
from jax.experimental import pallas as pl
from jax.experimental.pallas import tpu as pltpu
from jax.sharding import PartitionSpec as P

D = 768
HEADS = 12
HEAD_DIM = 64
VOCAB = 256
WINDOW = 512
EPSILON = 1e-05
B = 128
SEQ_DEVS = 32
REACH = WINDOW // B
SPAN = (REACH + 1) * B
PAIRS = D // B
MESH = pl.DeviceIdType.MESH
BF = jnp.bfloat16
F32 = jnp.float32


def rope_tables():
    frequency = 10000.0 ** (-2.0 * np.arange(HEAD_DIM // 2) / HEAD_DIM)
    lane_frequency = np.tile(frequency, 4)[None, :]
    inside = np.arange(B)[:, None] * lane_frequency
    blocks = (np.arange(SEQ_DEVS) * B)[:, None] * lane_frequency
    return [
        np.asarray(part, np.float32)
        for part in (np.cos(inside), np.sin(inside), np.cos(blocks), np.sin(blocks))
    ]


def nn(a, b):
    return lax.dot_general(a, b, (((1,), (0,)), ((), ())), preferred_element_type=F32)


def nt(a, b):
    return lax.dot_general(a, b, (((1,), (1,)), ((), ())), preferred_element_type=F32)


def tn(a, b):
    return lax.dot_general(a, b, (((0,), (0,)), ((), ())), preferred_element_type=F32)


def swap_halves(x):
    lane = lax.broadcasted_iota(jnp.int32, x.shape, 1)
    first = (lane // (HEAD_DIM // 2)) % 2 == 0
    return jnp.where(first, pltpu.roll(x, B - HEAD_DIM // 2, 1), pltpu.roll(x, HEAD_DIM // 2, 1))


def rope(x, cosine, sine):
    return x * cosine + swap_halves(x) * sine


def unrope(x, cosine, sine):
    return x * cosine - swap_halves(x) * sine


def kernel(
    ids_ref, cot_hbm, table_hbm, wq_hbm, wk_hbm, wv_hbm, wo_hbm, window_ref, cr_ref, sr_ref, cb_ref, sb_ref,
    gin_ref, wg_ref,
    ids_all, ids_dp, cot_all, table, wq, wk, wv, wo, ntab, qtab, ktab, vtab, hot, emb, cosv, sinv, seen, seeing,
    keys, values, query, gatt, att, gq, gk, gv, statc, stats, probs_s, ds_s, hot_dp,
    q_out, kv_out, q_in, kv_in, tok_sum, tok_in, z_out, z_in, final,
    out_term, out_core, out_x, out_x_in, out_y, out_y_in, out_z, out_z_in, out_final,
    load_sem, ids_send, ids_recv, idp_send, idp_recv, cot_send, cot_recv, st_send, st_recv,
    q_send, q_recv, kv_send, kv_recv, tok_send, tok_recv, z_send, z_recv, fin_send, fin_recv,
    oc_send, oc_recv, ox_send, ox_recv, oy_send, oy_recv, oz_send, oz_recv, of_send, of_recv,
):
    dp = lax.axis_index("dp")
    sq = lax.axis_index("seq")
    x, z = sq // 8, sq % 8
    y, c = dp // 2, dp % 2
    base = sq * B

    loads = [
        pltpu.make_async_copy(src, dst, load_sem.at[i])
        for i, (src, dst) in enumerate(
            [(table_hbm, table), (cot_hbm, cot_all.at[0]), (wk_hbm, wk), (wv_hbm, wv), (wq_hbm, wq), (wo_hbm, wo)]
        )
    ]
    for load in loads:
        load.start()

    def seq_of(new_x, new_z):
        return new_x * 8 + new_z

    def shift(distance):
        return lax.rem(sq + distance + SEQ_DEVS, SEQ_DEVS)

    def other_dp(step):
        return lax.rem(dp + step, 8)

    def other_y(step):
        return lax.rem(y + step, 4)

    def other_x(step):
        return lax.rem(x + step, 4)

    def other_z(step):
        return lax.rem(z + step, 8)

    barrier = pltpu.get_barrier_semaphore()
    partners = [(dp, shift(d)) for d in (1, 2, 3, 4, -1, -2, -3, -4)]
    partners += [(other_dp(d), sq) for d in range(1, 8)]
    partners += [(dp, seq_of(other_x(d), z)) for d in range(1, 4)]
    partners += [(dp, seq_of(x, other_z(d))) for d in range(1, 8)]
    for partner in partners:
        pl.semaphore_signal(barrier, inc=1, device_id=partner, device_id_type=MESH)

    lane_row = lax.broadcasted_iota(jnp.int32, (1, B), 1)
    sign = jnp.where((lane_row // (HEAD_DIM // 2)) % 2 == 0, -1.0, 1.0)

    def rope_block(i, carry):
        block = lax.rem(sq + i - REACH + SEQ_DEVS, SEQ_DEVS)
        cb = cb_ref[pl.ds(block, 1), :]
        sb = sb_ref[pl.ds(block, 1), :]
        rows = pl.ds(pl.multiple_of(i * B, B), B)
        cosv[rows, :] = cr_ref[...] * cb - sr_ref[...] * sb
        sinv[rows, :] = (sr_ref[...] * cb + cr_ref[...] * sb) * sign
        return carry

    lax.fori_loop(0, 2 * REACH + 1, rope_block, 0)

    loads[0].wait()
    rows_f = table[...].astype(F32)
    table_inv = lax.rsqrt(jnp.mean(rows_f * rows_f, axis=1, keepdims=True) + EPSILON)
    ntab[...] = (rows_f * table_inv).astype(BF)

    def project_table(w, out):
        def slab(j, carry):
            lanes = pl.ds(pl.multiple_of(j * 2 * B, B), 2 * B)
            out[:, lanes] = nn(ntab[...], w[:, lanes]).astype(BF)
            return carry

        lax.fori_loop(0, PAIRS // 2, slab, 0)

    loads[2].wait()
    project_table(wk, ktab)
    loads[1].wait()
    pl.semaphore_wait(barrier, len(partners))

    def remote(src, dst, send, recv, device):
        return pltpu.make_async_remote_copy(
            src_ref=src, dst_ref=dst, send_sem=send, recv_sem=recv, device_id=device, device_id_type=MESH
        )

    id_copies = []
    for i, d in enumerate((1, 2, 3, 4, -1, -2, -3, -4)):
        id_copies.append(remote(ids_ref, ids_all.at[d + REACH], ids_send.at[i], ids_recv.at[i], (dp, shift(-d))))
    idp_copies = []
    for d in range(1, 8):
        idp_copies.append(
            remote(ids_ref, ids_dp.at[8 - d], idp_send.at[d - 1], idp_recv.at[d - 1], (other_dp(d), sq))
        )
    relays = [
        remote(cot_all.at[step], cot_all.at[step + 1], cot_send.at[step], cot_recv.at[step], (dp, shift(-1)))
        for step in range(REACH)
    ]
    for copy in id_copies:
        copy.start()
    relays[0].start()
    for copy in idp_copies:
        copy.start()
    ids_all[REACH] = ids_ref[...]
    ids_dp[0] = ids_ref[...]

    loads[3].wait()
    project_table(wv, vtab)
    loads[4].wait()
    project_table(wq, qtab)
    loads[5].wait()
    gatt[pl.ds(0, B), :] = nt(cot_all[0], wo[...]).astype(BF)

    far = 1 << 20
    dist = lax.broadcasted_iota(jnp.int32, (B, SPAN), 0) + WINDOW - lax.broadcasted_iota(jnp.int32, (B, SPAN), 1)
    col = lax.broadcasted_iota(jnp.int32, (B, SPAN), 1)
    seen[...] = jnp.where((dist >= 0) & (col >= WINDOW - base), dist, far)
    dist = col - lax.broadcasted_iota(jnp.int32, (B, SPAN), 0)
    seeing[...] = jnp.where((dist >= 0) & (col < SEQ_DEVS * B - base), dist, far)

    for copy in id_copies:
        copy.wait_recv()

    token = lax.broadcasted_iota(jnp.int32, (VOCAB, B), 0)

    def hot_rows(i, carry):
        hot[pl.ds(pl.multiple_of(i * B, B), B), :] = (token == ids_all[i]).astype(F32).T.astype(BF)
        return carry

    lax.fori_loop(0, 2 * REACH + 1, hot_rows, 0)

    def select(tab, out, first, to, count, rotated, scale):
        def slab(j, carry):
            lanes = pl.ds(pl.multiple_of(j * 2 * B, B), 2 * B)
            got = nn(hot[pl.ds(first, count), :], tab[:, lanes])
            for half in range(2):
                part = got[:, half * B : (half + 1) * B]
                if rotated:
                    part = rope(part, cosv[pl.ds(first, count), :], sinv[pl.ds(first, count), :])
                if scale != 1.0:
                    part = part * scale
                out[pl.ds(to, count), pl.ds(pl.multiple_of((2 * j + half) * B, B), B)] = part.astype(BF)
            return carry

        lax.fori_loop(0, PAIRS // 2, slab, 0)

    select(ktab, keys, 0, 0, SPAN, True, 1.0)
    relays[0].wait_recv()
    relays[1].start()
    select(vtab, values, 0, 0, SPAN, False, 1.0)
    select(qtab, query, REACH * B, 0, B, True, HEAD_DIM ** (-0.5))

    lane_one = lax.broadcasted_iota(jnp.int32, (1, B), 1)
    left = (lane_one < HEAD_DIM).astype(BF)
    right = (lane_one >= HEAD_DIM).astype(BF)

    def stacked(a):
        return jnp.concatenate([a * left, a * right], axis=0)

    def picked(a):
        return jnp.where(lane_one < HEAD_DIM, a[:B], a[B:])

    own_cos = cosv[pl.ds(REACH * B, B), :]
    own_sin = sinv[pl.ds(REACH * B, B), :]
    statc[...] = jnp.zeros_like(statc)

    def q_copy(p):
        return remote(q_out.at[p], q_in.at[dp], q_send.at[p], q_recv.at[dp], (p, sq))

    def kv_copy(p):
        return remote(kv_out.at[p], kv_in.at[dp], kv_send.at[p], kv_recv.at[dp], (p, sq))

    def pass_one(p, carry):
        lanes = pl.ds(pl.multiple_of(p * B, B), B)
        k, v = keys[:, lanes], values[:, lanes]
        scores = nt(stacked(query[pl.ds(0, B), lanes]), k)
        reach = seen[...]
        masked = jnp.concatenate(
            [
                jnp.where(reach < window_ref[2 * p], scores[:B], -1e30),
                jnp.where(reach < window_ref[2 * p + 1], scores[B:], -1e30),
            ],
            axis=0,
        )
        top = jnp.max(masked, axis=1, keepdims=True)
        weights = jnp.exp(masked - top)
        whole = jnp.sum(weights, axis=1, keepdims=True)
        probs = weights * (1.0 / whole)
        grad_probs = nt(stacked(gatt[pl.ds(0, B), lanes]), v)
        row_term = jnp.sum(probs * grad_probs, axis=1, keepdims=True)
        ds = (probs * (grad_probs - row_term)).astype(BF)
        att[:, lanes] = picked(nn(probs.astype(BF), v)).astype(BF)
        grad_query = picked(nn(ds, k)) * HEAD_DIM ** (-0.5)
        got = unrope(grad_query, own_cos, own_sin).astype(BF)
        gq[:, lanes] = got

        @pl.when(p != dp)
        def _():
            q_out[p] = got
            q_copy(p).start()

        @pl.when(p == dp)
        def _():
            q_in[dp] = got

        held = statc[...]
        for j, stat in enumerate((top + jnp.log(whole), row_term)):
            held = jnp.where(lane_one == 16 * j + 2 * p, stat[:B], held)
            held = jnp.where(lane_one == 16 * j + 2 * p + 1, stat[B:], held)
        statc[...] = held

        @pl.when(p == 5)
        def _():
            relays[1].wait_recv()
            relays[2].start()

        return carry

    lax.fori_loop(0, PAIRS, pass_one, 0)

    stats[0] = statc[...].T[: 2 * 16]
    stat_copies = [
        remote(stats.at[0], stats.at[d], st_send.at[d - 1], st_recv.at[d - 1], (dp, shift(-d)))
        for d in range(1, REACH + 1)
    ]
    for copy in stat_copies:
        copy.start()

    emb[...] = nn(hot[pl.ds(REACH * B, B), :], table[...])
    select(qtab, query, (REACH + 1) * B, B, REACH * B, True, HEAD_DIM ** (-0.5))

    att_t = att[...].T

    def out_terms(p, carry):
        lanes = pl.ds(pl.multiple_of(p * B, B), B)
        got = nn(att_t, cot_all[0, :, lanes]).astype(BF)
        for block in range(4):
            out_term[p % 2, block, p // 2] = got[block * 192 : (block + 1) * 192]
        return carry

    lax.fori_loop(0, PAIRS, out_terms, 0)
    oc = remote(out_term.at[1 - c], out_core, oc_send.at[0], oc_recv.at[0], (y * 2 + 1 - c, sq))
    oc.start()

    for d in range(1, 3):
        gatt[pl.ds(d * B, B), :] = nt(cot_all[d], wo[...]).astype(BF)
    relays[2].wait_recv()
    relays[3].start()
    gatt[pl.ds(3 * B, B), :] = nt(cot_all[3], wo[...]).astype(BF)

    oc.wait_recv()
    for block in range(4):
        out_x[block] = (out_term[c, block].astype(F32) + out_core[block].astype(F32)).astype(BF)

    def ox(step):
        return remote(
            out_x.at[other_x(step)], out_x_in.at[step - 1], ox_send.at[step - 1], ox_recv.at[step - 1],
            (dp, seq_of(other_x(step), z)),
        )

    for step in range(1, 4):
        ox(step).start()

    relays[3].wait_recv()
    gatt[pl.ds(REACH * B, B), :] = nt(cot_all[REACH], wo[...]).astype(BF)
    for copy in stat_copies:
        copy.wait_recv()

    def oy(step):
        return remote(
            out_y.at[lax.min(other_y(step), 2)], out_y_in.at[step - 1], oy_send.at[step - 1], oy_recv.at[step - 1],
            (other_y(step) * 2 + c, sq),
        )

    def pass_two(p, carry):
        lanes = pl.ds(pl.multiple_of(p * B, B), B)
        k2 = stacked(keys[pl.ds(REACH * B, B), lanes])
        v2 = stacked(values[pl.ds(REACH * B, B), lanes])
        for d in range(REACH + 1):
            q, g = query[pl.ds(d * B, B), lanes], gatt[pl.ds(d * B, B), lanes]
            reach = seeing[:, pl.ds(d * B, B)]
            allowed = jnp.concatenate([reach < window_ref[2 * p], reach < window_ref[2 * p + 1]], axis=0)

            def spread(j):
                a = jnp.broadcast_to(stats[d, pl.ds(16 * j + 2 * p, 1), :], (B, B))
                b = jnp.broadcast_to(stats[d, pl.ds(16 * j + 2 * p + 1, 1), :], (B, B))
                return jnp.concatenate([a, b], axis=0)

            probs = jnp.exp(jnp.where(allowed, nt(k2, q) - spread(0), -1e30))
            ds = probs * (nt(v2, g) - spread(1))
            probs_s[:, pl.ds(d * B, B)] = probs.astype(BF)
            ds_s[:, pl.ds(d * B, B)] = ds.astype(BF)
        grad_value = picked(nn(probs_s[...], gatt[:, lanes])).astype(BF)
        grad_key = unrope(picked(nn(ds_s[...], query[:, lanes])), own_cos, own_sin).astype(BF)
        gv[:, lanes] = grad_value
        gk[:, lanes] = grad_key

        @pl.when(p != dp)
        def _():
            kv_out[p, 0] = grad_key
            kv_out[p, 1] = grad_value
            kv_copy(p).start()

        @pl.when(p == dp)
        def _():
            kv_in[dp, 0] = grad_key
            kv_in[dp, 1] = grad_value

        @pl.when(p == 4)
        def _():
            for step in range(1, 4):
                ox(step).wait_recv()
            for row in range(3):
                total = out_x[x, row].astype(F32)
                for step in range(3):
                    total += out_x_in[step, row].astype(F32)
                out_y[row] = total.astype(BF)
            for step in range(1, 4):
                @pl.when(other_y(step) < 3)
                def _():
                    oy(step).start()

        return carry

    lax.fori_loop(0, PAIRS, pass_two, 0)

    grad_normed = nt(gq[...], wq[...]) + nt(gk[...], wk[...]) + nt(gv[...], wv[...])
    own = emb[...]
    inv = lax.rsqrt(jnp.mean(own * own, axis=1, keepdims=True) + EPSILON)
    scaled = own * inv
    gin_ref[...] = (
        inv * (grad_normed - scaled * jnp.mean(grad_normed * scaled, axis=1, keepdims=True))
    ).astype(BF)

    def tok(step, target):
        return remote(
            tok_sum.at[target], tok_in.at[step - 1], tok_send.at[step - 1], tok_recv.at[step - 1],
            (dp, seq_of(target, z)),
        )

    def oz_step(i):
        return lax.rem(2 * x + i - z + 8, 8)

    def oz(i):
        step = lax.max(oz_step(i), 1)
        return remote(
            out_z.at[i], out_z_in.at[step - 1], oz_send.at[i], oz_recv.at[step - 1], (dp, seq_of(x, 2 * x + i))
        )

    def oz_in(step):
        return remote(
            out_z.at[0], out_z_in.at[step - 1], oz_send.at[0], oz_recv.at[step - 1], (dp, seq_of(x, z))
        )

    def zs(step):
        return remote(
            z_out.at[other_z(step)], z_in.at[step - 1], z_send.at[step - 1], z_recv.at[step - 1],
            (dp, seq_of(x, other_z(step))),
        )

    mine = lax.min(dp, PAIRS - 1)

    def fin(step):
        return remote(
            final.at[mine], final.at[mine], fin_send.at[step - 1], fin_recv.at[mine], (other_dp(step), sq)
        )

    def out_fin():
        return remote(out_final, final.at[mine], of_send.at[0], of_recv.at[0], (dp, seq_of(3, z)))

    def fin_in(p):
        return remote(final.at[p], final.at[p], fin_send.at[0], fin_recv.at[p], (p, sq))

    for copy in idp_copies:
        copy.wait_recv()

    @pl.when(dp < PAIRS)
    def _():
        def hot_block(i, carry):
            owner = lax.rem(dp + i, 8)
            hot_dp[owner] = (token == ids_dp[i]).astype(BF)
            return carry

        lax.fori_loop(0, 8, hot_block, 0)

        for i in range(8):
            @pl.when(i != dp)
            def _():
                remote(q_out.at[0], q_in.at[i], q_send.at[0], q_recv.at[i], (mine, sq)).wait_recv()

        hot = jnp.concatenate([hot_dp[i] for i in range(8)], axis=1)
        tok_sum[0] = nn(hot, q_in[...].reshape(8 * B, B)).astype(BF)
        for i in range(8):
            @pl.when(i != dp)
            def _():
                remote(kv_out.at[0], kv_in.at[i], kv_send.at[0], kv_recv.at[i], (mine, sq)).wait_recv()
        tok_sum[1] = nn(hot, kv_in[:, 0].reshape(8 * B, B)).astype(BF)
        tok_sum[2] = nn(hot, kv_in[:, 1].reshape(8 * B, B)).astype(BF)
        for step in range(1, 4):
            @pl.when(other_x(step) < 3)
            def _():
                tok(step, lax.min(other_x(step), 2)).start()

        for step in range(1, 4):
            oy(step).wait_recv()
        total = out_y[lax.min(y, 2)].astype(F32)
        for step in range(3):
            total += out_y_in[step].astype(F32)
        out_z[...] = total.astype(BF).reshape(2, D // 8, B)
        for i in range(2):
            @pl.when(oz_step(i) != 0)
            def _():
                oz(i).start()

        @pl.when(x < 3)
        def _():
            for step in range(1, 4):
                tok(step, lax.min(x, 2)).wait_recv()
            total = tok_sum[lax.min(x, 2)].astype(F32)
            for step in range(3):
                total += tok_in[step].astype(F32)
            z_out[...] = tn(ntab[...], total.astype(BF)).astype(BF).reshape(8, D // 8, B)
            for step in range(1, 8):
                zs(step).start()

        @pl.when(z // 2 == x)
        def _():
            for step in range(1, 8):
                oz_in(step).wait_recv()
            total = out_z[z % 2].astype(F32)
            for step in range(7):
                total += out_z_in[step].astype(F32)
            out_final[...] = total.astype(BF)

            @pl.when(x < 3)
            def _():
                out_fin().start()

            @pl.when(x == 3)
            def _():
                final[mine] = out_final[...]

        @pl.when(x < 3)
        def _():
            for step in range(1, 8):
                zs(step).wait_recv()
            total = z_out[z].astype(F32)
            for step in range(7):
                total += z_in[step].astype(F32)
            final[mine] = total.astype(BF)

        @pl.when((x == 3) & (z < 6))
        def _():
            out_fin().wait_recv()

        for step in range(1, 8):
            fin(step).start()

    for p in range(PAIRS):
        @pl.when(dp != p)
        def _():
            fin_in(p).wait_recv()

        wg_ref[:, pl.ds(p * B, B)] = final[p].astype(F32)

    for copy in id_copies + idp_copies + relays + stat_copies + [oc] + [ox(step) for step in range(1, 4)]:
        copy.wait_send()
    for p in range(PAIRS):
        @pl.when(p != dp)
        def _():
            q_copy(p).wait_send()
            kv_copy(p).wait_send()
    for step in range(1, 4):
        @pl.when(other_y(step) < 3)
        def _():
            oy(step).wait_send()

    @pl.when(dp < PAIRS)
    def _():
        for step in range(1, 4):
            @pl.when(other_x(step) < 3)
            def _():
                tok(step, lax.min(other_x(step), 2)).wait_send()
        for i in range(2):
            @pl.when(oz_step(i) != 0)
            def _():
                oz(i).wait_send()

        @pl.when(x < 3)
        def _():
            for step in range(1, 8):
                zs(step).wait_send()

        @pl.when((z // 2 == x) & (x < 3))
        def _():
            out_fin().wait_send()

        for step in range(1, 8):
            fin(step).wait_send()


def on_device(token_ids, cotangent, table, w_query, w_key, w_value, w_out, window):
    tables = [jnp.asarray(part) for part in rope_tables()]
    vmem = pl.BlockSpec(memory_space=pltpu.VMEM)
    hbm = pl.BlockSpec(memory_space=pl.ANY)
    smem = pl.BlockSpec(memory_space=pltpu.SMEM)
    dma = pltpu.SemaphoreType.DMA
    grad_input, weight_grads = pl.pallas_call(
        kernel,
        out_shape=(
            jax.ShapeDtypeStruct((B, D), BF),
            jax.ShapeDtypeStruct((D // 8, D), F32),
        ),
        in_specs=[vmem] + [hbm] * 6 + [smem] + [vmem] * 4,
        out_specs=(vmem, vmem),
        scratch_shapes=[
            pltpu.VMEM((2 * REACH + 1, 1, B), jnp.int32),
            pltpu.VMEM((8, 1, B), jnp.int32),
            pltpu.VMEM((REACH + 1, B, D), BF),
            pltpu.VMEM((VOCAB, D), BF),
            pltpu.VMEM((D, D), BF),
            pltpu.VMEM((D, D), BF),
            pltpu.VMEM((D, D), BF),
            pltpu.VMEM((D, D), BF),
            pltpu.VMEM((VOCAB, D), BF),
            pltpu.VMEM((VOCAB, D), BF),
            pltpu.VMEM((VOCAB, D), BF),
            pltpu.VMEM((VOCAB, D), BF),
            pltpu.VMEM(((2 * REACH + 1) * B, VOCAB), BF),
            pltpu.VMEM((B, D), F32),
            pltpu.VMEM(((2 * REACH + 1) * B, B), F32),
            pltpu.VMEM(((2 * REACH + 1) * B, B), F32),
            pltpu.VMEM((B, SPAN), jnp.int32),
            pltpu.VMEM((B, SPAN), jnp.int32),
            pltpu.VMEM((SPAN, D), BF),
            pltpu.VMEM((SPAN, D), BF),
            pltpu.VMEM((SPAN, D), BF),
            pltpu.VMEM((SPAN, D), BF),
            pltpu.VMEM((B, D), BF),
            pltpu.VMEM((B, D), BF),
            pltpu.VMEM((B, D), BF),
            pltpu.VMEM((B, D), BF),
            pltpu.VMEM((B, B), F32),
            pltpu.VMEM((REACH + 1, 32, B), F32),
            pltpu.VMEM((2 * B, SPAN), BF),
            pltpu.VMEM((2 * B, SPAN), BF),
            pltpu.VMEM((8, VOCAB, B), BF),
            pltpu.VMEM((PAIRS, B, B), BF),
            pltpu.VMEM((PAIRS, 2, B, B), BF),
            pltpu.VMEM((8, B, B), BF),
            pltpu.VMEM((8, 2, B, B), BF),
            pltpu.VMEM((3, VOCAB, B), BF),
            pltpu.VMEM((3, VOCAB, B), BF),
            pltpu.VMEM((8, D // 8, B), BF),
            pltpu.VMEM((7, D // 8, B), BF),
            pltpu.VMEM((PAIRS, D // 8, B), BF),
            pltpu.VMEM((2, 4, 3, D // 4, B), BF),
            pltpu.VMEM((4, 3, D // 4, B), BF),
            pltpu.VMEM((4, 3, D // 4, B), BF),
            pltpu.VMEM((3, 3, D // 4, B), BF),
            pltpu.VMEM((3, D // 4, B), BF),
            pltpu.VMEM((3, D // 4, B), BF),
            pltpu.VMEM((2, D // 8, B), BF),
            pltpu.VMEM((7, D // 8, B), BF),
            pltpu.VMEM((D // 8, B), BF),
            dma((6,)), dma((8,)), dma((8,)), dma((7,)), dma((7,)), dma((4,)), dma((4,)), dma((4,)), dma((4,)),
            dma((PAIRS,)), dma((8,)), dma((PAIRS,)), dma((8,)), dma((3,)), dma((3,)), dma((7,)), dma((7,)),
            dma((7,)), dma((PAIRS,)),
            dma((1,)), dma((1,)), dma((3,)), dma((3,)), dma((3,)), dma((3,)), dma((2,)), dma((7,)), dma((1,)), dma((1,)),
        ],
        compiler_params=pltpu.CompilerParams(collective_id=0, has_side_effects=True),
    )(token_ids, cotangent[0], table, w_query, w_key, w_value, w_out, window, *tables)
    return (grad_input[None], weight_grads)


def solution(mesh):
    return jax.shard_map(
        on_device,
        mesh=mesh,
        in_specs=(P("dp", "seq"), P("dp", "seq", None), P(), P(), P(), P(), P(), P()),
        out_specs=(P("dp", "seq", None), P("seq", None)),
        check_vma=False,
    )
```

```python
import functools

import jax
import jax.numpy as jnp
import numpy as np
from jax import lax
from jax.experimental import pallas as pl
from jax.experimental.pallas import tpu as pltpu
from jax.sharding import PartitionSpec as P

D = 768
HEADS = 12
HEAD_DIM = 64
VOCAB = 256
WINDOW = 512
EPSILON = 1e-05
B = 128
SEQ_DEVS = 32
REACH = WINDOW // B
SPAN = (REACH + 1) * B
PAIRS = D // B
MESH = pl.DeviceIdType.MESH
BF = jnp.bfloat16
F32 = jnp.float32


def rope_tables():
    frequency = 10000.0 ** (-2.0 * np.arange(HEAD_DIM // 2) / HEAD_DIM)
    lane_frequency = np.tile(frequency, 4)[None, :]
    inside = np.arange(B)[:, None] * lane_frequency
    blocks = (np.arange(SEQ_DEVS) * B)[:, None] * lane_frequency
    return [
        np.asarray(part, np.float32)
        for part in (np.cos(inside), np.sin(inside), np.cos(blocks), np.sin(blocks))
    ]


def nn(a, b):
    return lax.dot_general(a, b, (((1,), (0,)), ((), ())), preferred_element_type=F32)


def nt(a, b):
    return lax.dot_general(a, b, (((1,), (1,)), ((), ())), preferred_element_type=F32)


def tn(a, b):
    return lax.dot_general(a, b, (((0,), (0,)), ((), ())), preferred_element_type=F32)


def swap_halves(x):
    lane = lax.broadcasted_iota(jnp.int32, x.shape, 1)
    first = (lane // (HEAD_DIM // 2)) % 2 == 0
    return jnp.where(first, pltpu.roll(x, B - HEAD_DIM // 2, 1), pltpu.roll(x, HEAD_DIM // 2, 1))


def rope(x, cosine, sine):
    return x * cosine + swap_halves(x) * sine


def unrope(x, cosine, sine):
    return x * cosine - swap_halves(x) * sine


def kernel(
    ids_ref, cot_hbm, table_hbm, wq_hbm, wk_hbm, wv_hbm, wo_hbm, window_ref, cr_ref, sr_ref, cb_ref, sb_ref,
    gin_ref, final,
    ids_all, ids_dp, cot_all, table, wq, wk, wv, wo, ntab_t, ntab, qtab, ktab, vtab, hot, emb, cosv, sinv, seen, seeing,
    keys, values, query, gatt, att, gq, gk, gv, statc, stats, probs_s, ds_s, hot_dp,
    q_out, kv_out, q_in, kv_in, tok_sum, tok_in, z_out, z_in,
    out_term, out_core, out_x, out_x_in, out_y, out_y_in, out_z, out_z_in, out_final,
    load_sem, ids_send, ids_recv, idp_send, idp_recv, cot_send, cot_recv, st_send, st_recv,
    q_send, q_recv, kv_send, kv_recv, tok_send, tok_recv, z_send, z_recv, fin_send, fin_recv,
    oc_send, oc_recv, ox_send, ox_recv, oy_send, oy_recv, oz_send, oz_recv, of_send, of_recv,
):
    dp = lax.axis_index("dp")
    sq = lax.axis_index("seq")
    x, z = sq // 8, sq % 8
    y, c = dp // 2, dp % 2
    base = sq * B

    loads = [
        pltpu.make_async_copy(src, dst, load_sem.at[i])
        for i, (src, dst) in enumerate(
            [(table_hbm, table), (cot_hbm, cot_all.at[0]), (wk_hbm, wk), (wv_hbm, wv), (wq_hbm, wq), (wo_hbm, wo)]
        )
    ]
    for load in loads:
        load.start()

    def seq_of(new_x, new_z):
        return new_x * 8 + new_z

    def shift(distance):
        return lax.rem(sq + distance + SEQ_DEVS, SEQ_DEVS)

    def other_dp(step):
        return lax.rem(dp + step, 8)

    def other_y(step):
        return lax.rem(y + step, 4)

    def other_x(step):
        return lax.rem(x + step, 4)

    def other_z(step):
        return lax.rem(z + step, 8)

    barrier = pltpu.get_barrier_semaphore()
    partners = [(dp, shift(d)) for d in (1, 2, 3, 4, -1, -2, -3, -4)]
    partners += [(other_dp(d), sq) for d in range(1, 8)]
    partners += [(dp, seq_of(other_x(d), z)) for d in range(1, 4)]
    partners += [(dp, seq_of(x, other_z(d))) for d in range(1, 8)]
    for partner in partners:
        pl.semaphore_signal(barrier, inc=1, device_id=partner, device_id_type=MESH)

    pl.semaphore_wait(barrier, len(partners))

    def remote(src, dst, send, recv, device):
        return pltpu.make_async_remote_copy(
            src_ref=src, dst_ref=dst, send_sem=send, recv_sem=recv, device_id=device, device_id_type=MESH
        )

    id_copies = []
    for i, d in enumerate((4, -4, 3, -3, 2, -2, 1, -1)):
        id_copies.append(remote(ids_ref, ids_all.at[d + REACH], ids_send.at[i], ids_recv.at[i], (dp, shift(-d))))
    idp_copies = []
    for d in range(1, 8):
        idp_copies.append(
            remote(ids_ref, ids_dp.at[8 - d], idp_send.at[d - 1], idp_recv.at[d - 1], (other_dp(d), sq))
        )

    def relay(step, half):
        rows = pl.ds(half * (B // 2), B // 2)
        source = cot_hbm.at[rows] if step == 0 else cot_all.at[step, rows]
        return remote(
            source, cot_all.at[step + 1, rows], cot_send.at[2 * step + half], cot_recv.at[2 * step + half],
            (dp, shift(-1)),
        )

    def forward(step, half):
        relay(step - 1, half).wait_recv()
        relay(step, half).start()

    for copy in id_copies:
        copy.start()
    relay(0, 0).start()
    relay(0, 1).start()
    for copy in idp_copies:
        copy.start()
    ids_all[REACH] = ids_ref[...]
    ids_dp[0] = ids_ref[...]

    lane_row = lax.broadcasted_iota(jnp.int32, (1, B), 1)
    sign = jnp.where((lane_row // (HEAD_DIM // 2)) % 2 == 0, -1.0, 1.0)

    def rope_block(i, carry):
        block = lax.rem(sq + i - REACH + SEQ_DEVS, SEQ_DEVS)
        cb = cb_ref[pl.ds(block, 1), :]
        sb = sb_ref[pl.ds(block, 1), :]
        rows = pl.ds(pl.multiple_of(i * B, B), B)
        cosv[rows, :] = cr_ref[...] * cb - sr_ref[...] * sb
        sinv[rows, :] = (sr_ref[...] * cb + cr_ref[...] * sb) * sign
        return carry

    lax.fori_loop(0, 2 * REACH + 1, rope_block, 0)

    loads[0].wait()
    rows_f = table[...].astype(F32)
    table_inv = lax.rsqrt(jnp.mean(rows_f * rows_f, axis=1, keepdims=True) + EPSILON)
    ntab[...] = (rows_f * table_inv).astype(BF)

    def project_table(w, out):
        def slab(j, carry):
            lanes = pl.ds(pl.multiple_of(j * 2 * B, B), 2 * B)
            out[:, lanes] = nn(ntab[...], w[:, lanes]).astype(BF)
            return carry

        lax.fori_loop(0, PAIRS // 2, slab, 0)

    loads[2].wait()
    project_table(wk, ktab)
    loads[3].wait()
    project_table(wv, vtab)
    forward(1, 0)
    loads[4].wait()
    project_table(wq, qtab)
    loads[5].wait()
    loads[1].wait()
    gatt[pl.ds(0, B), :] = nt(cot_all[0], wo[...]).astype(BF)

    far = 1 << 20
    dist = lax.broadcasted_iota(jnp.int32, (B, SPAN), 0) + WINDOW - lax.broadcasted_iota(jnp.int32, (B, SPAN), 1)
    col = lax.broadcasted_iota(jnp.int32, (B, SPAN), 1)
    seen[...] = jnp.where((dist >= 0) & (col >= WINDOW - base), dist, far)
    dist = col - lax.broadcasted_iota(jnp.int32, (B, SPAN), 0)
    seeing[...] = jnp.where((dist >= 0) & (col < SEQ_DEVS * B - base), dist, far)

    for copy in id_copies:
        copy.wait_recv()

    token = lax.broadcasted_iota(jnp.int32, (VOCAB, B), 0)

    def hot_rows(i, carry):
        hot[pl.ds(pl.multiple_of(i * B, B), B), :] = (token == ids_all[i]).astype(F32).T.astype(BF)
        return carry

    lax.fori_loop(0, 2 * REACH + 1, hot_rows, 0)

    def select(tab, out, first, to, count, rotated, scale):
        def slab(j, carry):
            lanes = pl.ds(pl.multiple_of(j * 2 * B, B), 2 * B)
            got = nn(hot[pl.ds(first, count), :], tab[:, lanes])
            for half in range(2):
                part = got[:, half * B : (half + 1) * B]
                if rotated:
                    part = rope(part, cosv[pl.ds(first, count), :], sinv[pl.ds(first, count), :])
                if scale != 1.0:
                    part = part * scale
                out[pl.ds(to, count), pl.ds(pl.multiple_of((2 * j + half) * B, B), B)] = part.astype(BF)
            return carry

        lax.fori_loop(0, PAIRS // 2, slab, 0)

    forward(1, 1)
    select(ktab, keys, 0, 0, SPAN, True, 1.0)
    select(vtab, values, 0, 0, SPAN, False, 1.0)
    select(qtab, query, REACH * B, 0, B, True, HEAD_DIM ** (-0.5))
    forward(2, 0)

    lane_one = lax.broadcasted_iota(jnp.int32, (1, B), 1)
    left = (lane_one < HEAD_DIM).astype(BF)
    right = (lane_one >= HEAD_DIM).astype(BF)

    def stacked(a):
        return jnp.concatenate([a * left, a * right], axis=0)

    def picked(a):
        return jnp.where(lane_one < HEAD_DIM, a[:B], a[B:])

    own_cos = cosv[pl.ds(REACH * B, B), :]
    own_sin = sinv[pl.ds(REACH * B, B), :]
    statc[...] = jnp.zeros_like(statc)

    def q_copy(p):
        return remote(q_out.at[p], q_in.at[dp], q_send.at[p], q_recv.at[dp], (p, sq))

    def kv_copy(p):
        return remote(kv_out.at[p], kv_in.at[dp], kv_send.at[p], kv_recv.at[dp], (p, sq))

    def stat_copy(part, d):
        at = REACH * part + d - 1
        return remote(stats.at[part, 0], stats.at[part, d], st_send.at[at], st_recv.at[at], (dp, shift(-d)))

    def pass_one(p, carry):
        lanes = pl.ds(pl.multiple_of(p * B, B), B)
        k, v = keys[:, lanes], values[:, lanes]
        scores = nt(stacked(query[pl.ds(0, B), lanes]), k)
        reach = seen[...]
        masked = jnp.concatenate(
            [
                jnp.where(reach < window_ref[2 * p], scores[:B], -1e30),
                jnp.where(reach < window_ref[2 * p + 1], scores[B:], -1e30),
            ],
            axis=0,
        )
        top = jnp.max(masked, axis=1, keepdims=True)
        weights = jnp.exp(masked - top)
        whole = jnp.sum(weights, axis=1, keepdims=True)
        probs = weights * (1.0 / whole)
        grad_probs = nt(stacked(gatt[pl.ds(0, B), lanes]), v)
        row_term = jnp.sum(probs * grad_probs, axis=1, keepdims=True)
        ds = (probs * (grad_probs - row_term)).astype(BF)
        att[:, lanes] = picked(nn(probs.astype(BF), v)).astype(BF)
        grad_query = picked(nn(ds, k)) * HEAD_DIM ** (-0.5)
        got = unrope(grad_query, own_cos, own_sin).astype(BF)
        gq[:, lanes] = got

        @pl.when(p != dp)
        def _():
            q_out[p] = got
            q_copy(p).start()

        @pl.when(p == dp)
        def _():
            q_in[dp] = got

        held = statc[...]
        for j, stat in enumerate((top + jnp.log(whole), row_term)):
            first = 16 * (p // 3) + 8 * j + 2 * (p % 3)
            held = jnp.where(lane_one == first, stat[:B], held)
            held = jnp.where(lane_one == first + 1, stat[B:], held)
        statc[...] = held

        @pl.when(p == 1)
        def _():
            forward(2, 1)

        @pl.when(p == 2)
        def _():
            stats[0, 0] = statc[...].T[:16]
            for d in range(REACH, 0, -1):
                stat_copy(0, d).start()

        @pl.when(p == 3)
        def _():
            forward(3, 0)

        return carry

    lax.fori_loop(0, PAIRS, pass_one, 0)

    stats[1, 0] = statc[...].T[16:32]
    for d in range(REACH, 0, -1):
        stat_copy(1, d).start()
    forward(3, 1)

    ntab_t[...] = ntab[...].T
    emb[...] = nn(hot[pl.ds(REACH * B, B), :], table[...])
    select(qtab, query, (REACH + 1) * B, B, REACH * B, True, HEAD_DIM ** (-0.5))

    att_t = att[...].T

    def out_terms(p, carry):
        lanes = pl.ds(pl.multiple_of(p * B, B), B)
        got = nn(att_t, cot_all[0, :, lanes]).astype(BF)
        for block in range(4):
            out_term[p % 2, block, p // 2] = got[block * 192 : (block + 1) * 192]
        return carry

    lax.fori_loop(0, PAIRS, out_terms, 0)
    oc = remote(out_term.at[1 - c], out_core, oc_send.at[0], oc_recv.at[0], (y * 2 + 1 - c, sq))
    oc.start()

    for d in range(1, 4):
        gatt[pl.ds(d * B, B), :] = nt(cot_all[d], wo[...]).astype(BF)

    def tok(step, target):
        return remote(
            tok_sum.at[target], tok_in.at[step - 1], tok_send.at[step - 1], tok_recv.at[step - 1],
            (dp, seq_of(target, z)),
        )

    def oz_step(i):
        return lax.rem(2 * x + i - z + 8, 8)

    def oz(i):
        step = lax.max(oz_step(i), 1)
        return remote(
            out_z.at[i], out_z_in.at[step - 1], oz_send.at[i], oz_recv.at[step - 1], (dp, seq_of(x, 2 * x + i))
        )

    def oz_in(step):
        return remote(
            out_z.at[0], out_z_in.at[step - 1], oz_send.at[0], oz_recv.at[step - 1], (dp, seq_of(x, z))
        )

    def zs(step):
        return remote(
            z_out.at[other_z(step)], z_in.at[step - 1], z_send.at[step - 1], z_recv.at[step - 1],
            (dp, seq_of(x, other_z(step))),
        )

    mine = lax.min(dp, PAIRS - 1)

    def fin(step):
        return remote(
            final.at[mine], final.at[mine], fin_send.at[step - 1], fin_recv.at[mine], (other_dp(step), sq)
        )

    def out_fin():
        return remote(out_final, final.at[mine], of_send.at[0], of_recv.at[0], (dp, seq_of(3, z)))

    def fin_in(p):
        return remote(final.at[p], final.at[p], fin_send.at[0], fin_recv.at[p], (p, sq))

    oc.wait_recv()
    for block in range(4):
        out_x[block] = (out_term[c, block].astype(F32) + out_core[block].astype(F32)).astype(BF)

    def ox(step):
        return remote(
            out_x.at[other_x(step)], out_x_in.at[step - 1], ox_send.at[step - 1], ox_recv.at[step - 1],
            (dp, seq_of(other_x(step), z)),
        )

    for step in range(1, 4):
        ox(step).start()

    for copy in idp_copies:
        copy.wait_recv()

    def hot_of_all():
        return jnp.concatenate([hot_dp[i] for i in range(8)], axis=1)

    @pl.when(dp < PAIRS)
    def _():
        def hot_block(i, carry):
            owner = lax.rem(dp + i, 8)
            hot_dp[owner] = (token == ids_dp[i]).astype(BF)
            return carry

        lax.fori_loop(0, 8, hot_block, 0)

        for i in range(8):
            @pl.when(i != dp)
            def _():
                remote(q_out.at[0], q_in.at[i], q_send.at[0], q_recv.at[i], (mine, sq)).wait_recv()

        tok_sum[0] = nn(hot_of_all(), q_in[...].reshape(8 * B, B)).astype(BF)
        for step in range(1, 4):
            @pl.when(other_x(step) == 0)
            def _():
                tok(step, 0).start()

    for half in range(2):
        relay(3, half).wait_recv()
    gatt[pl.ds(REACH * B, B), :] = nt(cot_all[REACH], wo[...]).astype(BF)
    for d in range(1, REACH + 1):
        stat_copy(0, d).wait_recv()

    def oy(step):
        return remote(
            out_y.at[lax.min(other_y(step), 2)], out_y_in.at[step - 1], oy_send.at[step - 1], oy_recv.at[step - 1],
            (other_y(step) * 2 + c, sq),
        )

    def pass_two(p, carry):
        @pl.when(p == 3)
        def _():
            for d in range(1, REACH + 1):
                stat_copy(1, d).wait_recv()

        lanes = pl.ds(pl.multiple_of(p * B, B), B)
        k2 = stacked(keys[pl.ds(REACH * B, B), lanes])
        v2 = stacked(values[pl.ds(REACH * B, B), lanes])
        for d in range(REACH + 1):
            q, g = query[pl.ds(d * B, B), lanes], gatt[pl.ds(d * B, B), lanes]
            reach = seeing[:, pl.ds(d * B, B)]
            allowed = jnp.concatenate([reach < window_ref[2 * p], reach < window_ref[2 * p + 1]], axis=0)

            def spread(j):
                first = 8 * j + 2 * (p % 3)
                a = jnp.broadcast_to(stats[p // 3, d, pl.ds(first, 1), :], (B, B))
                b = jnp.broadcast_to(stats[p // 3, d, pl.ds(first + 1, 1), :], (B, B))
                return jnp.concatenate([a, b], axis=0)

            probs = jnp.exp(jnp.where(allowed, nt(k2, q) - spread(0), -1e30))
            ds = probs * (nt(v2, g) - spread(1))
            probs_s[:, pl.ds(d * B, B)] = probs.astype(BF)
            ds_s[:, pl.ds(d * B, B)] = ds.astype(BF)
        grad_value = picked(nn(probs_s[...], gatt[:, lanes])).astype(BF)
        grad_key = unrope(picked(nn(ds_s[...], query[:, lanes])), own_cos, own_sin).astype(BF)
        gv[:, lanes] = grad_value
        gk[:, lanes] = grad_key

        @pl.when(p != dp)
        def _():
            kv_out[p, 0] = grad_key
            kv_out[p, 1] = grad_value
            kv_copy(p).start()

        @pl.when(p == dp)
        def _():
            kv_in[dp, 0] = grad_key
            kv_in[dp, 1] = grad_value

        @pl.when(p == 2)
        def _():
            for step in range(1, 4):
                ox(step).wait_recv()
            for row in range(3):
                total = out_x[x, row].astype(F32)
                for step in range(3):
                    total += out_x_in[step, row].astype(F32)
                out_y[row] = total.astype(BF)
            for step in range(1, 4):
                @pl.when(other_y(step) < 3)
                def _():
                    oy(step).start()

        @pl.when((p == 5) & (dp < PAIRS))
        def _():
            for step in range(1, 4):
                oy(step).wait_recv()
            total = out_y[lax.min(y, 2)].astype(F32)
            for step in range(3):
                total += out_y_in[step].astype(F32)
            out_z[...] = total.astype(BF).reshape(2, D // 8, B)
            for i in range(2):
                @pl.when(oz_step(i) != 0)
                def _():
                    oz(i).start()

        return carry

    lax.fori_loop(0, PAIRS, pass_two, 0)

    grad_normed = nt(gq[...], wq[...]) + nt(gk[...], wk[...]) + nt(gv[...], wv[...])
    own = emb[...]
    inv = lax.rsqrt(jnp.mean(own * own, axis=1, keepdims=True) + EPSILON)
    scaled = own * inv
    gin_ref[...] = (
        inv * (grad_normed - scaled * jnp.mean(grad_normed * scaled, axis=1, keepdims=True))
    ).astype(BF)

    @pl.when(dp < PAIRS)
    def _():
        for i in range(8):
            @pl.when(i != dp)
            def _():
                remote(kv_out.at[0], kv_in.at[i], kv_send.at[0], kv_recv.at[i], (mine, sq)).wait_recv()
        hot_all = hot_of_all()
        tok_sum[1] = nn(hot_all, kv_in[:, 0].reshape(8 * B, B)).astype(BF)
        tok_sum[2] = nn(hot_all, kv_in[:, 1].reshape(8 * B, B)).astype(BF)
        for step in range(1, 4):
            @pl.when((other_x(step) > 0) & (other_x(step) < 3))
            def _():
                tok(step, lax.clamp(1, other_x(step), 2)).start()

        @pl.when(x < 3)
        def _():
            for step in range(1, 4):
                tok(step, lax.min(x, 2)).wait_recv()
            total = tok_sum[lax.min(x, 2)].astype(F32)
            for step in range(3):
                total += tok_in[step].astype(F32)
            z_out[...] = nn(ntab_t[...], total.astype(BF)).astype(BF).reshape(8, D // 8, B)
            for step in (4, 3, 5, 2, 6, 1, 7):
                zs(step).start()

        @pl.when(z // 2 == x)
        def _():
            for step in range(1, 8):
                oz_in(step).wait_recv()
            total = out_z[z % 2].astype(F32)
            for step in range(7):
                total += out_z_in[step].astype(F32)
            out_final[...] = total.astype(BF)

            @pl.when(x < 3)
            def _():
                out_fin().start()

            @pl.when(x == 3)
            def _():
                final[mine] = out_final[...]

        @pl.when(x < 3)
        def _():
            for step in range(1, 8):
                zs(step).wait_recv()
            total = z_out[z].astype(F32)
            for step in range(7):
                total += z_in[step].astype(F32)
            final[mine] = total.astype(BF)

        @pl.when((x == 3) & (z < 6))
        def _():
            out_fin().wait_recv()

        for step in (4, 3, 5, 2, 6, 1, 7):
            fin(step).start()

    for p in range(PAIRS):
        @pl.when(dp != p)
        def _():
            fin_in(p).wait_recv()

    relays = [relay(step, half) for step in range(REACH) for half in range(2)]
    stat_copies = [stat_copy(part, d) for part in range(2) for d in range(1, REACH + 1)]
    for copy in id_copies + idp_copies + relays + stat_copies + [oc] + [ox(step) for step in range(1, 4)]:
        copy.wait_send()
    for p in range(PAIRS):
        @pl.when(p != dp)
        def _():
            q_copy(p).wait_send()
            kv_copy(p).wait_send()
    for step in range(1, 4):
        @pl.when(other_y(step) < 3)
        def _():
            oy(step).wait_send()

    @pl.when(dp < PAIRS)
    def _():
        for step in range(1, 4):
            @pl.when(other_x(step) < 3)
            def _():
                tok(step, lax.min(other_x(step), 2)).wait_send()
        for i in range(2):
            @pl.when(oz_step(i) != 0)
            def _():
                oz(i).wait_send()

        @pl.when(x < 3)
        def _():
            for step in range(1, 8):
                zs(step).wait_send()

        @pl.when((z // 2 == x) & (x < 3))
        def _():
            out_fin().wait_send()

        for step in range(1, 8):
            fin(step).wait_send()


def finish(gin_ref, pieces_ref, gin_out, wg_out):
    gin_out[...] = gin_ref[...]
    for p in range(PAIRS):
        wg_out[:, pl.ds(p * B, B)] = pieces_ref[p].astype(F32)


def on_device(token_ids, cotangent, table, w_query, w_key, w_value, w_out, window):
    tables = [jnp.asarray(part) for part in rope_tables()]
    vmem = pl.BlockSpec(memory_space=pltpu.VMEM)
    hbm = pl.BlockSpec(memory_space=pl.ANY)
    smem = pl.BlockSpec(memory_space=pltpu.SMEM)
    dma = pltpu.SemaphoreType.DMA
    grad_input, pieces = pl.pallas_call(
        kernel,
        out_shape=(
            jax.ShapeDtypeStruct((B, D), BF),
            jax.ShapeDtypeStruct((PAIRS, D // 8, B), BF),
        ),
        in_specs=[vmem] + [hbm] * 6 + [smem] + [vmem] * 4,
        out_specs=(vmem, vmem),
        scratch_shapes=[
            pltpu.VMEM((2 * REACH + 1, 1, B), jnp.int32),
            pltpu.VMEM((8, 1, B), jnp.int32),
            pltpu.VMEM((REACH + 1, B, D), BF),
            pltpu.VMEM((VOCAB, D), BF),
            pltpu.VMEM((D, D), BF),
            pltpu.VMEM((D, D), BF),
            pltpu.VMEM((D, D), BF),
            pltpu.VMEM((D, D), BF),
            pltpu.VMEM((D, VOCAB), BF),
            pltpu.VMEM((VOCAB, D), BF),
            pltpu.VMEM((VOCAB, D), BF),
            pltpu.VMEM((VOCAB, D), BF),
            pltpu.VMEM((VOCAB, D), BF),
            pltpu.VMEM(((2 * REACH + 1) * B, VOCAB), BF),
            pltpu.VMEM((B, D), F32),
            pltpu.VMEM(((2 * REACH + 1) * B, B), F32),
            pltpu.VMEM(((2 * REACH + 1) * B, B), F32),
            pltpu.VMEM((B, SPAN), jnp.int32),
            pltpu.VMEM((B, SPAN), jnp.int32),
            pltpu.VMEM((SPAN, D), BF),
            pltpu.VMEM((SPAN, D), BF),
            pltpu.VMEM((SPAN, D), BF),
            pltpu.VMEM((SPAN, D), BF),
            pltpu.VMEM((B, D), BF),
            pltpu.VMEM((B, D), BF),
            pltpu.VMEM((B, D), BF),
            pltpu.VMEM((B, D), BF),
            pltpu.VMEM((B, B), F32),
            pltpu.VMEM((2, REACH + 1, 16, B), F32),
            pltpu.VMEM((2 * B, SPAN), BF),
            pltpu.VMEM((2 * B, SPAN), BF),
            pltpu.VMEM((8, VOCAB, B), BF),
            pltpu.VMEM((PAIRS, B, B), BF),
            pltpu.VMEM((PAIRS, 2, B, B), BF),
            pltpu.VMEM((8, B, B), BF),
            pltpu.VMEM((8, 2, B, B), BF),
            pltpu.VMEM((3, VOCAB, B), BF),
            pltpu.VMEM((3, VOCAB, B), BF),
            pltpu.VMEM((8, D // 8, B), BF),
            pltpu.VMEM((7, D // 8, B), BF),
            pltpu.VMEM((2, 4, 3, D // 4, B), BF),
            pltpu.VMEM((4, 3, D // 4, B), BF),
            pltpu.VMEM((4, 3, D // 4, B), BF),
            pltpu.VMEM((3, 3, D // 4, B), BF),
            pltpu.VMEM((3, D // 4, B), BF),
            pltpu.VMEM((3, D // 4, B), BF),
            pltpu.VMEM((2, D // 8, B), BF),
            pltpu.VMEM((7, D // 8, B), BF),
            pltpu.VMEM((D // 8, B), BF),
            dma((6,)), dma((8,)), dma((8,)), dma((7,)), dma((7,)), dma((8,)), dma((8,)), dma((8,)), dma((8,)),
            dma((PAIRS,)), dma((8,)), dma((PAIRS,)), dma((8,)), dma((3,)), dma((3,)), dma((7,)), dma((7,)),
            dma((7,)), dma((PAIRS,)),
            dma((1,)), dma((1,)), dma((3,)), dma((3,)), dma((3,)), dma((3,)), dma((2,)), dma((7,)), dma((1,)), dma((1,)),
        ],
        compiler_params=pltpu.CompilerParams(collective_id=0, has_side_effects=True),
    )(token_ids, cotangent[0], table, w_query, w_key, w_value, w_out, window, *tables)
    grad_input, weight_grads = pl.pallas_call(
        finish,
        out_shape=(
            jax.ShapeDtypeStruct((B, D), BF),
            jax.ShapeDtypeStruct((D // 8, D), F32),
        ),
        in_specs=[vmem, vmem],
        out_specs=(vmem, vmem),
    )(grad_input, pieces)
    return (grad_input[None], weight_grads)


def solution(mesh):
    return jax.shard_map(
        on_device,
        mesh=mesh,
        in_specs=(P("dp", "seq"), P("dp", "seq", None), P(), P(), P(), P(), P(), P()),
        out_specs=(P("dp", "seq", None), P("seq", None)),
        check_vma=False,
    )
```

```python
import functools

import jax
import jax.numpy as jnp
import numpy as np
from jax import lax
from jax.experimental import pallas as pl
from jax.experimental.pallas import tpu as pltpu
from jax.sharding import PartitionSpec as P

D = 768
HEADS = 12
HEAD_DIM = 64
VOCAB = 256
WINDOW = 512
EPSILON = 1e-05
B = 128
SEQ_DEVS = 32
REACH = WINDOW // B
SPAN = (REACH + 1) * B
PAIRS = D // B
MESH = pl.DeviceIdType.MESH
BF = jnp.bfloat16
F32 = jnp.float32


def rope_tables():
    frequency = 10000.0 ** (-2.0 * np.arange(HEAD_DIM // 2) / HEAD_DIM)
    lane_frequency = np.tile(frequency, 4)[None, :]
    inside = np.arange(B)[:, None] * lane_frequency
    blocks = (np.arange(SEQ_DEVS) * B)[:, None] * lane_frequency
    return [
        np.asarray(part, np.float32)
        for part in (np.cos(inside), np.sin(inside), np.cos(blocks), np.sin(blocks))
    ]


def nn(a, b):
    return lax.dot_general(a, b, (((1,), (0,)), ((), ())), preferred_element_type=F32)


def nt(a, b):
    return lax.dot_general(a, b, (((1,), (1,)), ((), ())), preferred_element_type=F32)


def tn(a, b):
    return lax.dot_general(a, b, (((0,), (0,)), ((), ())), preferred_element_type=F32)


def swap_halves(x):
    lane = lax.broadcasted_iota(jnp.int32, x.shape, 1)
    first = (lane // (HEAD_DIM // 2)) % 2 == 0
    return jnp.where(first, pltpu.roll(x, B - HEAD_DIM // 2, 1), pltpu.roll(x, HEAD_DIM // 2, 1))


def rope(x, cosine, sine):
    return x * cosine + swap_halves(x) * sine


def unrope(x, cosine, sine):
    return x * cosine - swap_halves(x) * sine


def kernel(
    ids_ref, cot_hbm, table_hbm, wq_hbm, wk_hbm, wv_hbm, wo_hbm, window_ref, cr_ref, sr_ref, cb_ref, sb_ref,
    gin_ref, final,
    ids_all, ids_dp, cot_all, table, wq, wk, wv, wo, ntab_t, ntab, qtab, ktab, vtab, hot, emb, cosv, sinv, seen, seeing,
    keys, values, query, gatt, att, gq, gk, gv, statc, stats, probs_s, ds_s, hot_dp,
    q_out, kv_out, q_in, kv_in, tok_sum, tok_in, z_out, z_in,
    out_term, out_core, out_x, out_x_in, out_y, out_y_in, out_z, out_z_in, out_final,
    load_sem, ids_send, ids_recv, idp_send, idp_recv, cot_send, cot_recv, st_send, st_recv,
    q_send, q_recv, kv_send, kv_recv, tok_send, tok_recv, z_send, z_recv, fin_send, fin_recv,
    oc_send, oc_recv, ox_send, ox_recv, oy_send, oy_recv, oz_send, oz_recv, of_send, of_recv,
):
    dp = lax.axis_index("dp")
    sq = lax.axis_index("seq")
    x, z = sq // 8, sq % 8
    y, c = dp // 2, dp % 2
    base = sq * B

    loads = [
        pltpu.make_async_copy(src, dst, load_sem.at[i])
        for i, (src, dst) in enumerate(
            [(table_hbm, table), (cot_hbm, cot_all.at[0]), (wk_hbm, wk), (wv_hbm, wv), (wq_hbm, wq), (wo_hbm, wo)]
        )
    ]
    for load in loads:
        load.start()

    def seq_of(new_x, new_z):
        return new_x * 8 + new_z

    def shift(distance):
        return lax.rem(sq + distance + SEQ_DEVS, SEQ_DEVS)

    def other_dp(step):
        return lax.rem(dp + step, 8)

    def other_y(step):
        return lax.rem(y + step, 4)

    def other_x(step):
        return lax.rem(x + step, 4)

    def other_z(step):
        return lax.rem(z + step, 8)

    barrier = pltpu.get_barrier_semaphore()
    partners = [(dp, shift(d)) for d in (1, 2, 3, 4, -1, -2, -3, -4)]
    partners += [(other_dp(d), sq) for d in range(1, 8)]
    partners += [(dp, seq_of(other_x(d), z)) for d in range(1, 4)]
    partners += [(dp, seq_of(x, other_z(d))) for d in range(1, 8)]
    for partner in partners:
        pl.semaphore_signal(barrier, inc=1, device_id=partner, device_id_type=MESH)

    pl.semaphore_wait(barrier, len(partners))

    def remote(src, dst, send, recv, device):
        return pltpu.make_async_remote_copy(
            src_ref=src, dst_ref=dst, send_sem=send, recv_sem=recv, device_id=device, device_id_type=MESH
        )

    id_copies = []
    for i, d in enumerate((4, -4, 3, -3, 2, -2, 1, -1)):
        id_copies.append(remote(ids_ref, ids_all.at[d + REACH], ids_send.at[i], ids_recv.at[i], (dp, shift(-d))))
    idp_copies = []
    for d in range(1, 8):
        idp_copies.append(
            remote(ids_ref, ids_dp.at[8 - d], idp_send.at[d - 1], idp_recv.at[d - 1], (other_dp(d), sq))
        )

    def relay(step, half):
        rows = pl.ds(half * (B // 2), B // 2)
        source = cot_hbm.at[rows] if step == 0 else cot_all.at[step, rows]
        return remote(
            source, cot_all.at[step + 1, rows], cot_send.at[2 * step + half], cot_recv.at[2 * step + half],
            (dp, shift(-1)),
        )

    def forward(step, half):
        relay(step - 1, half).wait_recv()
        relay(step, half).start()

    for copy in id_copies:
        copy.start()
    relay(0, 0).start()
    relay(0, 1).start()
    for copy in idp_copies:
        copy.start()
    ids_all[REACH] = ids_ref[...]
    ids_dp[0] = ids_ref[...]

    lane_row = lax.broadcasted_iota(jnp.int32, (1, B), 1)
    sign = jnp.where((lane_row // (HEAD_DIM // 2)) % 2 == 0, -1.0, 1.0)

    def rope_block(i, carry):
        block = lax.rem(sq + i - REACH + SEQ_DEVS, SEQ_DEVS)
        cb = cb_ref[pl.ds(block, 1), :]
        sb = sb_ref[pl.ds(block, 1), :]
        rows = pl.ds(pl.multiple_of(i * B, B), B)
        cosv[rows, :] = cr_ref[...] * cb - sr_ref[...] * sb
        sinv[rows, :] = (sr_ref[...] * cb + cr_ref[...] * sb) * sign
        return carry

    lax.fori_loop(0, 2 * REACH + 1, rope_block, 0)

    loads[0].wait()
    rows_f = table[...].astype(F32)
    table_inv = lax.rsqrt(jnp.mean(rows_f * rows_f, axis=1, keepdims=True) + EPSILON)
    ntab[...] = (rows_f * table_inv).astype(BF)

    def project_table(w, out):
        def slab(j, carry):
            lanes = pl.ds(pl.multiple_of(j * 2 * B, B), 2 * B)
            out[:, lanes] = nn(ntab[...], w[:, lanes]).astype(BF)
            return carry

        lax.fori_loop(0, PAIRS // 2, slab, 0)

    loads[2].wait()
    project_table(wk, ktab)
    loads[3].wait()
    project_table(wv, vtab)
    forward(1, 0)
    loads[4].wait()
    project_table(wq, qtab)
    loads[5].wait()
    loads[1].wait()
    gatt[pl.ds(0, B), :] = nt(cot_all[0], wo[...]).astype(BF)

    far = 1 << 20
    dist = lax.broadcasted_iota(jnp.int32, (B, SPAN), 0) + WINDOW - lax.broadcasted_iota(jnp.int32, (B, SPAN), 1)
    col = lax.broadcasted_iota(jnp.int32, (B, SPAN), 1)
    seen[...] = jnp.where((dist >= 0) & (col >= WINDOW - base), dist, far)
    dist = col - lax.broadcasted_iota(jnp.int32, (B, SPAN), 0)
    seeing[...] = jnp.where((dist >= 0) & (col < SEQ_DEVS * B - base), dist, far)

    for copy in id_copies:
        copy.wait_recv()

    token = lax.broadcasted_iota(jnp.int32, (VOCAB, B), 0)

    def hot_rows(i, carry):
        hot[pl.ds(pl.multiple_of(i * B, B), B), :] = (token == ids_all[i]).astype(F32).T.astype(BF)
        return carry

    lax.fori_loop(0, 2 * REACH + 1, hot_rows, 0)

    def select(tab, out, first, to, count, rotated, scale):
        def slab(j, carry):
            lanes = pl.ds(pl.multiple_of(j * 2 * B, B), 2 * B)
            got = nn(hot[pl.ds(first, count), :], tab[:, lanes])
            for half in range(2):
                part = got[:, half * B : (half + 1) * B]
                if rotated:
                    part = rope(part, cosv[pl.ds(first, count), :], sinv[pl.ds(first, count), :])
                if scale != 1.0:
                    part = part * scale
                out[pl.ds(to, count), pl.ds(pl.multiple_of((2 * j + half) * B, B), B)] = part.astype(BF)
            return carry

        lax.fori_loop(0, PAIRS // 2, slab, 0)

    forward(1, 1)
    select(ktab, keys, 0, 0, SPAN, True, 1.0)
    select(vtab, values, 0, 0, SPAN, False, 1.0)
    select(qtab, query, REACH * B, 0, B, True, HEAD_DIM ** (-0.5))
    forward(2, 0)

    lane_one = lax.broadcasted_iota(jnp.int32, (1, B), 1)
    left = (lane_one < HEAD_DIM).astype(BF)
    right = (lane_one >= HEAD_DIM).astype(BF)

    def stacked(a):
        return jnp.concatenate([a * left, a * right], axis=0)

    def picked(a):
        return jnp.where(lane_one < HEAD_DIM, a[:B], a[B:])

    own_cos = cosv[pl.ds(REACH * B, B), :]
    own_sin = sinv[pl.ds(REACH * B, B), :]
    statc[...] = jnp.zeros_like(statc)

    def q_copy(p):
        return remote(q_out.at[p], q_in.at[dp], q_send.at[p], q_recv.at[dp], (p, sq))

    def kv_copy(p):
        return remote(kv_out.at[p], kv_in.at[dp], kv_send.at[p], kv_recv.at[dp], (p, sq))

    def stat_copy(part, d):
        at = REACH * part + d - 1
        return remote(stats.at[part, 0], stats.at[part, d], st_send.at[at], st_recv.at[at], (dp, shift(-d)))

    def pass_one(p):
        lanes = pl.ds(pl.multiple_of(p * B, B), B)
        k, v = keys[:, lanes], values[:, lanes]
        scores = nt(stacked(query[pl.ds(0, B), lanes]), k)
        reach = seen[...]
        masked = jnp.concatenate(
            [
                jnp.where(reach < window_ref[2 * p], scores[:B], -1e30),
                jnp.where(reach < window_ref[2 * p + 1], scores[B:], -1e30),
            ],
            axis=0,
        )
        top = jnp.max(masked, axis=1, keepdims=True)
        weights = jnp.exp(masked - top)
        whole = jnp.sum(weights, axis=1, keepdims=True)
        probs = weights * (1.0 / whole)
        grad_probs = nt(stacked(gatt[pl.ds(0, B), lanes]), v)
        row_term = jnp.sum(probs * grad_probs, axis=1, keepdims=True)
        ds = (probs * (grad_probs - row_term)).astype(BF)
        att[:, lanes] = picked(nn(probs.astype(BF), v)).astype(BF)
        grad_query = picked(nn(ds, k)) * HEAD_DIM ** (-0.5)
        got = unrope(grad_query, own_cos, own_sin).astype(BF)
        gq[:, lanes] = got

        q_out[p] = got
        held = statc[...]
        for j, stat in enumerate((top + jnp.log(whole), row_term)):
            first = 16 * (p // 4) + 8 * j + 2 * (p % 4)
            held = jnp.where(lane_one == first, stat[:B], held)
            held = jnp.where(lane_one == first + 1, stat[B:], held)
        statc[...] = held


    def send_q(p):
        @pl.when(p != dp)
        def _():
            q_copy(p).start()

        @pl.when(p == dp)
        def _():
            q_in[dp] = q_out[p]

    def pass_one_pairs(i, carry):
        pass_one(2 * i)
        pass_one(2 * i + 1)
        send_q(2 * i)
        send_q(2 * i + 1)

        @pl.when(i == 0)
        def _():
            forward(2, 1)

        @pl.when(i == 1)
        def _():
            stats[0, 0] = statc[...].T[:16]
            for d in range(REACH, 0, -1):
                stat_copy(0, d).start()
            forward(3, 0)

        return carry

    lax.fori_loop(0, PAIRS // 2, pass_one_pairs, 0)

    stats[1, 0] = statc[...].T[16:32]
    for d in range(REACH, 0, -1):
        stat_copy(1, d).start()
    forward(3, 1)

    ntab_t[...] = ntab[...].T
    emb[...] = nn(hot[pl.ds(REACH * B, B), :], table[...])
    select(qtab, query, (REACH + 1) * B, B, REACH * B, True, HEAD_DIM ** (-0.5))

    att_t = att[...].T

    def out_terms(p, carry):
        lanes = pl.ds(pl.multiple_of(p * B, B), B)
        got = nn(att_t, cot_all[0, :, lanes]).astype(BF)
        for block in range(4):
            out_term[p % 2, block, p // 2] = got[block * 192 : (block + 1) * 192]
        return carry

    lax.fori_loop(0, PAIRS, out_terms, 0)
    oc = remote(out_term.at[1 - c], out_core, oc_send.at[0], oc_recv.at[0], (y * 2 + 1 - c, sq))
    oc.start()

    for d in range(1, 4):
        gatt[pl.ds(d * B, B), :] = nt(cot_all[d], wo[...]).astype(BF)

    def tok(step, target):
        return remote(
            tok_sum.at[target], tok_in.at[step - 1], tok_send.at[step - 1], tok_recv.at[step - 1],
            (dp, seq_of(target, z)),
        )

    def oz_step(i):
        return lax.rem(2 * x + i - z + 8, 8)

    def oz(i):
        step = lax.max(oz_step(i), 1)
        return remote(
            out_z.at[i], out_z_in.at[step - 1], oz_send.at[i], oz_recv.at[step - 1], (dp, seq_of(x, 2 * x + i))
        )

    def oz_in(step):
        return remote(
            out_z.at[0], out_z_in.at[step - 1], oz_send.at[0], oz_recv.at[step - 1], (dp, seq_of(x, z))
        )

    def zs(step):
        return remote(
            z_out.at[other_z(step)], z_in.at[step - 1], z_send.at[step - 1], z_recv.at[step - 1],
            (dp, seq_of(x, other_z(step))),
        )

    mine = lax.min(dp, PAIRS - 1)

    def fin(step):
        return remote(
            final.at[mine], final.at[mine], fin_send.at[step - 1], fin_recv.at[mine], (other_dp(step), sq)
        )

    def out_fin():
        return remote(out_final, final.at[mine], of_send.at[0], of_recv.at[0], (dp, seq_of(3, z)))

    def fin_in(p):
        return remote(final.at[p], final.at[p], fin_send.at[0], fin_recv.at[p], (p, sq))

    oc.wait_recv()
    for block in range(4):
        out_x[block] = (out_term[c, block].astype(F32) + out_core[block].astype(F32)).astype(BF)

    def ox(step):
        return remote(
            out_x.at[other_x(step)], out_x_in.at[step - 1], ox_send.at[step - 1], ox_recv.at[step - 1],
            (dp, seq_of(other_x(step), z)),
        )

    for step in range(1, 4):
        ox(step).start()

    for copy in idp_copies:
        copy.wait_recv()

    def hot_of_all():
        return jnp.concatenate([hot_dp[i] for i in range(8)], axis=1)

    @pl.when(dp < PAIRS)
    def _():
        def hot_block(i, carry):
            owner = lax.rem(dp + i, 8)
            hot_dp[owner] = (token == ids_dp[i]).astype(BF)
            return carry

        lax.fori_loop(0, 8, hot_block, 0)

        for i in range(8):
            @pl.when(i != dp)
            def _():
                remote(q_out.at[0], q_in.at[i], q_send.at[0], q_recv.at[i], (mine, sq)).wait_recv()

        tok_sum[0] = nn(hot_of_all(), q_in[...].reshape(8 * B, B)).astype(BF)
        for step in range(1, 4):
            @pl.when(other_x(step) == 0)
            def _():
                tok(step, 0).start()

    for half in range(2):
        relay(3, half).wait_recv()
    gatt[pl.ds(REACH * B, B), :] = nt(cot_all[REACH], wo[...]).astype(BF)
    for d in range(1, REACH + 1):
        stat_copy(0, d).wait_recv()

    def oy(step):
        return remote(
            out_y.at[lax.min(other_y(step), 2)], out_y_in.at[step - 1], oy_send.at[step - 1], oy_recv.at[step - 1],
            (other_y(step) * 2 + c, sq),
        )

    def pass_two(i, slot):
        p = 2 * i + slot
        lanes = pl.ds(pl.multiple_of(p * B, B), B)
        k2 = stacked(keys[pl.ds(REACH * B, B), lanes])
        v2 = stacked(values[pl.ds(REACH * B, B), lanes])
        for d in range(REACH + 1):
            q, g = query[pl.ds(d * B, B), lanes], gatt[pl.ds(d * B, B), lanes]
            reach = seeing[:, pl.ds(d * B, B)]
            allowed = jnp.concatenate([reach < window_ref[2 * p], reach < window_ref[2 * p + 1]], axis=0)

            def spread(j):
                first = 8 * j + 2 * (p % 4)
                a = jnp.broadcast_to(stats[p // 4, d, pl.ds(first, 1), :], (B, B))
                b = jnp.broadcast_to(stats[p // 4, d, pl.ds(first + 1, 1), :], (B, B))
                return jnp.concatenate([a, b], axis=0)

            probs = jnp.exp(jnp.where(allowed, nt(k2, q) - spread(0), -1e30))
            ds = probs * (nt(v2, g) - spread(1))
            probs_s[slot, :, pl.ds(d * B, B)] = probs.astype(BF)
            ds_s[slot, :, pl.ds(d * B, B)] = ds.astype(BF)
        grad_value = picked(nn(probs_s[slot], gatt[:, lanes])).astype(BF)
        grad_key = unrope(picked(nn(ds_s[slot], query[:, lanes])), own_cos, own_sin).astype(BF)
        gv[:, lanes] = grad_value
        gk[:, lanes] = grad_key

        kv_out[p, 0] = grad_key
        kv_out[p, 1] = grad_value

    def send_kv(p):
        @pl.when(p != dp)
        def _():
            kv_copy(p).start()

        @pl.when(p == dp)
        def _():
            kv_in[dp] = kv_out[p]

    def pass_two_pairs(i, carry):
        @pl.when(i == 2)
        def _():
            for d in range(1, REACH + 1):
                stat_copy(1, d).wait_recv()

        pass_two(i, 0)
        pass_two(i, 1)
        send_kv(2 * i)
        send_kv(2 * i + 1)
        return carry

    lax.fori_loop(0, PAIRS // 2, pass_two_pairs, 0)

    for step in range(1, 4):
        ox(step).wait_recv()
    for row in range(3):
        total = out_x[x, row].astype(F32)
        for step in range(3):
            total += out_x_in[step, row].astype(F32)
        out_y[row] = total.astype(BF)
    for step in range(1, 4):
        @pl.when(other_y(step) < 3)
        def _():
            oy(step).start()

    grad_normed = nt(gq[...], wq[...]) + nt(gk[...], wk[...]) + nt(gv[...], wv[...])
    own = emb[...]
    inv = lax.rsqrt(jnp.mean(own * own, axis=1, keepdims=True) + EPSILON)
    scaled = own * inv
    gin_ref[...] = (
        inv * (grad_normed - scaled * jnp.mean(grad_normed * scaled, axis=1, keepdims=True))
    ).astype(BF)

    @pl.when(dp < PAIRS)
    def _():
        for i in range(8):
            @pl.when(i != dp)
            def _():
                remote(kv_out.at[0], kv_in.at[i], kv_send.at[0], kv_recv.at[i], (mine, sq)).wait_recv()
        hot_all = hot_of_all()
        tok_sum[1] = nn(hot_all, kv_in[:, 0].reshape(8 * B, B)).astype(BF)
        tok_sum[2] = nn(hot_all, kv_in[:, 1].reshape(8 * B, B)).astype(BF)
        for step in range(1, 4):
            @pl.when((other_x(step) > 0) & (other_x(step) < 3))
            def _():
                tok(step, lax.clamp(1, other_x(step), 2)).start()

        for step in range(1, 4):
            oy(step).wait_recv()
        total = out_y[lax.min(y, 2)].astype(F32)
        for step in range(3):
            total += out_y_in[step].astype(F32)
        out_z[...] = total.astype(BF).reshape(2, D // 8, B)
        for i in range(2):
            @pl.when(oz_step(i) != 0)
            def _():
                oz(i).start()

        @pl.when(x < 3)
        def _():
            for step in range(1, 4):
                tok(step, lax.min(x, 2)).wait_recv()
            total = tok_sum[lax.min(x, 2)].astype(F32)
            for step in range(3):
                total += tok_in[step].astype(F32)
            z_out[...] = nn(ntab_t[...], total.astype(BF)).astype(BF).reshape(8, D // 8, B)
            for step in (4, 3, 5, 2, 6, 1, 7):
                zs(step).start()

        @pl.when(z // 2 == x)
        def _():
            for step in range(1, 8):
                oz_in(step).wait_recv()
            total = out_z[z % 2].astype(F32)
            for step in range(7):
                total += out_z_in[step].astype(F32)
            out_final[...] = total.astype(BF)

            @pl.when(x < 3)
            def _():
                out_fin().start()

            @pl.when(x == 3)
            def _():
                final[mine] = out_final[...]

        @pl.when(x < 3)
        def _():
            for step in range(1, 8):
                zs(step).wait_recv()
            total = z_out[z].astype(F32)
            for step in range(7):
                total += z_in[step].astype(F32)
            final[mine] = total.astype(BF)

        @pl.when((x == 3) & (z < 6))
        def _():
            out_fin().wait_recv()

        for step in (4, 3, 5, 2, 6, 1, 7):
            fin(step).start()

    for p in range(PAIRS):
        @pl.when(dp != p)
        def _():
            fin_in(p).wait_recv()

    relays = [relay(step, half) for step in range(REACH) for half in range(2)]
    stat_copies = [stat_copy(part, d) for part in range(2) for d in range(1, REACH + 1)]
    for copy in id_copies + idp_copies + relays + stat_copies + [oc] + [ox(step) for step in range(1, 4)]:
        copy.wait_send()
    for p in range(PAIRS):
        @pl.when(p != dp)
        def _():
            q_copy(p).wait_send()
            kv_copy(p).wait_send()
    for step in range(1, 4):
        @pl.when(other_y(step) < 3)
        def _():
            oy(step).wait_send()

    @pl.when(dp < PAIRS)
    def _():
        for step in range(1, 4):
            @pl.when(other_x(step) < 3)
            def _():
                tok(step, lax.min(other_x(step), 2)).wait_send()
        for i in range(2):
            @pl.when(oz_step(i) != 0)
            def _():
                oz(i).wait_send()

        @pl.when(x < 3)
        def _():
            for step in range(1, 8):
                zs(step).wait_send()

        @pl.when((z // 2 == x) & (x < 3))
        def _():
            out_fin().wait_send()

        for step in range(1, 8):
            fin(step).wait_send()


def finish(gin_ref, pieces_ref, gin_out, wg_out):
    gin_out[...] = gin_ref[...]
    for p in range(PAIRS):
        wg_out[:, pl.ds(p * B, B)] = pieces_ref[p].astype(F32)


def on_device(token_ids, cotangent, table, w_query, w_key, w_value, w_out, window):
    tables = [jnp.asarray(part) for part in rope_tables()]
    vmem = pl.BlockSpec(memory_space=pltpu.VMEM)
    hbm = pl.BlockSpec(memory_space=pl.ANY)
    smem = pl.BlockSpec(memory_space=pltpu.SMEM)
    dma = pltpu.SemaphoreType.DMA
    grad_input, pieces = pl.pallas_call(
        kernel,
        out_shape=(
            jax.ShapeDtypeStruct((B, D), BF),
            jax.ShapeDtypeStruct((PAIRS, D // 8, B), BF),
        ),
        in_specs=[vmem] + [hbm] * 6 + [smem] + [vmem] * 4,
        out_specs=(vmem, vmem),
        scratch_shapes=[
            pltpu.VMEM((2 * REACH + 1, 1, B), jnp.int32),
            pltpu.VMEM((8, 1, B), jnp.int32),
            pltpu.VMEM((REACH + 1, B, D), BF),
            pltpu.VMEM((VOCAB, D), BF),
            pltpu.VMEM((D, D), BF),
            pltpu.VMEM((D, D), BF),
            pltpu.VMEM((D, D), BF),
            pltpu.VMEM((D, D), BF),
            pltpu.VMEM((D, VOCAB), BF),
            pltpu.VMEM((VOCAB, D), BF),
            pltpu.VMEM((VOCAB, D), BF),
            pltpu.VMEM((VOCAB, D), BF),
            pltpu.VMEM((VOCAB, D), BF),
            pltpu.VMEM(((2 * REACH + 1) * B, VOCAB), BF),
            pltpu.VMEM((B, D), F32),
            pltpu.VMEM(((2 * REACH + 1) * B, B), F32),
            pltpu.VMEM(((2 * REACH + 1) * B, B), F32),
            pltpu.VMEM((B, SPAN), jnp.int32),
            pltpu.VMEM((B, SPAN), jnp.int32),
            pltpu.VMEM((SPAN, D), BF),
            pltpu.VMEM((SPAN, D), BF),
            pltpu.VMEM((SPAN, D), BF),
            pltpu.VMEM((SPAN, D), BF),
            pltpu.VMEM((B, D), BF),
            pltpu.VMEM((B, D), BF),
            pltpu.VMEM((B, D), BF),
            pltpu.VMEM((B, D), BF),
            pltpu.VMEM((B, B), F32),
            pltpu.VMEM((2, REACH + 1, 16, B), F32),
            pltpu.VMEM((2, 2 * B, SPAN), BF),
            pltpu.VMEM((2, 2 * B, SPAN), BF),
            pltpu.VMEM((8, VOCAB, B), BF),
            pltpu.VMEM((PAIRS, B, B), BF),
            pltpu.VMEM((PAIRS, 2, B, B), BF),
            pltpu.VMEM((8, B, B), BF),
            pltpu.VMEM((8, 2, B, B), BF),
            pltpu.VMEM((3, VOCAB, B), BF),
            pltpu.VMEM((3, VOCAB, B), BF),
            pltpu.VMEM((8, D // 8, B), BF),
            pltpu.VMEM((7, D // 8, B), BF),
            pltpu.VMEM((2, 4, 3, D // 4, B), BF),
            pltpu.VMEM((4, 3, D // 4, B), BF),
            pltpu.VMEM((4, 3, D // 4, B), BF),
            pltpu.VMEM((3, 3, D // 4, B), BF),
            pltpu.VMEM((3, D // 4, B), BF),
            pltpu.VMEM((3, D // 4, B), BF),
            pltpu.VMEM((2, D // 8, B), BF),
            pltpu.VMEM((7, D // 8, B), BF),
            pltpu.VMEM((D // 8, B), BF),
            dma((6,)), dma((8,)), dma((8,)), dma((7,)), dma((7,)), dma((8,)), dma((8,)), dma((8,)), dma((8,)),
            dma((PAIRS,)), dma((8,)), dma((PAIRS,)), dma((8,)), dma((3,)), dma((3,)), dma((7,)), dma((7,)),
            dma((7,)), dma((PAIRS,)),
            dma((1,)), dma((1,)), dma((3,)), dma((3,)), dma((3,)), dma((3,)), dma((2,)), dma((7,)), dma((1,)), dma((1,)),
        ],
        compiler_params=pltpu.CompilerParams(collective_id=0, has_side_effects=True),
    )(token_ids, cotangent[0], table, w_query, w_key, w_value, w_out, window, *tables)
    grad_input, weight_grads = pl.pallas_call(
        finish,
        out_shape=(
            jax.ShapeDtypeStruct((B, D), BF),
            jax.ShapeDtypeStruct((D // 8, D), F32),
        ),
        in_specs=[vmem, vmem],
        out_specs=(vmem, vmem),
    )(grad_input, pieces)
    return (grad_input[None], weight_grads)


def solution(mesh):
    return jax.shard_map(
        on_device,
        mesh=mesh,
        in_specs=(P("dp", "seq"), P("dp", "seq", None), P(), P(), P(), P(), P(), P()),
        out_specs=(P("dp", "seq", None), P("seq", None)),
        check_vma=False,
    )
```

```python
import functools

import jax
import jax.numpy as jnp
import numpy as np
from jax import lax
from jax.experimental import pallas as pl
from jax.experimental.pallas import tpu as pltpu
from jax.sharding import PartitionSpec as P

D = 768
HEADS = 12
HEAD_DIM = 64
VOCAB = 256
WINDOW = 512
EPSILON = 1e-05
B = 128
SEQ_DEVS = 32
REACH = WINDOW // B
SPAN = (REACH + 1) * B
PAIRS = D // B
MESH = pl.DeviceIdType.MESH
BF = jnp.bfloat16
F32 = jnp.float32


def rope_tables():
    frequency = 10000.0 ** (-2.0 * np.arange(HEAD_DIM // 2) / HEAD_DIM)
    lane_frequency = np.tile(frequency, 4)[None, :]
    inside = np.arange(B)[:, None] * lane_frequency
    blocks = (np.arange(SEQ_DEVS) * B)[:, None] * lane_frequency
    return [
        np.asarray(part, np.float32)
        for part in (np.cos(inside), np.sin(inside), np.cos(blocks), np.sin(blocks))
    ]


def nn(a, b):
    return lax.dot_general(a, b, (((1,), (0,)), ((), ())), preferred_element_type=F32)


def nt(a, b):
    return lax.dot_general(a, b, (((1,), (1,)), ((), ())), preferred_element_type=F32)


def tn(a, b):
    return lax.dot_general(a, b, (((0,), (0,)), ((), ())), preferred_element_type=F32)


def swap_halves(x):
    lane = lax.broadcasted_iota(jnp.int32, x.shape, 1)
    first = (lane // (HEAD_DIM // 2)) % 2 == 0
    return jnp.where(first, pltpu.roll(x, B - HEAD_DIM // 2, 1), pltpu.roll(x, HEAD_DIM // 2, 1))


def rope(x, cosine, sine):
    return x * cosine + swap_halves(x) * sine


def unrope(x, cosine, sine):
    return x * cosine - swap_halves(x) * sine


def kernel(
    ids_ref, cot_hbm, table_hbm, wq_hbm, wk_hbm, wv_hbm, wo_hbm, window_ref, cr_ref, sr_ref, cb_ref, sb_ref,
    gin_ref, final,
    ids_all, ids_dp, cot_all, table, wq, wk, wv, wo, ntab_t, ntab, qtab, ktab, vtab, hot, emb, cosv, sinv, seen, seeing,
    keys, values, query, gatt, att, gq, gk, gv, statc, stats, probs_s, ds_s, hot_dp,
    q_out, kv_out, q_in, kv_in, tok_sum, tok_in, z_out, z_in,
    out_term, out_core, out_x, out_x_in, out_y, out_y_in, out_z, out_z_in, out_final,
    load_sem, ids_send, ids_recv, idp_send, idp_recv, cot_send, cot_recv, st_send, st_recv,
    q_send, q_recv, kv_send, kv_recv, tok_send, tok_recv, z_send, z_recv, fin_send, fin_recv,
    oc_send, oc_recv, ox_send, ox_recv, oy_send, oy_recv, oz_send, oz_recv, of_send, of_recv,
):
    dp = lax.axis_index("dp")
    sq = lax.axis_index("seq")
    x, z = sq // 8, sq % 8
    y, c = dp // 2, dp % 2
    base = sq * B

    loads = [
        pltpu.make_async_copy(src, dst, load_sem.at[i])
        for i, (src, dst) in enumerate(
            [(table_hbm, table), (cot_hbm, cot_all.at[0]), (wk_hbm, wk), (wv_hbm, wv), (wq_hbm, wq), (wo_hbm, wo)]
        )
    ]
    for load in loads:
        load.start()

    def seq_of(new_x, new_z):
        return new_x * 8 + new_z

    def shift(distance):
        return lax.rem(sq + distance + SEQ_DEVS, SEQ_DEVS)

    def other_dp(step):
        return lax.rem(dp + step, 8)

    def other_y(step):
        return lax.rem(y + step, 4)

    def other_x(step):
        return lax.rem(x + step, 4)

    def other_z(step):
        return lax.rem(z + step, 8)

    barrier = pltpu.get_barrier_semaphore()
    partners = [(dp, shift(d)) for d in (1, 2, 3, 4, -1, -2, -3, -4)]
    partners += [(other_dp(d), sq) for d in range(1, 8)]
    partners += [(dp, seq_of(other_x(d), z)) for d in range(1, 4)]
    partners += [(dp, seq_of(x, other_z(d))) for d in range(1, 8)]
    for partner in partners:
        pl.semaphore_signal(barrier, inc=1, device_id=partner, device_id_type=MESH)

    pl.semaphore_wait(barrier, len(partners))

    def remote(src, dst, send, recv, device):
        return pltpu.make_async_remote_copy(
            src_ref=src, dst_ref=dst, send_sem=send, recv_sem=recv, device_id=device, device_id_type=MESH
        )

    id_copies = []
    for i, d in enumerate((4, -4, 3, -3, 2, -2, 1, -1)):
        id_copies.append(remote(ids_ref, ids_all.at[d + REACH], ids_send.at[i], ids_recv.at[i], (dp, shift(-d))))
    idp_copies = []
    for d in range(1, 8):
        idp_copies.append(
            remote(ids_ref, ids_dp.at[8 - d], idp_send.at[d - 1], idp_recv.at[d - 1], (other_dp(d), sq))
        )

    def relay(step, half):
        rows = pl.ds(half * (B // 2), B // 2)
        source = cot_hbm.at[rows] if step == 0 else cot_all.at[step, rows]
        return remote(
            source, cot_all.at[step + 1, rows], cot_send.at[2 * step + half], cot_recv.at[2 * step + half],
            (dp, shift(-1)),
        )

    def forward(step, half):
        relay(step - 1, half).wait_recv()
        relay(step, half).start()

    for copy in id_copies:
        copy.start()
    relay(0, 0).start()
    relay(0, 1).start()
    for copy in idp_copies:
        copy.start()
    ids_all[REACH] = ids_ref[...]
    ids_dp[0] = ids_ref[...]

    lane_row = lax.broadcasted_iota(jnp.int32, (1, B), 1)
    sign = jnp.where((lane_row // (HEAD_DIM // 2)) % 2 == 0, -1.0, 1.0)

    def rope_block(i, carry):
        block = lax.rem(sq + i - REACH + SEQ_DEVS, SEQ_DEVS)
        cb = cb_ref[pl.ds(block, 1), :]
        sb = sb_ref[pl.ds(block, 1), :]
        rows = pl.ds(pl.multiple_of(i * B, B), B)
        cosv[rows, :] = cr_ref[...] * cb - sr_ref[...] * sb
        sinv[rows, :] = (sr_ref[...] * cb + cr_ref[...] * sb) * sign
        return carry

    lax.fori_loop(0, 2 * REACH + 1, rope_block, 0)

    loads[0].wait()
    rows_f = table[...].astype(F32)
    table_inv = lax.rsqrt(jnp.mean(rows_f * rows_f, axis=1, keepdims=True) + EPSILON)
    ntab[...] = (rows_f * table_inv).astype(BF)

    def project_table(w, out):
        def slab(j, carry):
            lanes = pl.ds(pl.multiple_of(j * 2 * B, B), 2 * B)
            out[:, lanes] = nn(ntab[...], w[:, lanes]).astype(BF)
            return carry

        lax.fori_loop(0, PAIRS // 2, slab, 0)

    loads[2].wait()
    project_table(wk, ktab)
    loads[3].wait()
    project_table(wv, vtab)
    forward(1, 0)
    loads[4].wait()
    project_table(wq, qtab)
    loads[5].wait()
    loads[1].wait()
    gatt[pl.ds(0, B), :] = nt(cot_all[0], wo[...]).astype(BF)

    far = 1 << 20
    dist = lax.broadcasted_iota(jnp.int32, (B, SPAN), 0) + WINDOW - lax.broadcasted_iota(jnp.int32, (B, SPAN), 1)
    col = lax.broadcasted_iota(jnp.int32, (B, SPAN), 1)
    seen[...] = jnp.where((dist >= 0) & (col >= WINDOW - base), dist, far)
    dist = col - lax.broadcasted_iota(jnp.int32, (B, SPAN), 0)
    seeing[...] = jnp.where((dist >= 0) & (col < SEQ_DEVS * B - base), dist, far)

    for copy in id_copies:
        copy.wait_recv()

    token = lax.broadcasted_iota(jnp.int32, (VOCAB, B), 0)

    def hot_rows(i, carry):
        hot[pl.ds(pl.multiple_of(i * B, B), B), :] = (token == ids_all[i]).astype(F32).T.astype(BF)
        return carry

    lax.fori_loop(0, 2 * REACH + 1, hot_rows, 0)

    def select(tab, out, first, to, count, rotated, scale):
        def slab(j, carry):
            lanes = pl.ds(pl.multiple_of(j * 2 * B, B), 2 * B)
            got = nn(hot[pl.ds(first, count), :], tab[:, lanes])
            for half in range(2):
                part = got[:, half * B : (half + 1) * B]
                if rotated:
                    part = rope(part, cosv[pl.ds(first, count), :], sinv[pl.ds(first, count), :])
                if scale != 1.0:
                    part = part * scale
                out[pl.ds(to, count), pl.ds(pl.multiple_of((2 * j + half) * B, B), B)] = part.astype(BF)
            return carry

        lax.fori_loop(0, PAIRS // 2, slab, 0)

    forward(1, 1)
    select(ktab, keys, 0, 0, SPAN, True, 1.0)
    select(vtab, values, 0, 0, SPAN, False, 1.0)
    select(qtab, query, REACH * B, 0, B, True, HEAD_DIM ** (-0.5))
    forward(2, 0)

    lane_one = lax.broadcasted_iota(jnp.int32, (1, B), 1)
    left = (lane_one < HEAD_DIM).astype(BF)
    right = (lane_one >= HEAD_DIM).astype(BF)

    def stacked(a):
        return jnp.concatenate([a * left, a * right], axis=0)

    def picked(a):
        return jnp.where(lane_one < HEAD_DIM, a[:B], a[B:])

    own_cos = cosv[pl.ds(REACH * B, B), :]
    own_sin = sinv[pl.ds(REACH * B, B), :]
    statc[...] = jnp.zeros_like(statc)

    def q_copy(p):
        return remote(q_out.at[p], q_in.at[dp], q_send.at[p], q_recv.at[dp], (p, sq))

    def kv_copy(p):
        return remote(kv_out.at[p], kv_in.at[dp], kv_send.at[p], kv_recv.at[dp], (p, sq))

    def stat_copy(part, d):
        at = REACH * part + d - 1
        return remote(stats.at[part, 0], stats.at[part, d], st_send.at[at], st_recv.at[at], (dp, shift(-d)))

    def pair_of(i, slot):
        return 3 + i if slot else 2 - i

    def pass_one(i, slot):
        p = pair_of(i, slot)
        lanes = pl.ds(pl.multiple_of(p * B, B), B)
        k, v = keys[:, lanes], values[:, lanes]
        scores = nt(stacked(query[pl.ds(0, B), lanes]), k)
        reach = seen[...]
        masked = jnp.concatenate(
            [
                jnp.where(reach < window_ref[2 * p], scores[:B], -1e30),
                jnp.where(reach < window_ref[2 * p + 1], scores[B:], -1e30),
            ],
            axis=0,
        )
        top = jnp.max(masked, axis=1, keepdims=True)
        weights = jnp.exp(masked - top)
        whole = jnp.sum(weights, axis=1, keepdims=True)
        probs = weights * (1.0 / whole)
        grad_probs = nt(stacked(gatt[pl.ds(0, B), lanes]), v)
        row_term = jnp.sum(probs * grad_probs, axis=1, keepdims=True)
        ds = (probs * (grad_probs - row_term)).astype(BF)
        att[:, lanes] = picked(nn(probs.astype(BF), v)).astype(BF)
        grad_query = picked(nn(ds, k)) * HEAD_DIM ** (-0.5)
        got = unrope(grad_query, own_cos, own_sin).astype(BF)
        gq[:, lanes] = got

        q_out[p] = got
        held = statc[...]
        for j, stat in enumerate((top + jnp.log(whole), row_term)):
            first = 16 * (i // 2) + 8 * j + 2 * (2 * (i % 2) + slot)
            held = jnp.where(lane_one == first, stat[:B], held)
            held = jnp.where(lane_one == first + 1, stat[B:], held)
        statc[...] = held


    def send_q(p):
        @pl.when(p != dp)
        def _():
            q_copy(p).start()

        @pl.when(p == dp)
        def _():
            q_in[dp] = q_out[p]

    def out_terms(first, count, blocks):
        att_t = att[:, pl.ds(first, count)].T

        def one_pair(p, carry):
            lanes = pl.ds(pl.multiple_of(p * B, B), B)
            got = nn(att_t, cot_all[0, :, lanes]).astype(BF)
            for block in blocks:
                start = block * (D // 4) - first
                out_term[p % 2, block, p // 2] = got[start : start + D // 4]
            return carry

        lax.fori_loop(0, PAIRS, one_pair, 0)
        for block in blocks:
            oc(block).start()

    def oc(block):
        return remote(
            out_term.at[1 - c, block], out_core.at[block], oc_send.at[block], oc_recv.at[block],
            (y * 2 + 1 - c, sq),
        )

    def ox(step):
        return remote(
            out_x.at[other_x(step)], out_x_in.at[step - 1], ox_send.at[step - 1], ox_recv.at[step - 1],
            (dp, seq_of(other_x(step), z)),
        )

    def out_core_sum(blocks):
        for block in blocks:
            oc(block).wait_recv()
            out_x[block] = (out_term[c, block].astype(F32) + out_core[block].astype(F32)).astype(BF)
        for step in range(1, 4):
            for block in blocks:
                @pl.when(other_x(step) == block)
                def _():
                    ox(step).start()

    def pass_one_pairs(i, carry):
        for slot in range(2):
            pass_one(i, slot)
        for slot in range(2):
            send_q(pair_of(i, slot))

        @pl.when(i == 0)
        def _():
            forward(2, 1)

        @pl.when(i == 1)
        def _():
            stats[0, 0] = statc[...].T[:16]
            for d in range(REACH, 0, -1):
                stat_copy(0, d).start()
            forward(3, 0)
            out_terms(B, 4 * B, (1, 2))

        return carry

    lax.fori_loop(0, PAIRS // 2, pass_one_pairs, 0)

    stats[1, 0] = statc[...].T[16:32]
    for d in range(REACH, 0, -1):
        stat_copy(1, d).start()
    forward(3, 1)
    out_terms(0, D, (0, 3))
    out_core_sum((1, 2))

    ntab_t[...] = ntab[...].T
    emb[...] = nn(hot[pl.ds(REACH * B, B), :], table[...])
    select(qtab, query, (REACH + 1) * B, B, REACH * B, True, HEAD_DIM ** (-0.5))

    for d in range(1, 4):
        gatt[pl.ds(d * B, B), :] = nt(cot_all[d], wo[...]).astype(BF)

    def tok(step, target):
        return remote(
            tok_sum.at[target], tok_in.at[step - 1], tok_send.at[step - 1], tok_recv.at[step - 1],
            (dp, seq_of(target, z)),
        )

    def oz_step(i):
        return lax.rem(2 * x + i - z + 8, 8)

    def oz(i):
        step = lax.max(oz_step(i), 1)
        return remote(
            out_z.at[i], out_z_in.at[step - 1], oz_send.at[i], oz_recv.at[step - 1], (dp, seq_of(x, 2 * x + i))
        )

    def oz_in(step):
        return remote(
            out_z.at[0], out_z_in.at[step - 1], oz_send.at[0], oz_recv.at[step - 1], (dp, seq_of(x, z))
        )

    part_rows = D // 16

    def zs(step, half):
        rows = pl.ds(half * part_rows, part_rows)
        at = 7 * half + step - 1
        return remote(
            z_out.at[other_z(step), rows], z_in.at[step - 1, rows], z_send.at[at], z_recv.at[at],
            (dp, seq_of(x, other_z(step))),
        )

    mine = lax.min(dp, PAIRS - 1)

    def fin(step, half):
        part = final.at[mine, pl.ds(half * part_rows, part_rows)]
        return remote(
            part, part, fin_send.at[7 * half + step - 1], fin_recv.at[half, mine], (other_dp(step), sq)
        )

    def out_fin():
        return remote(out_final, final.at[mine], of_send.at[0], of_recv.at[0], (dp, seq_of(3, z)))

    def fin_in(p, half):
        part = final.at[p, pl.ds(half * part_rows, part_rows)]
        return remote(part, part, fin_send.at[0], fin_recv.at[half, p], (p, sq))

    out_core_sum((0, 3))

    for copy in idp_copies:
        copy.wait_recv()

    def hot_of_all():
        return jnp.concatenate([hot_dp[i] for i in range(8)], axis=1)

    @pl.when(dp < PAIRS)
    def _():
        def hot_block(i, carry):
            owner = lax.rem(dp + i, 8)
            hot_dp[owner] = (token == ids_dp[i]).astype(BF)
            return carry

        lax.fori_loop(0, 8, hot_block, 0)

        for i in range(8):
            @pl.when(i != dp)
            def _():
                remote(q_out.at[0], q_in.at[i], q_send.at[0], q_recv.at[i], (mine, sq)).wait_recv()

        tok_sum[0] = nn(hot_of_all(), q_in[...].reshape(8 * B, B)).astype(BF)
        for step in range(1, 4):
            @pl.when(other_x(step) == 0)
            def _():
                tok(step, 0).start()

    for half in range(2):
        relay(3, half).wait_recv()
    gatt[pl.ds(REACH * B, B), :] = nt(cot_all[REACH], wo[...]).astype(BF)
    for d in range(1, REACH + 1):
        stat_copy(0, d).wait_recv()

    def oy(step):
        return remote(
            out_y.at[lax.min(other_y(step), 2)], out_y_in.at[step - 1], oy_send.at[step - 1], oy_recv.at[step - 1],
            (other_y(step) * 2 + c, sq),
        )

    def pass_two(i, slot):
        p = pair_of(i, slot)
        lanes = pl.ds(pl.multiple_of(p * B, B), B)
        k2 = stacked(keys[pl.ds(REACH * B, B), lanes])
        v2 = stacked(values[pl.ds(REACH * B, B), lanes])
        for d in range(REACH + 1):
            q, g = query[pl.ds(d * B, B), lanes], gatt[pl.ds(d * B, B), lanes]
            reach = seeing[:, pl.ds(d * B, B)]
            allowed = jnp.concatenate([reach < window_ref[2 * p], reach < window_ref[2 * p + 1]], axis=0)

            def spread(j):
                first = 8 * j + 2 * (2 * (i % 2) + slot)
                a = jnp.broadcast_to(stats[i // 2, d, pl.ds(first, 1), :], (B, B))
                b = jnp.broadcast_to(stats[i // 2, d, pl.ds(first + 1, 1), :], (B, B))
                return jnp.concatenate([a, b], axis=0)

            probs = jnp.exp(jnp.where(allowed, nt(k2, q) - spread(0), -1e30))
            ds = probs * (nt(v2, g) - spread(1))
            probs_s[slot, :, pl.ds(d * B, B)] = probs.astype(BF)
            ds_s[slot, :, pl.ds(d * B, B)] = ds.astype(BF)
        grad_value = picked(nn(probs_s[slot], gatt[:, lanes])).astype(BF)
        grad_key = unrope(picked(nn(ds_s[slot], query[:, lanes])), own_cos, own_sin).astype(BF)
        gv[:, lanes] = grad_value
        gk[:, lanes] = grad_key

        kv_out[p, 0] = grad_key
        kv_out[p, 1] = grad_value

    def send_kv(p):
        @pl.when(p != dp)
        def _():
            kv_copy(p).start()

        @pl.when(p == dp)
        def _():
            kv_in[dp] = kv_out[p]

    def pass_two_pairs(i, carry):
        @pl.when(i == 2)
        def _():
            for d in range(1, REACH + 1):
                stat_copy(1, d).wait_recv()

        for slot in range(2):
            pass_two(i, slot)
        for slot in range(2):
            send_kv(pair_of(i, slot))
        return carry

    lax.fori_loop(0, PAIRS // 2, pass_two_pairs, 0)

    for step in range(1, 4):
        ox(step).wait_recv()
    for row in range(3):
        total = out_x[x, row].astype(F32)
        for step in range(3):
            total += out_x_in[step, row].astype(F32)
        out_y[row] = total.astype(BF)
    for step in range(1, 4):
        @pl.when(other_y(step) < 3)
        def _():
            oy(step).start()

    grad_normed = nt(gq[...], wq[...]) + nt(gk[...], wk[...]) + nt(gv[...], wv[...])
    own = emb[...]
    inv = lax.rsqrt(jnp.mean(own * own, axis=1, keepdims=True) + EPSILON)
    scaled = own * inv
    gin_ref[...] = (
        inv * (grad_normed - scaled * jnp.mean(grad_normed * scaled, axis=1, keepdims=True))
    ).astype(BF)

    @pl.when(dp < PAIRS)
    def _():
        for i in range(8):
            @pl.when(i != dp)
            def _():
                remote(kv_out.at[0], kv_in.at[i], kv_send.at[0], kv_recv.at[i], (mine, sq)).wait_recv()
        hot_all = hot_of_all()
        tok_sum[1] = nn(hot_all, kv_in[:, 0].reshape(8 * B, B)).astype(BF)
        for step in range(1, 4):
            @pl.when(other_x(step) == 1)
            def _():
                tok(step, 1).start()

        tok_sum[2] = nn(hot_all, kv_in[:, 1].reshape(8 * B, B)).astype(BF)
        for step in range(1, 4):
            @pl.when(other_x(step) == 2)
            def _():
                tok(step, 2).start()

        for step in range(1, 4):
            oy(step).wait_recv()
        total = out_y[lax.min(y, 2)].astype(F32)
        for step in range(3):
            total += out_y_in[step].astype(F32)
        out_z[...] = total.astype(BF).reshape(2, D // 8, B)
        for i in range(2):
            @pl.when(oz_step(i) != 0)
            def _():
                oz(i).start()

        @pl.when(x < 3)
        def _():
            for step in range(1, 4):
                tok(step, lax.min(x, 2)).wait_recv()
            total = tok_sum[lax.min(x, 2)].astype(F32)
            for step in range(3):
                total += tok_in[step].astype(F32)
            z_out[...] = nn(ntab_t[...], total.astype(BF)).astype(BF).reshape(8, D // 8, B)
            for half in range(2):
                for step in (4, 3, 5, 2, 6, 1, 7):
                    zs(step, half).start()

        @pl.when(z // 2 == x)
        def _():
            for step in range(1, 8):
                oz_in(step).wait_recv()
            total = out_z[z % 2].astype(F32)
            for step in range(7):
                total += out_z_in[step].astype(F32)
            out_final[...] = total.astype(BF)

            @pl.when(x < 3)
            def _():
                out_fin().start()

            @pl.when(x == 3)
            def _():
                final[mine] = out_final[...]

        @pl.when(x < 3)
        def _():
            for half in range(2):
                rows = pl.ds(half * part_rows, part_rows)
                for step in range(1, 8):
                    zs(step, half).wait_recv()
                total = z_out[z, rows].astype(F32)
                for step in range(7):
                    total += z_in[step, rows].astype(F32)
                final[mine, rows] = total.astype(BF)
                for step in (4, 3, 5, 2, 6, 1, 7):
                    fin(step, half).start()

        @pl.when(x == 3)
        def _():
            @pl.when(z < 6)
            def _():
                out_fin().wait_recv()

            for half in range(2):
                for step in (4, 3, 5, 2, 6, 1, 7):
                    fin(step, half).start()

    for p in range(PAIRS):
        @pl.when(dp != p)
        def _():
            for half in range(2):
                fin_in(p, half).wait_recv()

    relays = [relay(step, half) for step in range(REACH) for half in range(2)]
    stat_copies = [stat_copy(part, d) for part in range(2) for d in range(1, REACH + 1)]
    for copy in id_copies + idp_copies + relays + stat_copies + [oc(block) for block in range(4)] + [ox(step) for step in range(1, 4)]:
        copy.wait_send()
    for p in range(PAIRS):
        @pl.when(p != dp)
        def _():
            q_copy(p).wait_send()
            kv_copy(p).wait_send()
    for step in range(1, 4):
        @pl.when(other_y(step) < 3)
        def _():
            oy(step).wait_send()

    @pl.when(dp < PAIRS)
    def _():
        for step in range(1, 4):
            @pl.when(other_x(step) < 3)
            def _():
                tok(step, lax.min(other_x(step), 2)).wait_send()
        for i in range(2):
            @pl.when(oz_step(i) != 0)
            def _():
                oz(i).wait_send()

        @pl.when(x < 3)
        def _():
            for half in range(2):
                for step in range(1, 8):
                    zs(step, half).wait_send()

        @pl.when((z // 2 == x) & (x < 3))
        def _():
            out_fin().wait_send()

        for half in range(2):
            for step in range(1, 8):
                fin(step, half).wait_send()


def finish(gin_ref, pieces_ref, gin_out, wg_out):
    gin_out[...] = gin_ref[...]
    for p in range(PAIRS):
        wg_out[:, pl.ds(p * B, B)] = pieces_ref[p].astype(F32)


def on_device(token_ids, cotangent, table, w_query, w_key, w_value, w_out, window):
    tables = [jnp.asarray(part) for part in rope_tables()]
    vmem = pl.BlockSpec(memory_space=pltpu.VMEM)
    hbm = pl.BlockSpec(memory_space=pl.ANY)
    smem = pl.BlockSpec(memory_space=pltpu.SMEM)
    dma = pltpu.SemaphoreType.DMA
    grad_input, pieces = pl.pallas_call(
        kernel,
        out_shape=(
            jax.ShapeDtypeStruct((B, D), BF),
            jax.ShapeDtypeStruct((PAIRS, D // 8, B), BF),
        ),
        in_specs=[vmem] + [hbm] * 6 + [smem] + [vmem] * 4,
        out_specs=(vmem, vmem),
        scratch_shapes=[
            pltpu.VMEM((2 * REACH + 1, 1, B), jnp.int32),
            pltpu.VMEM((8, 1, B), jnp.int32),
            pltpu.VMEM((REACH + 1, B, D), BF),
            pltpu.VMEM((VOCAB, D), BF),
            pltpu.VMEM((D, D), BF),
            pltpu.VMEM((D, D), BF),
            pltpu.VMEM((D, D), BF),
            pltpu.VMEM((D, D), BF),
            pltpu.VMEM((D, VOCAB), BF),
            pltpu.VMEM((VOCAB, D), BF),
            pltpu.VMEM((VOCAB, D), BF),
            pltpu.VMEM((VOCAB, D), BF),
            pltpu.VMEM((VOCAB, D), BF),
            pltpu.VMEM(((2 * REACH + 1) * B, VOCAB), BF),
            pltpu.VMEM((B, D), F32),
            pltpu.VMEM(((2 * REACH + 1) * B, B), F32),
            pltpu.VMEM(((2 * REACH + 1) * B, B), F32),
            pltpu.VMEM((B, SPAN), jnp.int32),
            pltpu.VMEM((B, SPAN), jnp.int32),
            pltpu.VMEM((SPAN, D), BF),
            pltpu.VMEM((SPAN, D), BF),
            pltpu.VMEM((SPAN, D), BF),
            pltpu.VMEM((SPAN, D), BF),
            pltpu.VMEM((B, D), BF),
            pltpu.VMEM((B, D), BF),
            pltpu.VMEM((B, D), BF),
            pltpu.VMEM((B, D), BF),
            pltpu.VMEM((B, B), F32),
            pltpu.VMEM((2, REACH + 1, 16, B), F32),
            pltpu.VMEM((2, 2 * B, SPAN), BF),
            pltpu.VMEM((2, 2 * B, SPAN), BF),
            pltpu.VMEM((8, VOCAB, B), BF),
            pltpu.VMEM((PAIRS, B, B), BF),
            pltpu.VMEM((PAIRS, 2, B, B), BF),
            pltpu.VMEM((8, B, B), BF),
            pltpu.VMEM((8, 2, B, B), BF),
            pltpu.VMEM((3, VOCAB, B), BF),
            pltpu.VMEM((3, VOCAB, B), BF),
            pltpu.VMEM((8, D // 8, B), BF),
            pltpu.VMEM((7, D // 8, B), BF),
            pltpu.VMEM((2, 4, 3, D // 4, B), BF),
            pltpu.VMEM((4, 3, D // 4, B), BF),
            pltpu.VMEM((4, 3, D // 4, B), BF),
            pltpu.VMEM((3, 3, D // 4, B), BF),
            pltpu.VMEM((3, D // 4, B), BF),
            pltpu.VMEM((3, D // 4, B), BF),
            pltpu.VMEM((2, D // 8, B), BF),
            pltpu.VMEM((7, D // 8, B), BF),
            pltpu.VMEM((D // 8, B), BF),
            dma((6,)), dma((8,)), dma((8,)), dma((7,)), dma((7,)), dma((8,)), dma((8,)), dma((8,)), dma((8,)),
            dma((PAIRS,)), dma((8,)), dma((PAIRS,)), dma((8,)), dma((3,)), dma((3,)), dma((14,)), dma((14,)),
            dma((14,)), dma((2, PAIRS)),
            dma((4,)), dma((4,)), dma((3,)), dma((3,)), dma((3,)), dma((3,)), dma((2,)), dma((7,)), dma((1,)), dma((1,)),
        ],
        compiler_params=pltpu.CompilerParams(collective_id=0, has_side_effects=True),
    )(token_ids, cotangent[0], table, w_query, w_key, w_value, w_out, window, *tables)
    grad_input, weight_grads = pl.pallas_call(
        finish,
        out_shape=(
            jax.ShapeDtypeStruct((B, D), BF),
            jax.ShapeDtypeStruct((D // 8, D), F32),
        ),
        in_specs=[vmem, vmem],
        out_specs=(vmem, vmem),
    )(grad_input, pieces)
    return (grad_input[None], weight_grads)


def solution(mesh):
    return jax.shard_map(
        on_device,
        mesh=mesh,
        in_specs=(P("dp", "seq"), P("dp", "seq", None), P(), P(), P(), P(), P(), P()),
        out_specs=(P("dp", "seq", None), P("seq", None)),
        check_vma=False,
    )
```

```python
import functools

import jax
import jax.numpy as jnp
import numpy as np
from jax import lax
from jax.experimental import pallas as pl
from jax.experimental.pallas import tpu as pltpu
from jax.sharding import PartitionSpec as P

D = 768
HEADS = 12
HEAD_DIM = 64
VOCAB = 256
WINDOW = 512
EPSILON = 1e-05
B = 128
SEQ_DEVS = 32
REACH = WINDOW // B
SPAN = (REACH + 1) * B
PAIRS = D // B
MESH = pl.DeviceIdType.MESH
BF = jnp.bfloat16
F32 = jnp.float32


def rope_tables():
    frequency = 10000.0 ** (-2.0 * np.arange(HEAD_DIM // 2) / HEAD_DIM)
    lane_frequency = np.tile(frequency, 4)[None, :]
    inside = np.arange(B)[:, None] * lane_frequency
    blocks = (np.arange(SEQ_DEVS) * B)[:, None] * lane_frequency
    return [
        np.asarray(part, np.float32)
        for part in (np.cos(inside), np.sin(inside), np.cos(blocks), np.sin(blocks))
    ]


def nn(a, b):
    return lax.dot_general(a, b, (((1,), (0,)), ((), ())), preferred_element_type=F32)


def nt(a, b):
    return lax.dot_general(a, b, (((1,), (1,)), ((), ())), preferred_element_type=F32)


def tn(a, b):
    return lax.dot_general(a, b, (((0,), (0,)), ((), ())), preferred_element_type=F32)


def swap_halves(x):
    lane = lax.broadcasted_iota(jnp.int32, x.shape, 1)
    first = (lane // (HEAD_DIM // 2)) % 2 == 0
    return jnp.where(first, pltpu.roll(x, B - HEAD_DIM // 2, 1), pltpu.roll(x, HEAD_DIM // 2, 1))


def rope(x, cosine, sine):
    return x * cosine + swap_halves(x) * sine


def unrope(x, cosine, sine):
    return x * cosine - swap_halves(x) * sine


def kernel(
    ids_ref, cot_hbm, table_hbm, wq_hbm, wk_hbm, wv_hbm, wo_hbm, window_ref, cr_ref, sr_ref, cb_ref, sb_ref,
    gin_ref, final,
    ids_all, ids_dp, cot_all, table, wq, wk, wv, wo, ntab_t, ntab, qtab, ktab, vtab, hot, emb, cosv, sinv, seen, seeing,
    keys, values, query, gatt, att, gq, gk, gv, statc, stats, probs_s, ds_s, hot_dp,
    q_out, kv_out, q_in, kv_in, tok_sum, tok_in, z_out, z_in,
    out_term, out_core, out_x, out_x_in, out_y, out_y_in, out_z, out_z_in, out_final,
    load_sem, ids_send, ids_recv, idp_send, idp_recv, cot_send, cot_recv, st_send, st_recv,
    q_send, q_recv, kv_send, kv_recv, tok_send, tok_recv, z_send, z_recv, fin_send, fin_recv,
    oc_send, oc_recv, ox_send, ox_recv, oy_send, oy_recv, oz_send, oz_recv, of_send, of_recv,
):
    dp = lax.axis_index("dp")
    sq = lax.axis_index("seq")
    x, z = sq // 8, sq % 8
    y, c = dp // 2, dp % 2
    base = sq * B

    loads = [
        pltpu.make_async_copy(src, dst, load_sem.at[i])
        for i, (src, dst) in enumerate(
            [(table_hbm, table), (cot_hbm, cot_all.at[0]), (wk_hbm, wk), (wv_hbm, wv), (wq_hbm, wq), (wo_hbm, wo)]
        )
    ]
    for load in loads:
        load.start()

    def seq_of(new_x, new_z):
        return new_x * 8 + new_z

    def shift(distance):
        return lax.rem(sq + distance + SEQ_DEVS, SEQ_DEVS)

    def other_dp(step):
        return lax.rem(dp + step, 8)

    def other_y(step):
        return lax.rem(y + step, 4)

    def other_x(step):
        return lax.rem(x + step, 4)

    def other_z(step):
        return lax.rem(z + step, 8)

    barrier = pltpu.get_barrier_semaphore()
    partners = [(dp, shift(d)) for d in (1, 2, 3, 4, -1, -2, -3, -4)]
    partners += [(other_dp(d), sq) for d in range(1, 8)]
    partners += [(dp, seq_of(other_x(d), z)) for d in range(1, 4)]
    partners += [(dp, seq_of(x, other_z(d))) for d in range(1, 8)]
    for partner in partners:
        pl.semaphore_signal(barrier, inc=1, device_id=partner, device_id_type=MESH)

    pl.semaphore_wait(barrier, len(partners))

    def remote(src, dst, send, recv, device):
        return pltpu.make_async_remote_copy(
            src_ref=src, dst_ref=dst, send_sem=send, recv_sem=recv, device_id=device, device_id_type=MESH
        )

    id_copies = []
    for i, d in enumerate((4, -4, 3, -3, 2, -2, 1, -1)):
        id_copies.append(remote(ids_ref, ids_all.at[d + REACH], ids_send.at[i], ids_recv.at[i], (dp, shift(-d))))
    idp_copies = []
    for d in range(1, 8):
        idp_copies.append(
            remote(ids_ref, ids_dp.at[8 - d], idp_send.at[d - 1], idp_recv.at[d - 1], (other_dp(d), sq))
        )

    def relay(step, half):
        rows = pl.ds(half * (B // 2), B // 2)
        source = cot_hbm.at[rows] if step == 0 else cot_all.at[step, rows]
        return remote(
            source, cot_all.at[step + 1, rows], cot_send.at[2 * step + half], cot_recv.at[2 * step + half],
            (dp, shift(-1)),
        )

    def forward(step, half):
        relay(step - 1, half).wait_recv()
        relay(step, half).start()

    for copy in id_copies:
        copy.start()
    relay(0, 0).start()
    relay(0, 1).start()
    for copy in idp_copies:
        copy.start()
    ids_all[REACH] = ids_ref[...]
    ids_dp[0] = ids_ref[...]

    lane_row = lax.broadcasted_iota(jnp.int32, (1, B), 1)
    sign = jnp.where((lane_row // (HEAD_DIM // 2)) % 2 == 0, -1.0, 1.0)

    def rope_block(i, carry):
        block = lax.rem(sq + i - REACH + SEQ_DEVS, SEQ_DEVS)
        cb = cb_ref[pl.ds(block, 1), :]
        sb = sb_ref[pl.ds(block, 1), :]
        rows = pl.ds(pl.multiple_of(i * B, B), B)
        cosv[rows, :] = cr_ref[...] * cb - sr_ref[...] * sb
        sinv[rows, :] = (sr_ref[...] * cb + cr_ref[...] * sb) * sign
        return carry

    lax.fori_loop(0, 2 * REACH + 1, rope_block, 0)

    loads[0].wait()
    rows_f = table[...].astype(F32)
    table_inv = lax.rsqrt(jnp.mean(rows_f * rows_f, axis=1, keepdims=True) + EPSILON)
    ntab[...] = (rows_f * table_inv).astype(BF)

    def project_table(w, out):
        def slab(j, carry):
            lanes = pl.ds(pl.multiple_of(j * 2 * B, B), 2 * B)
            out[:, lanes] = nn(ntab[...], w[:, lanes]).astype(BF)
            return carry

        lax.fori_loop(0, PAIRS // 2, slab, 0)

    loads[2].wait()
    project_table(wk, ktab)
    loads[3].wait()
    project_table(wv, vtab)
    forward(1, 0)
    loads[4].wait()
    project_table(wq, qtab)
    loads[5].wait()
    loads[1].wait()
    gatt[pl.ds(0, B), :] = nt(cot_all[0], wo[...]).astype(BF)

    far = 1 << 20
    dist = lax.broadcasted_iota(jnp.int32, (B, SPAN), 0) + WINDOW - lax.broadcasted_iota(jnp.int32, (B, SPAN), 1)
    col = lax.broadcasted_iota(jnp.int32, (B, SPAN), 1)
    seen[...] = jnp.where((dist >= 0) & (col >= WINDOW - base), dist, far)
    dist = col - lax.broadcasted_iota(jnp.int32, (B, SPAN), 0)
    seeing[...] = jnp.where((dist >= 0) & (col < SEQ_DEVS * B - base), dist, far)

    for copy in id_copies:
        copy.wait_recv()

    token = lax.broadcasted_iota(jnp.int32, (VOCAB, B), 0)

    def hot_rows(i, carry):
        hot[pl.ds(pl.multiple_of(i * B, B), B), :] = (token == ids_all[i]).astype(F32).T.astype(BF)
        return carry

    lax.fori_loop(0, 2 * REACH + 1, hot_rows, 0)

    def select(tab, out, first, to, count, rotated, scale):
        def slab(j, carry):
            lanes = pl.ds(pl.multiple_of(j * 2 * B, B), 2 * B)
            got = nn(hot[pl.ds(first, count), :], tab[:, lanes])
            for half in range(2):
                part = got[:, half * B : (half + 1) * B]
                if rotated:
                    part = rope(part, cosv[pl.ds(first, count), :], sinv[pl.ds(first, count), :])
                if scale != 1.0:
                    part = part * scale
                out[pl.ds(to, count), pl.ds(pl.multiple_of((2 * j + half) * B, B), B)] = part.astype(BF)
            return carry

        lax.fori_loop(0, PAIRS // 2, slab, 0)

    forward(1, 1)
    select(ktab, keys, 0, 0, SPAN, True, 1.0)
    select(vtab, values, 0, 0, SPAN, False, 1.0)
    select(qtab, query, REACH * B, 0, B, True, HEAD_DIM ** (-0.5))
    forward(2, 0)

    lane_one = lax.broadcasted_iota(jnp.int32, (1, B), 1)
    left = (lane_one < HEAD_DIM).astype(BF)
    right = (lane_one >= HEAD_DIM).astype(BF)

    def stacked(a):
        return jnp.concatenate([a * left, a * right], axis=0)

    def picked(a):
        return jnp.where(lane_one < HEAD_DIM, a[:B], a[B:])

    own_cos = cosv[pl.ds(REACH * B, B), :]
    own_sin = sinv[pl.ds(REACH * B, B), :]
    statc[...] = jnp.zeros_like(statc)

    def owner_of(p):
        return p + 3 * jnp.where(p == 3, 1, 0)

    owns_tokens = (dp != 3) & (dp != 7)
    owned = jnp.where(dp == 6, 3, lax.min(dp, PAIRS - 1))

    def q_copy(p):
        return remote(q_out.at[p], q_in.at[dp], q_send.at[p], q_recv.at[dp], (owner_of(p), sq))

    def kv_copy(p):
        return remote(kv_out.at[p], kv_in.at[dp], kv_send.at[p], kv_recv.at[dp], (owner_of(p), sq))

    def stat_copy(part, d):
        at = REACH * part + d - 1
        rows = pl.ds(0, 8 if part else 16)
        return remote(
            stats.at[part, 0, rows], stats.at[part, d, rows], st_send.at[at], st_recv.at[at], (dp, shift(-d))
        )

    def pair_of(i, slot):
        return 3 + i if slot else 2 - i

    def pass_one(i, slot):
        p = pair_of(i, slot)
        lanes = pl.ds(pl.multiple_of(p * B, B), B)
        k, v = keys[:, lanes], values[:, lanes]
        scores = nt(stacked(query[pl.ds(0, B), lanes]), k)
        reach = seen[...]
        masked = jnp.concatenate(
            [
                jnp.where(reach < window_ref[2 * p], scores[:B], -1e30),
                jnp.where(reach < window_ref[2 * p + 1], scores[B:], -1e30),
            ],
            axis=0,
        )
        top = jnp.max(masked, axis=1, keepdims=True)
        weights = jnp.exp(masked - top)
        whole = jnp.sum(weights, axis=1, keepdims=True)
        probs = weights * (1.0 / whole)
        grad_probs = nt(stacked(gatt[pl.ds(0, B), lanes]), v)
        row_term = jnp.sum(probs * grad_probs, axis=1, keepdims=True)
        ds = (probs * (grad_probs - row_term)).astype(BF)
        att[:, lanes] = picked(nn(probs.astype(BF), v)).astype(BF)
        grad_query = picked(nn(ds, k)) * HEAD_DIM ** (-0.5)
        got = unrope(grad_query, own_cos, own_sin).astype(BF)
        gq[:, lanes] = got

        q_out[p] = got
        held = statc[...]
        for j, stat in enumerate((top + jnp.log(whole), row_term)):
            first = 16 * (i // 2) + (8 - 4 * (i // 2)) * j + 2 * (2 * (i % 2) + slot)
            held = jnp.where(lane_one == first, stat[:B], held)
            held = jnp.where(lane_one == first + 1, stat[B:], held)
        statc[...] = held


    def send_q(p):
        @pl.when(owner_of(p) != dp)
        def _():
            q_copy(p).start()

        @pl.when(owner_of(p) == dp)
        def _():
            q_in[dp] = q_out[p]

    def out_terms(first, count, blocks):
        att_t = att[:, pl.ds(first, count)].T

        def one_pair(p, carry):
            lanes = pl.ds(pl.multiple_of(p * B, B), B)
            got = nn(att_t, cot_all[0, :, lanes]).astype(BF)
            for block in blocks:
                start = block * (D // 4) - first
                out_term[p % 2, block, p // 2] = got[start : start + D // 4]
            return carry

        lax.fori_loop(0, PAIRS, one_pair, 0)
        for block in blocks:
            oc(block).start()

    def oc(block):
        return remote(
            out_term.at[1 - c, block], out_core.at[block], oc_send.at[block], oc_recv.at[block],
            (y * 2 + 1 - c, sq),
        )

    def ox(step):
        return remote(
            out_x.at[other_x(step)], out_x_in.at[step - 1], ox_send.at[step - 1], ox_recv.at[step - 1],
            (dp, seq_of(other_x(step), z)),
        )

    def out_core_sum(blocks):
        for block in blocks:
            oc(block).wait_recv()
            out_x[block] = (out_term[c, block].astype(F32) + out_core[block].astype(F32)).astype(BF)
        for step in range(1, 4):
            for block in blocks:
                @pl.when(other_x(step) == block)
                def _():
                    ox(step).start()

    def pass_one_pairs(i, carry):
        for slot in range(2):
            pass_one(i, slot)
        for slot in range(2):
            send_q(pair_of(i, slot))

        @pl.when(i == 0)
        def _():
            forward(2, 1)

        @pl.when(i == 1)
        def _():
            stats[0, 0] = statc[...].T[:16]
            for d in range(REACH, 0, -1):
                stat_copy(0, d).start()
            forward(3, 0)
            out_terms(B, 4 * B, (1, 2))

        return carry

    lax.fori_loop(0, PAIRS // 2, pass_one_pairs, 0)

    forward(3, 1)
    stats[1, 0, pl.ds(0, 8)] = statc[...].T[16:24]
    for d in range(REACH, 0, -1):
        stat_copy(1, d).start()
    out_terms(0, D, (0, 3))
    out_core_sum((1, 2))

    ntab_t[...] = ntab[...].T
    emb[...] = nn(hot[pl.ds(REACH * B, B), :], table[...])
    select(qtab, query, (REACH + 1) * B, B, REACH * B, True, HEAD_DIM ** (-0.5))

    for d in range(1, 4):
        gatt[pl.ds(d * B, B), :] = nt(cot_all[d], wo[...]).astype(BF)

    def tok(step, target):
        return remote(
            tok_sum.at[target], tok_in.at[step - 1], tok_send.at[step - 1], tok_recv.at[step - 1],
            (dp, seq_of(target, z)),
        )

    def oz_step(i):
        return lax.rem(2 * x + i - z + 8, 8)

    def oz(i):
        step = lax.max(oz_step(i), 1)
        return remote(
            out_z.at[i], out_z_in.at[step - 1], oz_send.at[i], oz_recv.at[step - 1], (dp, seq_of(x, 2 * x + i))
        )

    def oz_in(step):
        return remote(
            out_z.at[0], out_z_in.at[step - 1], oz_send.at[0], oz_recv.at[step - 1], (dp, seq_of(x, z))
        )

    part_rows = D // 16

    def zs(step, half):
        rows = pl.ds(half * part_rows, part_rows)
        at = 7 * half + step - 1
        return remote(
            z_out.at[other_z(step), rows], z_in.at[step - 1, rows], z_send.at[at], z_recv.at[at],
            (dp, seq_of(x, other_z(step))),
        )

    mine = lax.min(dp, PAIRS - 1)
    slot_here = jnp.where(x == 3, mine, owned)

    def fin(step, half):
        part = final.at[slot_here, pl.ds(half * part_rows, part_rows)]
        return remote(
            part, part, fin_send.at[7 * half + step - 1], fin_recv.at[half, slot_here], (other_dp(step), sq)
        )

    def out_fin():
        return remote(out_final, final.at[mine], of_send.at[0], of_recv.at[0], (dp, seq_of(3, z)))

    def fin_in(p, half):
        part = final.at[p, pl.ds(half * part_rows, part_rows)]
        return remote(part, part, fin_send.at[0], fin_recv.at[half, p], (p, sq))

    out_core_sum((0, 3))

    for copy in idp_copies:
        copy.wait_recv()

    def hot_of_all():
        return jnp.concatenate([hot_dp[i] for i in range(8)], axis=1)

    @pl.when(owns_tokens)
    def _():
        def hot_block(i, carry):
            owner = lax.rem(dp + i, 8)
            hot_dp[owner] = (token == ids_dp[i]).astype(BF)
            return carry

        lax.fori_loop(0, 8, hot_block, 0)

        for i in range(8):
            @pl.when(i != dp)
            def _():
                remote(q_out.at[0], q_in.at[i], q_send.at[0], q_recv.at[i], (mine, sq)).wait_recv()

        tok_sum[0] = nn(hot_of_all(), q_in[...].reshape(8 * B, B)).astype(BF)
        for step in range(1, 4):
            @pl.when(other_x(step) == 0)
            def _():
                tok(step, 0).start()

    for half in range(2):
        relay(3, half).wait_recv()
    gatt[pl.ds(REACH * B, B), :] = nt(cot_all[REACH], wo[...]).astype(BF)
    for d in range(1, REACH + 1):
        stat_copy(0, d).wait_recv()

    def oy(step):
        return remote(
            out_y.at[lax.min(other_y(step), 2)], out_y_in.at[step - 1], oy_send.at[step - 1], oy_recv.at[step - 1],
            (other_y(step) * 2 + c, sq),
        )

    def pass_two(i, slot):
        p = pair_of(i, slot)
        lanes = pl.ds(pl.multiple_of(p * B, B), B)
        k2 = stacked(keys[pl.ds(REACH * B, B), lanes])
        v2 = stacked(values[pl.ds(REACH * B, B), lanes])
        for d in range(REACH + 1):
            q, g = query[pl.ds(d * B, B), lanes], gatt[pl.ds(d * B, B), lanes]
            reach = seeing[:, pl.ds(d * B, B)]
            allowed = jnp.concatenate([reach < window_ref[2 * p], reach < window_ref[2 * p + 1]], axis=0)

            def spread(j):
                first = (8 - 4 * (i // 2)) * j + 2 * (2 * (i % 2) + slot)
                a = jnp.broadcast_to(stats[i // 2, d, pl.ds(first, 1), :], (B, B))
                b = jnp.broadcast_to(stats[i // 2, d, pl.ds(first + 1, 1), :], (B, B))
                return jnp.concatenate([a, b], axis=0)

            probs = jnp.exp(jnp.where(allowed, nt(k2, q) - spread(0), -1e30))
            ds = probs * (nt(v2, g) - spread(1))
            probs_s[slot, :, pl.ds(d * B, B)] = probs.astype(BF)
            ds_s[slot, :, pl.ds(d * B, B)] = ds.astype(BF)
        grad_value = picked(nn(probs_s[slot], gatt[:, lanes])).astype(BF)
        grad_key = unrope(picked(nn(ds_s[slot], query[:, lanes])), own_cos, own_sin).astype(BF)
        gv[:, lanes] = grad_value
        gk[:, lanes] = grad_key

        kv_out[p, 0] = grad_key
        kv_out[p, 1] = grad_value

    def send_kv(p):
        @pl.when(owner_of(p) != dp)
        def _():
            kv_copy(p).start()

        @pl.when(owner_of(p) == dp)
        def _():
            kv_in[dp] = kv_out[p]

    def pass_two_pairs(i, carry):
        @pl.when(i == 2)
        def _():
            for d in range(1, REACH + 1):
                stat_copy(1, d).wait_recv()

        for slot in range(2):
            pass_two(i, slot)
        for slot in range(2):
            send_kv(pair_of(i, slot))
        return carry

    lax.fori_loop(0, PAIRS // 2, pass_two_pairs, 0)

    for step in range(1, 4):
        ox(step).wait_recv()
    for row in range(3):
        total = out_x[x, row].astype(F32)
        for step in range(3):
            total += out_x_in[step, row].astype(F32)
        out_y[row] = total.astype(BF)
    for step in range(1, 4):
        @pl.when(other_y(step) < 3)
        def _():
            oy(step).start()

    grad_normed = nt(gq[...], wq[...]) + nt(gk[...], wk[...]) + nt(gv[...], wv[...])
    own = emb[...]
    inv = lax.rsqrt(jnp.mean(own * own, axis=1, keepdims=True) + EPSILON)
    scaled = own * inv
    gin_ref[...] = (
        inv * (grad_normed - scaled * jnp.mean(grad_normed * scaled, axis=1, keepdims=True))
    ).astype(BF)

    @pl.when(owns_tokens)
    def _():
        for i in range(8):
            @pl.when(i != dp)
            def _():
                remote(kv_out.at[0], kv_in.at[i], kv_send.at[0], kv_recv.at[i], (mine, sq)).wait_recv()
        hot_all = hot_of_all()
        tok_sum[1] = nn(hot_all, kv_in[:, 0].reshape(8 * B, B)).astype(BF)
        for step in range(1, 4):
            @pl.when(other_x(step) == 1)
            def _():
                tok(step, 1).start()

        tok_sum[2] = nn(hot_all, kv_in[:, 1].reshape(8 * B, B)).astype(BF)
        for step in range(1, 4):
            @pl.when(other_x(step) == 2)
            def _():
                tok(step, 2).start()

    @pl.when(dp < PAIRS)
    def _():
        for step in range(1, 4):
            oy(step).wait_recv()
        total = out_y[lax.min(y, 2)].astype(F32)
        for step in range(3):
            total += out_y_in[step].astype(F32)
        out_z[...] = total.astype(BF).reshape(2, D // 8, B)
        for i in range(2):
            @pl.when(oz_step(i) != 0)
            def _():
                oz(i).start()

    @pl.when(owns_tokens)
    def _():
        @pl.when(x < 3)
        def _():
            for step in range(1, 4):
                tok(step, lax.min(x, 2)).wait_recv()
            total = tok_sum[lax.min(x, 2)].astype(F32)
            for step in range(3):
                total += tok_in[step].astype(F32)
            z_out[...] = nn(ntab_t[...], total.astype(BF)).astype(BF).reshape(8, D // 8, B)
            for half in range(2):
                for step in (4, 3, 5, 2, 6, 1, 7):
                    zs(step, half).start()

    @pl.when(dp < PAIRS)
    def _():
        @pl.when(z // 2 == x)
        def _():
            for step in range(1, 8):
                oz_in(step).wait_recv()
            total = out_z[z % 2].astype(F32)
            for step in range(7):
                total += out_z_in[step].astype(F32)
            out_final[...] = total.astype(BF)

            @pl.when(x < 3)
            def _():
                out_fin().start()

            @pl.when(x == 3)
            def _():
                final[mine] = out_final[...]

    @pl.when(owns_tokens)
    def _():
        @pl.when(x < 3)
        def _():
            for half in range(2):
                rows = pl.ds(half * part_rows, part_rows)
                for step in range(1, 8):
                    zs(step, half).wait_recv()
                total = z_out[z, rows].astype(F32)
                for step in range(7):
                    total += z_in[step, rows].astype(F32)
                final[owned, rows] = total.astype(BF)
                for step in (4, 3, 5, 2, 6, 1, 7):
                    fin(step, half).start()

    @pl.when(dp < PAIRS)
    def _():
        @pl.when(x == 3)
        def _():
            @pl.when(z < 6)
            def _():
                out_fin().wait_recv()

            for half in range(2):
                for step in (4, 3, 5, 2, 6, 1, 7):
                    fin(step, half).start()

    for p in range(PAIRS):
        @pl.when(dp != (p if p != 3 else jnp.where(x == 3, 3, 6)))
        def _():
            for half in range(2):
                fin_in(p, half).wait_recv()

    relays = [relay(step, half) for step in range(REACH) for half in range(2)]
    stat_copies = [stat_copy(part, d) for part in range(2) for d in range(1, REACH + 1)]
    for copy in id_copies + idp_copies + relays + stat_copies + [oc(block) for block in range(4)] + [ox(step) for step in range(1, 4)]:
        copy.wait_send()
    for p in range(PAIRS):
        @pl.when(owner_of(p) != dp)
        def _():
            q_copy(p).wait_send()
            kv_copy(p).wait_send()
    for step in range(1, 4):
        @pl.when(other_y(step) < 3)
        def _():
            oy(step).wait_send()

    @pl.when(owns_tokens)
    def _():
        for step in range(1, 4):
            @pl.when(other_x(step) < 3)
            def _():
                tok(step, lax.min(other_x(step), 2)).wait_send()

        @pl.when(x < 3)
        def _():
            for half in range(2):
                for step in range(1, 8):
                    zs(step, half).wait_send()
                    fin(step, half).wait_send()

    @pl.when(dp < PAIRS)
    def _():
        for i in range(2):
            @pl.when(oz_step(i) != 0)
            def _():
                oz(i).wait_send()

        @pl.when((z // 2 == x) & (x < 3))
        def _():
            out_fin().wait_send()

        @pl.when(x == 3)
        def _():
            for half in range(2):
                for step in range(1, 8):
                    fin(step, half).wait_send()


def finish(gin_ref, pieces_ref, gin_out, wg_out):
    gin_out[...] = gin_ref[...]
    for p in range(PAIRS):
        wg_out[:, pl.ds(p * B, B)] = pieces_ref[p].astype(F32)


def on_device(token_ids, cotangent, table, w_query, w_key, w_value, w_out, window):
    tables = [jnp.asarray(part) for part in rope_tables()]
    vmem = pl.BlockSpec(memory_space=pltpu.VMEM)
    hbm = pl.BlockSpec(memory_space=pl.ANY)
    smem = pl.BlockSpec(memory_space=pltpu.SMEM)
    dma = pltpu.SemaphoreType.DMA
    grad_input, pieces = pl.pallas_call(
        kernel,
        out_shape=(
            jax.ShapeDtypeStruct((B, D), BF),
            jax.ShapeDtypeStruct((PAIRS, D // 8, B), BF),
        ),
        in_specs=[vmem] + [hbm] * 6 + [smem] + [vmem] * 4,
        out_specs=(vmem, vmem),
        scratch_shapes=[
            pltpu.VMEM((2 * REACH + 1, 1, B), jnp.int32),
            pltpu.VMEM((8, 1, B), jnp.int32),
            pltpu.VMEM((REACH + 1, B, D), BF),
            pltpu.VMEM((VOCAB, D), BF),
            pltpu.VMEM((D, D), BF),
            pltpu.VMEM((D, D), BF),
            pltpu.VMEM((D, D), BF),
            pltpu.VMEM((D, D), BF),
            pltpu.VMEM((D, VOCAB), BF),
            pltpu.VMEM((VOCAB, D), BF),
            pltpu.VMEM((VOCAB, D), BF),
            pltpu.VMEM((VOCAB, D), BF),
            pltpu.VMEM((VOCAB, D), BF),
            pltpu.VMEM(((2 * REACH + 1) * B, VOCAB), BF),
            pltpu.VMEM((B, D), F32),
            pltpu.VMEM(((2 * REACH + 1) * B, B), F32),
            pltpu.VMEM(((2 * REACH + 1) * B, B), F32),
            pltpu.VMEM((B, SPAN), jnp.int32),
            pltpu.VMEM((B, SPAN), jnp.int32),
            pltpu.VMEM((SPAN, D), BF),
            pltpu.VMEM((SPAN, D), BF),
            pltpu.VMEM((SPAN, D), BF),
            pltpu.VMEM((SPAN, D), BF),
            pltpu.VMEM((B, D), BF),
            pltpu.VMEM((B, D), BF),
            pltpu.VMEM((B, D), BF),
            pltpu.VMEM((B, D), BF),
            pltpu.VMEM((B, B), F32),
            pltpu.VMEM((2, REACH + 1, 16, B), F32),
            pltpu.VMEM((2, 2 * B, SPAN), BF),
            pltpu.VMEM((2, 2 * B, SPAN), BF),
            pltpu.VMEM((8, VOCAB, B), BF),
            pltpu.VMEM((PAIRS, B, B), BF),
            pltpu.VMEM((PAIRS, 2, B, B), BF),
            pltpu.VMEM((8, B, B), BF),
            pltpu.VMEM((8, 2, B, B), BF),
            pltpu.VMEM((3, VOCAB, B), BF),
            pltpu.VMEM((3, VOCAB, B), BF),
            pltpu.VMEM((8, D // 8, B), BF),
            pltpu.VMEM((7, D // 8, B), BF),
            pltpu.VMEM((2, 4, 3, D // 4, B), BF),
            pltpu.VMEM((4, 3, D // 4, B), BF),
            pltpu.VMEM((4, 3, D // 4, B), BF),
            pltpu.VMEM((3, 3, D // 4, B), BF),
            pltpu.VMEM((3, D // 4, B), BF),
            pltpu.VMEM((3, D // 4, B), BF),
            pltpu.VMEM((2, D // 8, B), BF),
            pltpu.VMEM((7, D // 8, B), BF),
            pltpu.VMEM((D // 8, B), BF),
            dma((6,)), dma((8,)), dma((8,)), dma((7,)), dma((7,)), dma((8,)), dma((8,)), dma((8,)), dma((8,)),
            dma((PAIRS,)), dma((8,)), dma((PAIRS,)), dma((8,)), dma((3,)), dma((3,)), dma((14,)), dma((14,)),
            dma((14,)), dma((2, PAIRS)),
            dma((4,)), dma((4,)), dma((3,)), dma((3,)), dma((3,)), dma((3,)), dma((2,)), dma((7,)), dma((1,)), dma((1,)),
        ],
        compiler_params=pltpu.CompilerParams(collective_id=0, has_side_effects=True),
    )(token_ids, cotangent[0], table, w_query, w_key, w_value, w_out, window, *tables)
    grad_input, weight_grads = pl.pallas_call(
        finish,
        out_shape=(
            jax.ShapeDtypeStruct((B, D), BF),
            jax.ShapeDtypeStruct((D // 8, D), F32),
        ),
        in_specs=[vmem, vmem],
        out_specs=(vmem, vmem),
    )(grad_input, pieces)
    return (grad_input[None], weight_grads)


def solution(mesh):
    return jax.shard_map(
        on_device,
        mesh=mesh,
        in_specs=(P("dp", "seq"), P("dp", "seq", None), P(), P(), P(), P(), P(), P()),
        out_specs=(P("dp", "seq", None), P("seq", None)),
        check_vma=False,
    )
```

```python
import functools

import jax
import jax.numpy as jnp
import numpy as np
from jax import lax
from jax.experimental import pallas as pl
from jax.experimental.pallas import tpu as pltpu
from jax.sharding import PartitionSpec as P

D = 768
HEADS = 12
HEAD_DIM = 64
VOCAB = 256
WINDOW = 512
EPSILON = 1e-05
B = 128
SEQ_DEVS = 32
REACH = WINDOW // B
SPAN = (REACH + 1) * B
PAIRS = D // B
MESH = pl.DeviceIdType.MESH
BF = jnp.bfloat16
F32 = jnp.float32


def rope_tables():
    frequency = 10000.0 ** (-2.0 * np.arange(HEAD_DIM // 2) / HEAD_DIM)
    lane_frequency = np.tile(frequency, 4)[None, :]
    inside = np.arange(B)[:, None] * lane_frequency
    blocks = (np.arange(SEQ_DEVS) * B)[:, None] * lane_frequency
    return [
        np.asarray(part, np.float32)
        for part in (np.cos(inside), np.sin(inside), np.cos(blocks), np.sin(blocks))
    ]


def nn(a, b):
    return lax.dot_general(a, b, (((1,), (0,)), ((), ())), preferred_element_type=F32)


def nt(a, b):
    return lax.dot_general(a, b, (((1,), (1,)), ((), ())), preferred_element_type=F32)


def tn(a, b):
    return lax.dot_general(a, b, (((0,), (0,)), ((), ())), preferred_element_type=F32)


def swap_halves(x):
    lane = lax.broadcasted_iota(jnp.int32, x.shape, 1)
    first = (lane // (HEAD_DIM // 2)) % 2 == 0
    return jnp.where(first, pltpu.roll(x, B - HEAD_DIM // 2, 1), pltpu.roll(x, HEAD_DIM // 2, 1))


def rope(x, cosine, sine):
    return x * cosine + swap_halves(x) * sine


def unrope(x, cosine, sine):
    return x * cosine - swap_halves(x) * sine


def kernel(
    ids_ref, cot_hbm, table_hbm, wq_hbm, wk_hbm, wv_hbm, wo_hbm, window_ref, cr_ref, sr_ref, cb_ref, sb_ref,
    gin_ref, final,
    ids_all, ids_dp, cot_all, table, wq, wk, wv, wo, ntab_t, ntab, qtab, ktab, vtab, hot, emb, cosv, sinv, seen, seeing,
    keys, values, query, gatt, att, gq, gk, gv, statc, stats, probs_s, ds_s, hot_dp,
    q_out, kv_out, q_in, kv_in, tok_sum, tok_in, z_out, z_in,
    out_term, out_core, out_x, out_x_in, out_y, out_y_in, out_z, out_z_in, out_final,
    load_sem, ids_send, ids_recv, idp_send, idp_recv, cot_send, cot_recv, st_send, st_recv,
    q_send, q_recv, kv_send, kv_recv, tok_send, tok_recv, z_send, z_recv, fin_send, fin_recv,
    oc_send, oc_recv, ox_send, ox_recv, oy_send, oy_recv, oz_send, oz_recv, of_send, of_recv,
):
    dp = lax.axis_index("dp")
    sq = lax.axis_index("seq")
    x, z = sq // 8, sq % 8
    y, c = dp // 2, dp % 2
    base = sq * B

    loads = [
        pltpu.make_async_copy(src, dst, load_sem.at[i])
        for i, (src, dst) in enumerate(
            [(table_hbm, table), (cot_hbm, cot_all.at[0]), (wk_hbm, wk), (wv_hbm, wv), (wq_hbm, wq), (wo_hbm, wo)]
        )
    ]
    for load in loads:
        load.start()

    def seq_of(new_x, new_z):
        return new_x * 8 + new_z

    def shift(distance):
        return lax.rem(sq + distance + SEQ_DEVS, SEQ_DEVS)

    def other_dp(step):
        return lax.rem(dp + step, 8)

    def other_y(step):
        return lax.rem(y + step, 4)

    def other_x(step):
        return lax.rem(x + step, 4)

    def other_z(step):
        return lax.rem(z + step, 8)

    barrier = pltpu.get_barrier_semaphore()
    partners = [(dp, shift(d)) for d in (1, 2, 3, 4, -1, -2, -3, -4)]
    partners += [(other_dp(d), sq) for d in range(1, 8)]
    partners += [(dp, seq_of(other_x(d), z)) for d in range(1, 4)]
    partners += [(dp, seq_of(x, other_z(d))) for d in range(1, 8)]
    for partner in partners:
        pl.semaphore_signal(barrier, inc=1, device_id=partner, device_id_type=MESH)

    pl.semaphore_wait(barrier, len(partners))

    def remote(src, dst, send, recv, device):
        return pltpu.make_async_remote_copy(
            src_ref=src, dst_ref=dst, send_sem=send, recv_sem=recv, device_id=device, device_id_type=MESH
        )

    id_copies = []
    for i, d in enumerate((4, -4, 3, -3, 2, -2, 1, -1)):
        id_copies.append(remote(ids_ref, ids_all.at[d + REACH], ids_send.at[i], ids_recv.at[i], (dp, shift(-d))))
    idp_copies = []
    for d in range(1, 8):
        idp_copies.append(
            remote(ids_ref, ids_dp.at[8 - d], idp_send.at[d - 1], idp_recv.at[d - 1], (other_dp(d), sq))
        )

    def relay(step, half):
        rows = pl.ds(half * (B // 2), B // 2)
        source = cot_hbm.at[rows] if step == 0 else cot_all.at[step, rows]
        return remote(
            source, cot_all.at[step + 1, rows], cot_send.at[2 * step + half], cot_recv.at[2 * step + half],
            (dp, shift(-1)),
        )

    def forward(step, half):
        relay(step - 1, half).wait_recv()
        relay(step, half).start()

    for copy in id_copies:
        copy.start()
    relay(0, 0).start()
    relay(0, 1).start()
    for copy in idp_copies:
        copy.start()
    ids_all[REACH] = ids_ref[...]
    ids_dp[0] = ids_ref[...]

    lane_row = lax.broadcasted_iota(jnp.int32, (1, B), 1)
    sign = jnp.where((lane_row // (HEAD_DIM // 2)) % 2 == 0, -1.0, 1.0)

    def rope_block(i, carry):
        block = lax.rem(sq + i - REACH + SEQ_DEVS, SEQ_DEVS)
        cb = cb_ref[pl.ds(block, 1), :]
        sb = sb_ref[pl.ds(block, 1), :]
        rows = pl.ds(pl.multiple_of(i * B, B), B)
        cosv[rows, :] = cr_ref[...] * cb - sr_ref[...] * sb
        sinv[rows, :] = (sr_ref[...] * cb + cr_ref[...] * sb) * sign
        return carry

    lax.fori_loop(0, 2 * REACH + 1, rope_block, 0)

    loads[0].wait()
    rows_f = table[...].astype(F32)
    table_inv = lax.rsqrt(jnp.mean(rows_f * rows_f, axis=1, keepdims=True) + EPSILON)
    ntab[...] = (rows_f * table_inv).astype(BF)

    def project_table(w, out):
        def slab(j, carry):
            lanes = pl.ds(pl.multiple_of(j * 2 * B, B), 2 * B)
            out[:, lanes] = nn(ntab[...], w[:, lanes]).astype(BF)
            return carry

        lax.fori_loop(0, PAIRS // 2, slab, 0)

    loads[2].wait()
    project_table(wk, ktab)
    loads[3].wait()
    project_table(wv, vtab)
    loads[4].wait()
    project_table(wq, qtab)
    loads[5].wait()
    loads[1].wait()
    gatt[pl.ds(0, B), :] = nt(cot_all[0], wo[...]).astype(BF)
    forward(1, 0)

    far = 1 << 20
    dist = lax.broadcasted_iota(jnp.int32, (B, SPAN), 0) + WINDOW - lax.broadcasted_iota(jnp.int32, (B, SPAN), 1)
    col = lax.broadcasted_iota(jnp.int32, (B, SPAN), 1)
    seen[...] = jnp.where((dist >= 0) & (col >= WINDOW - base), dist, far)
    dist = col - lax.broadcasted_iota(jnp.int32, (B, SPAN), 0)
    seeing[...] = jnp.where((dist >= 0) & (col < SEQ_DEVS * B - base), dist, far)

    for copy in id_copies:
        copy.wait_recv()

    token = lax.broadcasted_iota(jnp.int32, (VOCAB, B), 0)

    def hot_rows(i, carry):
        hot[pl.ds(pl.multiple_of(i * B, B), B), :] = (token == ids_all[i]).astype(F32).T.astype(BF)
        return carry

    lax.fori_loop(0, 2 * REACH + 1, hot_rows, 0)

    def select(tab, out, first, to, count, rotated, scale):
        def slab(j, carry):
            lanes = pl.ds(pl.multiple_of(j * 2 * B, B), 2 * B)
            got = nn(hot[pl.ds(first, count), :], tab[:, lanes])
            for half in range(2):
                part = got[:, half * B : (half + 1) * B]
                if rotated:
                    part = rope(part, cosv[pl.ds(first, count), :], sinv[pl.ds(first, count), :])
                if scale != 1.0:
                    part = part * scale
                out[pl.ds(to, count), pl.ds(pl.multiple_of((2 * j + half) * B, B), B)] = part.astype(BF)
            return carry

        lax.fori_loop(0, PAIRS // 2, slab, 0)

    forward(1, 1)
    select(ktab, keys, 0, 0, SPAN, True, 1.0)
    select(vtab, values, 0, 0, SPAN, False, 1.0)
    select(qtab, query, REACH * B, 0, B, True, HEAD_DIM ** (-0.5))
    forward(2, 0)

    lane_one = lax.broadcasted_iota(jnp.int32, (1, B), 1)
    left = (lane_one < HEAD_DIM).astype(BF)
    right = (lane_one >= HEAD_DIM).astype(BF)

    def stacked(a):
        return jnp.concatenate([a * left, a * right], axis=0)

    def picked(a):
        return jnp.where(lane_one < HEAD_DIM, a[:B], a[B:])

    own_cos = cosv[pl.ds(REACH * B, B), :]
    own_sin = sinv[pl.ds(REACH * B, B), :]
    statc[...] = jnp.zeros_like(statc)

    def q_copy(p):
        return remote(q_out.at[p], q_in.at[dp], q_send.at[p], q_recv.at[dp], (p, sq))

    def kv_copy(p):
        return remote(kv_out.at[p], kv_in.at[dp], kv_send.at[p], kv_recv.at[dp], (p, sq))

    def stat_copy(part, d):
        at = REACH * part + d - 1
        return remote(stats.at[part, 0], stats.at[part, d], st_send.at[at], st_recv.at[at], (dp, shift(-d)))

    def pair_of(i, slot):
        return 3 + i if slot else 2 - i

    def pass_one(i, slot):
        p = pair_of(i, slot)
        lanes = pl.ds(pl.multiple_of(p * B, B), B)
        k, v = keys[:, lanes], values[:, lanes]
        scores = nt(stacked(query[pl.ds(0, B), lanes]), k)
        reach = seen[...]
        masked = jnp.concatenate(
            [
                jnp.where(reach < window_ref[2 * p], scores[:B], -1e30),
                jnp.where(reach < window_ref[2 * p + 1], scores[B:], -1e30),
            ],
            axis=0,
        )
        top = jnp.max(masked, axis=1, keepdims=True)
        weights = jnp.exp(masked - top)
        whole = jnp.sum(weights, axis=1, keepdims=True)
        probs = weights * (1.0 / whole)
        grad_probs = nt(stacked(gatt[pl.ds(0, B), lanes]), v)
        row_term = jnp.sum(probs * grad_probs, axis=1, keepdims=True)
        ds = (probs * (grad_probs - row_term)).astype(BF)
        att[:, lanes] = picked(nn(probs.astype(BF), v)).astype(BF)
        grad_query = picked(nn(ds, k)) * HEAD_DIM ** (-0.5)
        got = unrope(grad_query, own_cos, own_sin).astype(BF)
        gq[:, lanes] = got

        q_out[p] = got
        held = statc[...]
        for j, stat in enumerate((top + jnp.log(whole), row_term)):
            first = 16 * (i // 2) + 8 * j + 2 * (2 * (i % 2) + slot)
            held = jnp.where(lane_one == first, stat[:B], held)
            held = jnp.where(lane_one == first + 1, stat[B:], held)
        statc[...] = held


    def send_q(p):
        @pl.when(p != dp)
        def _():
            q_copy(p).start()

        @pl.when(p == dp)
        def _():
            q_in[dp] = q_out[p]

    def out_terms(first, count, blocks):
        att_t = att[:, pl.ds(first, count)].T

        def one_pair(p, carry):
            lanes = pl.ds(pl.multiple_of(p * B, B), B)
            got = nn(att_t, cot_all[0, :, lanes]).astype(BF)
            for block in blocks:
                start = block * (D // 4) - first
                out_term[p % 2, block, p // 2] = got[start : start + D // 4]
            return carry

        lax.fori_loop(0, PAIRS, one_pair, 0)
        for block in blocks:
            oc(block).start()

    def oc(block):
        return remote(
            out_term.at[1 - c, block], out_core.at[block], oc_send.at[block], oc_recv.at[block],
            (y * 2 + 1 - c, sq),
        )

    def ox(step):
        return remote(
            out_x.at[other_x(step)], out_x_in.at[step - 1], ox_send.at[step - 1], ox_recv.at[step - 1],
            (dp, seq_of(other_x(step), z)),
        )

    def out_core_sum(blocks):
        for block in blocks:
            oc(block).wait_recv()
            out_x[block] = (out_term[c, block].astype(F32) + out_core[block].astype(F32)).astype(BF)
        for step in range(1, 4):
            for block in blocks:
                @pl.when(other_x(step) == block)
                def _():
                    ox(step).start()

    def pass_one_pairs(i, carry):
        for slot in range(2):
            pass_one(i, slot)
        for slot in range(2):
            send_q(pair_of(i, slot))

        @pl.when(i == 0)
        def _():
            forward(2, 1)

        @pl.when(i == 1)
        def _():
            stats[0, 0] = statc[...].T[:16]
            for d in range(REACH, 0, -1):
                stat_copy(0, d).start()
            forward(3, 0)
            out_terms(B, 4 * B, (1, 2))

        return carry

    lax.fori_loop(0, PAIRS // 2, pass_one_pairs, 0)

    forward(3, 1)
    stats[1, 0] = statc[...].T[16:32]
    for d in range(REACH, 0, -1):
        stat_copy(1, d).start()
    out_terms(0, 2 * B, (0,))
    out_terms(4 * B, 2 * B, (3,))
    out_core_sum((1, 2))

    ntab_t[...] = ntab[...].T
    emb[...] = nn(hot[pl.ds(REACH * B, B), :], table[...])
    select(qtab, query, (REACH + 1) * B, B, REACH * B, True, HEAD_DIM ** (-0.5))

    for d in range(1, 4):
        gatt[pl.ds(d * B, B), :] = nt(cot_all[d], wo[...]).astype(BF)

    def tok(step, target):
        return remote(
            tok_sum.at[target], tok_in.at[step - 1], tok_send.at[step - 1], tok_recv.at[step - 1],
            (dp, seq_of(target, z)),
        )

    def oz_step(i):
        return lax.rem(2 * x + i - z + 8, 8)

    def oz(i):
        step = lax.max(oz_step(i), 1)
        return remote(
            out_z.at[i], out_z_in.at[step - 1], oz_send.at[i], oz_recv.at[step - 1], (dp, seq_of(x, 2 * x + i))
        )

    def oz_in(step):
        return remote(
            out_z.at[0], out_z_in.at[step - 1], oz_send.at[0], oz_recv.at[step - 1], (dp, seq_of(x, z))
        )

    part_rows = D // 16

    def zs(step, half):
        rows = pl.ds(half * part_rows, part_rows)
        at = 7 * half + step - 1
        return remote(
            z_out.at[other_z(step), rows], z_in.at[step - 1, rows], z_send.at[at], z_recv.at[at],
            (dp, seq_of(x, other_z(step))),
        )

    mine = lax.min(dp, PAIRS - 1)

    def fin(step, half):
        part = final.at[mine, pl.ds(half * part_rows, part_rows)]
        return remote(
            part, part, fin_send.at[7 * half + step - 1], fin_recv.at[half, mine], (other_dp(step), sq)
        )

    def out_fin():
        return remote(out_final, final.at[mine], of_send.at[0], of_recv.at[0], (dp, seq_of(3, z)))

    def fin_in(p, half):
        part = final.at[p, pl.ds(half * part_rows, part_rows)]
        return remote(part, part, fin_send.at[0], fin_recv.at[half, p], (p, sq))

    out_core_sum((0, 3))

    for copy in idp_copies:
        copy.wait_recv()

    def hot_of_all():
        return jnp.concatenate([hot_dp[i] for i in range(8)], axis=1)

    @pl.when(dp < PAIRS)
    def _():
        def hot_block(i, carry):
            owner = lax.rem(dp + i, 8)
            hot_dp[owner] = (token == ids_dp[i]).astype(BF)
            return carry

        lax.fori_loop(0, 8, hot_block, 0)

        for i in range(8):
            @pl.when(i != dp)
            def _():
                remote(q_out.at[0], q_in.at[i], q_send.at[0], q_recv.at[i], (mine, sq)).wait_recv()

        tok_sum[0] = nn(hot_of_all(), q_in[...].reshape(8 * B, B)).astype(BF)
        for step in range(1, 4):
            @pl.when(other_x(step) == 0)
            def _():
                tok(step, 0).start()

    for half in range(2):
        relay(3, half).wait_recv()
    gatt[pl.ds(REACH * B, B), :] = nt(cot_all[REACH], wo[...]).astype(BF)
    for d in range(1, REACH + 1):
        stat_copy(0, d).wait_recv()

    def oy(step):
        return remote(
            out_y.at[lax.min(other_y(step), 2)], out_y_in.at[step - 1], oy_send.at[step - 1], oy_recv.at[step - 1],
            (other_y(step) * 2 + c, sq),
        )

    def pass_two(i, slot):
        p = pair_of(i, slot)
        lanes = pl.ds(pl.multiple_of(p * B, B), B)
        k2 = stacked(keys[pl.ds(REACH * B, B), lanes])
        v2 = stacked(values[pl.ds(REACH * B, B), lanes])
        for d in range(REACH + 1):
            q, g = query[pl.ds(d * B, B), lanes], gatt[pl.ds(d * B, B), lanes]
            reach = seeing[:, pl.ds(d * B, B)]
            allowed = jnp.concatenate([reach < window_ref[2 * p], reach < window_ref[2 * p + 1]], axis=0)

            def spread(j):
                first = 8 * j + 2 * (2 * (i % 2) + slot)
                a = jnp.broadcast_to(stats[i // 2, d, pl.ds(first, 1), :], (B, B))
                b = jnp.broadcast_to(stats[i // 2, d, pl.ds(first + 1, 1), :], (B, B))
                return jnp.concatenate([a, b], axis=0)

            probs = jnp.exp(jnp.where(allowed, nt(k2, q) - spread(0), -1e30))
            ds = probs * (nt(v2, g) - spread(1))
            probs_s[slot, :, pl.ds(d * B, B)] = probs.astype(BF)
            ds_s[slot, :, pl.ds(d * B, B)] = ds.astype(BF)
        grad_value = picked(nn(probs_s[slot], gatt[:, lanes])).astype(BF)
        grad_key = unrope(picked(nn(ds_s[slot], query[:, lanes])), own_cos, own_sin).astype(BF)
        gv[:, lanes] = grad_value
        gk[:, lanes] = grad_key

        kv_out[p, 0] = grad_key
        kv_out[p, 1] = grad_value

    def send_kv(p):
        @pl.when(p != dp)
        def _():
            kv_copy(p).start()

        @pl.when(p == dp)
        def _():
            kv_in[dp] = kv_out[p]

    def pass_two_pairs(i, carry):
        @pl.when(i == 2)
        def _():
            for d in range(1, REACH + 1):
                stat_copy(1, d).wait_recv()

        for slot in range(2):
            pass_two(i, slot)
        for slot in range(2):
            send_kv(pair_of(i, slot))
        return carry

    lax.fori_loop(0, PAIRS // 2, pass_two_pairs, 0)

    for step in range(1, 4):
        ox(step).wait_recv()
    for row in range(3):
        total = out_x[x, row].astype(F32)
        for step in range(3):
            total += out_x_in[step, row].astype(F32)
        out_y[row] = total.astype(BF)
    for step in range(1, 4):
        @pl.when(other_y(step) < 3)
        def _():
            oy(step).start()

    grad_normed = nt(gq[...], wq[...]) + nt(gk[...], wk[...]) + nt(gv[...], wv[...])
    own = emb[...]
    inv = lax.rsqrt(jnp.mean(own * own, axis=1, keepdims=True) + EPSILON)
    scaled = own * inv
    gin_ref[...] = (
        inv * (grad_normed - scaled * jnp.mean(grad_normed * scaled, axis=1, keepdims=True))
    ).astype(BF)

    @pl.when(dp < PAIRS)
    def _():
        for i in range(8):
            @pl.when(i != dp)
            def _():
                remote(kv_out.at[0], kv_in.at[i], kv_send.at[0], kv_recv.at[i], (mine, sq)).wait_recv()
        hot_all = hot_of_all()
        tok_sum[1] = nn(hot_all, kv_in[:, 0].reshape(8 * B, B)).astype(BF)
        for step in range(1, 4):
            @pl.when(other_x(step) == 1)
            def _():
                tok(step, 1).start()

        tok_sum[2] = nn(hot_all, kv_in[:, 1].reshape(8 * B, B)).astype(BF)
        for step in range(1, 4):
            @pl.when(other_x(step) == 2)
            def _():
                tok(step, 2).start()

        for step in range(1, 4):
            oy(step).wait_recv()
        total = out_y[lax.min(y, 2)].astype(F32)
        for step in range(3):
            total += out_y_in[step].astype(F32)
        out_z[...] = total.astype(BF).reshape(2, D // 8, B)
        for i in range(2):
            @pl.when(oz_step(i) != 0)
            def _():
                oz(i).start()

        @pl.when(x < 3)
        def _():
            for step in range(1, 4):
                tok(step, lax.min(x, 2)).wait_recv()
            total = tok_sum[lax.min(x, 2)].astype(F32)
            for step in range(3):
                total += tok_in[step].astype(F32)
            z_out[...] = nn(ntab_t[...], total.astype(BF)).astype(BF).reshape(8, D // 8, B)
            for half in range(2):
                for step in (4, 3, 5, 2, 6, 1, 7):
                    zs(step, half).start()

        @pl.when(z // 2 == x)
        def _():
            for step in range(1, 8):
                oz_in(step).wait_recv()
            total = out_z[z % 2].astype(F32)
            for step in range(7):
                total += out_z_in[step].astype(F32)
            out_final[...] = total.astype(BF)

            @pl.when(x < 3)
            def _():
                out_fin().start()

            @pl.when(x == 3)
            def _():
                final[mine] = out_final[...]

        @pl.when(x < 3)
        def _():
            for half in range(2):
                rows = pl.ds(half * part_rows, part_rows)
                for step in range(1, 8):
                    zs(step, half).wait_recv()
                total = z_out[z, rows].astype(F32)
                for step in range(7):
                    total += z_in[step, rows].astype(F32)
                final[mine, rows] = total.astype(BF)
                for step in (4, 3, 5, 2, 6, 1, 7):
                    fin(step, half).start()

        @pl.when(x == 3)
        def _():
            @pl.when(z < 6)
            def _():
                out_fin().wait_recv()

            for half in range(2):
                for step in (4, 3, 5, 2, 6, 1, 7):
                    fin(step, half).start()

    for p in range(PAIRS):
        @pl.when(dp != p)
        def _():
            for half in range(2):
                fin_in(p, half).wait_recv()

    relays = [relay(step, half) for step in range(REACH) for half in range(2)]
    stat_copies = [stat_copy(part, d) for part in range(2) for d in range(1, REACH + 1)]
    for copy in id_copies + idp_copies + relays + stat_copies + [oc(block) for block in range(4)] + [ox(step) for step in range(1, 4)]:
        copy.wait_send()
    for p in range(PAIRS):
        @pl.when(p != dp)
        def _():
            q_copy(p).wait_send()
            kv_copy(p).wait_send()
    for step in range(1, 4):
        @pl.when(other_y(step) < 3)
        def _():
            oy(step).wait_send()

    @pl.when(dp < PAIRS)
    def _():
        for step in range(1, 4):
            @pl.when(other_x(step) < 3)
            def _():
                tok(step, lax.min(other_x(step), 2)).wait_send()
        for i in range(2):
            @pl.when(oz_step(i) != 0)
            def _():
                oz(i).wait_send()

        @pl.when(x < 3)
        def _():
            for half in range(2):
                for step in range(1, 8):
                    zs(step, half).wait_send()

        @pl.when((z // 2 == x) & (x < 3))
        def _():
            out_fin().wait_send()

        for half in range(2):
            for step in range(1, 8):
                fin(step, half).wait_send()


def finish(gin_ref, pieces_ref, gin_out, wg_out):
    gin_out[...] = gin_ref[...]
    for p in range(PAIRS):
        wg_out[:, pl.ds(p * B, B)] = pieces_ref[p].astype(F32)


def on_device(token_ids, cotangent, table, w_query, w_key, w_value, w_out, window):
    tables = [jnp.asarray(part) for part in rope_tables()]
    vmem = pl.BlockSpec(memory_space=pltpu.VMEM)
    hbm = pl.BlockSpec(memory_space=pl.ANY)
    smem = pl.BlockSpec(memory_space=pltpu.SMEM)
    dma = pltpu.SemaphoreType.DMA
    grad_input, pieces = pl.pallas_call(
        kernel,
        out_shape=(
            jax.ShapeDtypeStruct((B, D), BF),
            jax.ShapeDtypeStruct((PAIRS, D // 8, B), BF),
        ),
        in_specs=[vmem] + [hbm] * 6 + [smem] + [vmem] * 4,
        out_specs=(vmem, vmem),
        scratch_shapes=[
            pltpu.VMEM((2 * REACH + 1, 1, B), jnp.int32),
            pltpu.VMEM((8, 1, B), jnp.int32),
            pltpu.VMEM((REACH + 1, B, D), BF),
            pltpu.VMEM((VOCAB, D), BF),
            pltpu.VMEM((D, D), BF),
            pltpu.VMEM((D, D), BF),
            pltpu.VMEM((D, D), BF),
            pltpu.VMEM((D, D), BF),
            pltpu.VMEM((D, VOCAB), BF),
            pltpu.VMEM((VOCAB, D), BF),
            pltpu.VMEM((VOCAB, D), BF),
            pltpu.VMEM((VOCAB, D), BF),
            pltpu.VMEM((VOCAB, D), BF),
            pltpu.VMEM(((2 * REACH + 1) * B, VOCAB), BF),
            pltpu.VMEM((B, D), F32),
            pltpu.VMEM(((2 * REACH + 1) * B, B), F32),
            pltpu.VMEM(((2 * REACH + 1) * B, B), F32),
            pltpu.VMEM((B, SPAN), jnp.int32),
            pltpu.VMEM((B, SPAN), jnp.int32),
            pltpu.VMEM((SPAN, D), BF),
            pltpu.VMEM((SPAN, D), BF),
            pltpu.VMEM((SPAN, D), BF),
            pltpu.VMEM((SPAN, D), BF),
            pltpu.VMEM((B, D), BF),
            pltpu.VMEM((B, D), BF),
            pltpu.VMEM((B, D), BF),
            pltpu.VMEM((B, D), BF),
            pltpu.VMEM((B, B), F32),
            pltpu.VMEM((2, REACH + 1, 16, B), F32),
            pltpu.VMEM((2, 2 * B, SPAN), BF),
            pltpu.VMEM((2, 2 * B, SPAN), BF),
            pltpu.VMEM((8, VOCAB, B), BF),
            pltpu.VMEM((PAIRS, B, B), BF),
            pltpu.VMEM((PAIRS, 2, B, B), BF),
            pltpu.VMEM((8, B, B), BF),
            pltpu.VMEM((8, 2, B, B), BF),
            pltpu.VMEM((3, VOCAB, B), BF),
            pltpu.VMEM((3, VOCAB, B), BF),
            pltpu.VMEM((8, D // 8, B), BF),
            pltpu.VMEM((7, D // 8, B), BF),
            pltpu.VMEM((2, 4, 3, D // 4, B), BF),
            pltpu.VMEM((4, 3, D // 4, B), BF),
            pltpu.VMEM((4, 3, D // 4, B), BF),
            pltpu.VMEM((3, 3, D // 4, B), BF),
            pltpu.VMEM((3, D // 4, B), BF),
            pltpu.VMEM((3, D // 4, B), BF),
            pltpu.VMEM((2, D // 8, B), BF),
            pltpu.VMEM((7, D // 8, B), BF),
            pltpu.VMEM((D // 8, B), BF),
            dma((6,)), dma((8,)), dma((8,)), dma((7,)), dma((7,)), dma((8,)), dma((8,)), dma((8,)), dma((8,)),
            dma((PAIRS,)), dma((8,)), dma((PAIRS,)), dma((8,)), dma((3,)), dma((3,)), dma((14,)), dma((14,)),
            dma((14,)), dma((2, PAIRS)),
            dma((4,)), dma((4,)), dma((3,)), dma((3,)), dma((3,)), dma((3,)), dma((2,)), dma((7,)), dma((1,)), dma((1,)),
        ],
        compiler_params=pltpu.CompilerParams(collective_id=0, has_side_effects=True),
    )(token_ids, cotangent[0], table, w_query, w_key, w_value, w_out, window, *tables)
    grad_input, weight_grads = pl.pallas_call(
        finish,
        out_shape=(
            jax.ShapeDtypeStruct((B, D), BF),
            jax.ShapeDtypeStruct((D // 8, D), F32),
        ),
        in_specs=[vmem, vmem],
        out_specs=(vmem, vmem),
    )(grad_input, pieces)
    return (grad_input[None], weight_grads)


def solution(mesh):
    return jax.shard_map(
        on_device,
        mesh=mesh,
        in_specs=(P("dp", "seq"), P("dp", "seq", None), P(), P(), P(), P(), P(), P()),
        out_specs=(P("dp", "seq", None), P("seq", None)),
        check_vma=False,
    )
```

```python
import functools

import jax
import jax.numpy as jnp
import numpy as np
from jax import lax
from jax.experimental import pallas as pl
from jax.experimental.pallas import tpu as pltpu
from jax.sharding import PartitionSpec as P

D = 768
HEADS = 12
HEAD_DIM = 64
VOCAB = 256
WINDOW = 512
EPSILON = 1e-05
B = 128
SEQ_DEVS = 32
REACH = WINDOW // B
SPAN = (REACH + 1) * B
PAIRS = D // B
MESH = pl.DeviceIdType.MESH
BF = jnp.bfloat16
F32 = jnp.float32


def rope_tables():
    frequency = 10000.0 ** (-2.0 * np.arange(HEAD_DIM // 2) / HEAD_DIM)
    lane_frequency = np.tile(frequency, 4)[None, :]
    inside = np.arange(B)[:, None] * lane_frequency
    blocks = (np.arange(SEQ_DEVS) * B)[:, None] * lane_frequency
    return [
        np.asarray(part, np.float32)
        for part in (np.cos(inside), np.sin(inside), np.cos(blocks), np.sin(blocks))
    ]


def nn(a, b):
    return lax.dot_general(a, b, (((1,), (0,)), ((), ())), preferred_element_type=F32)


def nt(a, b):
    return lax.dot_general(a, b, (((1,), (1,)), ((), ())), preferred_element_type=F32)


def tn(a, b):
    return lax.dot_general(a, b, (((0,), (0,)), ((), ())), preferred_element_type=F32)


def swap_halves(x):
    lane = lax.broadcasted_iota(jnp.int32, x.shape, 1)
    first = (lane // (HEAD_DIM // 2)) % 2 == 0
    return jnp.where(first, pltpu.roll(x, B - HEAD_DIM // 2, 1), pltpu.roll(x, HEAD_DIM // 2, 1))


def rope(x, cosine, sine):
    return x * cosine + swap_halves(x) * sine


def unrope(x, cosine, sine):
    return x * cosine - swap_halves(x) * sine


def kernel(
    ids_ref, cot_hbm, table_hbm, wq_hbm, wk_hbm, wv_hbm, wo_hbm, window_ref, cr_ref, sr_ref, cb_ref, sb_ref,
    gin_ref, final,
    ids_all, ids_dp, cot_all, table, wq, wk, wv, wo, ntab_t, ntab, qtab, ktab, vtab, hot, emb, cosv, sinv, seen, seeing,
    keys, values, query, gatt, att, gq, gk, gv, statc, stats, probs_s, ds_s, hot_dp,
    q_out, kv_out, q_in, kv_in, tok_sum, tok_in, z_out, z_in,
    out_term, out_core, out_x, out_x_in, out_y, out_y_in, out_z, out_z_in, out_final,
    load_sem, ids_send, ids_recv, idp_send, idp_recv, cot_send, cot_recv, st_send, st_recv,
    q_send, q_recv, kv_send, kv_recv, tok_send, tok_recv, z_send, z_recv, fin_send, fin_recv,
    oc_send, oc_recv, ox_send, ox_recv, oy_send, oy_recv, oz_send, oz_recv, of_send, of_recv,
):
    dp = lax.axis_index("dp")
    sq = lax.axis_index("seq")
    x, z = sq // 8, sq % 8
    y, c = dp // 2, dp % 2
    base = sq * B

    loads = [
        pltpu.make_async_copy(src, dst, load_sem.at[i])
        for i, (src, dst) in enumerate(
            [(table_hbm, table), (cot_hbm, cot_all.at[0]), (wk_hbm, wk), (wv_hbm, wv), (wq_hbm, wq), (wo_hbm, wo)]
        )
    ]
    for load in loads:
        load.start()

    def seq_of(new_x, new_z):
        return new_x * 8 + new_z

    def shift(distance):
        return lax.rem(sq + distance + SEQ_DEVS, SEQ_DEVS)

    def other_dp(step):
        return lax.rem(dp + step, 8)

    def other_y(step):
        return lax.rem(y + step, 4)

    def other_x(step):
        return lax.rem(x + step, 4)

    def other_z(step):
        return lax.rem(z + step, 8)

    barrier = pltpu.get_barrier_semaphore()
    partners = [(dp, shift(d)) for d in (1, 2, 3, 4, -1, -2, -3, -4)]
    partners += [(other_dp(d), sq) for d in range(1, 8)]
    partners += [(dp, seq_of(other_x(d), z)) for d in range(1, 4)]
    partners += [(dp, seq_of(x, other_z(d))) for d in range(1, 8)]
    for partner in partners:
        pl.semaphore_signal(barrier, inc=1, device_id=partner, device_id_type=MESH)

    pl.semaphore_wait(barrier, len(partners))

    def remote(src, dst, send, recv, device):
        return pltpu.make_async_remote_copy(
            src_ref=src, dst_ref=dst, send_sem=send, recv_sem=recv, device_id=device, device_id_type=MESH
        )

    id_copies = []
    for i, d in enumerate((4, -4, 3, -3, 2, -2, 1, -1)):
        id_copies.append(remote(ids_ref, ids_all.at[d + REACH], ids_send.at[i], ids_recv.at[i], (dp, shift(-d))))
    idp_copies = []
    for d in range(1, 8):
        idp_copies.append(
            remote(ids_ref, ids_dp.at[8 - d], idp_send.at[d - 1], idp_recv.at[d - 1], (other_dp(d), sq))
        )

    def relay(step, half):
        rows = pl.ds(half * (B // 2), B // 2)
        source = cot_hbm.at[rows] if step == 0 else cot_all.at[step, rows]
        return remote(
            source, cot_all.at[step + 1, rows], cot_send.at[2 * step + half], cot_recv.at[2 * step + half],
            (dp, shift(-1)),
        )

    def forward(step, half):
        relay(step - 1, half).wait_recv()
        relay(step, half).start()

    for copy in id_copies:
        copy.start()
    relay(0, 0).start()
    relay(0, 1).start()
    for copy in idp_copies:
        copy.start()
    ids_all[REACH] = ids_ref[...]
    ids_dp[0] = ids_ref[...]

    lane_row = lax.broadcasted_iota(jnp.int32, (1, B), 1)
    sign = jnp.where((lane_row // (HEAD_DIM // 2)) % 2 == 0, -1.0, 1.0)

    def rope_block(i, carry):
        block = lax.rem(sq + i - REACH + SEQ_DEVS, SEQ_DEVS)
        cb = cb_ref[pl.ds(block, 1), :]
        sb = sb_ref[pl.ds(block, 1), :]
        rows = pl.ds(pl.multiple_of(i * B, B), B)
        cosv[rows, :] = cr_ref[...] * cb - sr_ref[...] * sb
        sinv[rows, :] = (sr_ref[...] * cb + cr_ref[...] * sb) * sign
        return carry

    lax.fori_loop(0, 2 * REACH + 1, rope_block, 0)

    loads[0].wait()
    rows_f = table[...].astype(F32)
    table_inv = lax.rsqrt(jnp.mean(rows_f * rows_f, axis=1, keepdims=True) + EPSILON)
    ntab[...] = (rows_f * table_inv).astype(BF)

    def project_table(w, out):
        def slab(j, carry):
            lanes = pl.ds(pl.multiple_of(j * 2 * B, B), 2 * B)
            out[:, lanes] = nn(ntab[...], w[:, lanes]).astype(BF)
            return carry

        lax.fori_loop(0, PAIRS // 2, slab, 0)

    loads[2].wait()
    project_table(wk, ktab)
    loads[3].wait()
    project_table(wv, vtab)
    forward(1, 0)
    loads[4].wait()
    project_table(wq, qtab)
    loads[5].wait()
    loads[1].wait()
    gatt[pl.ds(0, B), :] = nt(cot_all[0], wo[...]).astype(BF)

    far = 1 << 20
    dist = lax.broadcasted_iota(jnp.int32, (B, SPAN), 0) + WINDOW - lax.broadcasted_iota(jnp.int32, (B, SPAN), 1)
    col = lax.broadcasted_iota(jnp.int32, (B, SPAN), 1)
    seen[...] = jnp.where((dist >= 0) & (col >= WINDOW - base), dist, far)
    dist = col - lax.broadcasted_iota(jnp.int32, (B, SPAN), 0)
    seeing[...] = jnp.where((dist >= 0) & (col < SEQ_DEVS * B - base), dist, far)

    for copy in id_copies:
        copy.wait_recv()

    token = lax.broadcasted_iota(jnp.int32, (VOCAB, B), 0)

    def hot_rows(i, carry):
        hot[pl.ds(pl.multiple_of(i * B, B), B), :] = (token == ids_all[i]).astype(F32).T.astype(BF)
        return carry

    lax.fori_loop(0, 2 * REACH + 1, hot_rows, 0)

    def select(tab, out, first, to, count, rotated, scale):
        def slab(j, carry):
            lanes = pl.ds(pl.multiple_of(j * 2 * B, B), 2 * B)
            got = nn(hot[pl.ds(first, count), :], tab[:, lanes])
            for half in range(2):
                part = got[:, half * B : (half + 1) * B]
                if rotated:
                    part = rope(part, cosv[pl.ds(first, count), :], sinv[pl.ds(first, count), :])
                if scale != 1.0:
                    part = part * scale
                out[pl.ds(to, count), pl.ds(pl.multiple_of((2 * j + half) * B, B), B)] = part.astype(BF)
            return carry

        lax.fori_loop(0, PAIRS // 2, slab, 0)

    forward(1, 1)
    select(ktab, keys, 0, 0, SPAN, True, 1.0)
    select(vtab, values, 0, 0, SPAN, False, 1.0)
    select(qtab, query, REACH * B, 0, B, True, HEAD_DIM ** (-0.5))
    forward(2, 0)

    lane_one = lax.broadcasted_iota(jnp.int32, (1, B), 1)
    left = (lane_one < HEAD_DIM).astype(BF)
    right = (lane_one >= HEAD_DIM).astype(BF)

    def stacked(a):
        return jnp.concatenate([a * left, a * right], axis=0)

    def picked(a):
        return jnp.where(lane_one < HEAD_DIM, a[:B], a[B:])

    own_cos = cosv[pl.ds(REACH * B, B), :]
    own_sin = sinv[pl.ds(REACH * B, B), :]
    statc[...] = jnp.zeros_like(statc)

    def q_copy(p):
        return remote(q_out.at[p], q_in.at[dp], q_send.at[p], q_recv.at[dp], (p, sq))

    def kv_copy(p):
        return remote(kv_out.at[p], kv_in.at[dp], kv_send.at[p], kv_recv.at[dp], (p, sq))

    def stat_copy(part, d):
        at = REACH * part + d - 1
        return remote(stats.at[part, 0], stats.at[part, d], st_send.at[at], st_recv.at[at], (dp, shift(-d)))

    def pair_of(i, slot):
        return 3 + i if slot else 2 - i

    def pass_one(i, slot):
        p = pair_of(i, slot)
        lanes = pl.ds(pl.multiple_of(p * B, B), B)
        k, v = keys[:, lanes], values[:, lanes]
        scores = nt(stacked(query[pl.ds(0, B), lanes]), k)
        reach = seen[...]
        masked = jnp.concatenate(
            [
                jnp.where(reach < window_ref[2 * p], scores[:B], -1e30),
                jnp.where(reach < window_ref[2 * p + 1], scores[B:], -1e30),
            ],
            axis=0,
        )
        top = jnp.max(masked, axis=1, keepdims=True)
        weights = jnp.exp(masked - top)
        whole = jnp.sum(weights, axis=1, keepdims=True)
        probs = weights * (1.0 / whole)
        grad_probs = nt(stacked(gatt[pl.ds(0, B), lanes]), v)
        row_term = jnp.sum(probs * grad_probs, axis=1, keepdims=True)
        ds = (probs * (grad_probs - row_term)).astype(BF)
        att[:, lanes] = picked(nn(probs.astype(BF), v)).astype(BF)
        grad_query = picked(nn(ds, k)) * HEAD_DIM ** (-0.5)
        got = unrope(grad_query, own_cos, own_sin).astype(BF)
        gq[:, lanes] = got

        q_out[p] = got
        held = statc[...]
        for j, stat in enumerate((top + jnp.log(whole), row_term)):
            first = 16 * (i // 2) + 8 * j + 2 * (2 * (i % 2) + slot)
            held = jnp.where(lane_one == first, stat[:B], held)
            held = jnp.where(lane_one == first + 1, stat[B:], held)
        statc[...] = held


    def send_q(p):
        @pl.when(p != dp)
        def _():
            q_copy(p).start()

        @pl.when(p == dp)
        def _():
            q_in[dp] = q_out[p]

    def out_terms(first, count, blocks):
        att_t = att[:, pl.ds(first, count)].T

        def one_pair(p, carry):
            lanes = pl.ds(pl.multiple_of(p * B, B), B)
            got = nn(att_t, cot_all[0, :, lanes]).astype(BF)
            for block in blocks:
                start = block * (D // 4) - first
                out_term[p % 2, block, p // 2] = got[start : start + D // 4]
            return carry

        lax.fori_loop(0, PAIRS, one_pair, 0)
        for block in blocks:
            oc(block).start()

    def oc(block):
        return remote(
            out_term.at[1 - c, block], out_core.at[block], oc_send.at[block], oc_recv.at[block],
            (y * 2 + 1 - c, sq),
        )

    def ox(step):
        return remote(
            out_x.at[other_x(step)], out_x_in.at[step - 1], ox_send.at[step - 1], ox_recv.at[step - 1],
            (dp, seq_of(other_x(step), z)),
        )

    def out_core_sum(blocks):
        for block in blocks:
            oc(block).wait_recv()
            out_x[block] = (out_term[c, block].astype(F32) + out_core[block].astype(F32)).astype(BF)
        for step in range(1, 4):
            for block in blocks:
                @pl.when(other_x(step) == block)
                def _():
                    ox(step).start()

    def pass_one_pairs(i, carry):
        for slot in range(2):
            pass_one(i, slot)
        for slot in range(2):
            send_q(pair_of(i, slot))

        @pl.when(i == 0)
        def _():
            forward(2, 1)

        @pl.when(i == 1)
        def _():
            stats[0, 0] = statc[...].T[:16]
            for d in range(REACH, 0, -1):
                stat_copy(0, d).start()
            forward(3, 0)
            out_terms(B, 4 * B, (1, 2))

        return carry

    lax.fori_loop(0, PAIRS // 2, pass_one_pairs, 0)

    stats[1, 0] = statc[...].T[16:32]
    for d in range(REACH, 0, -1):
        stat_copy(1, d).start()
    forward(3, 1)
    out_terms(0, D, (0, 3))
    out_core_sum((1, 2))

    ntab_t[...] = ntab[...].T
    emb[...] = nn(hot[pl.ds(REACH * B, B), :], table[...])
    select(qtab, query, (REACH + 1) * B, B, REACH * B, True, HEAD_DIM ** (-0.5))

    for d in range(1, 4):
        gatt[pl.ds(d * B, B), :] = nt(cot_all[d], wo[...]).astype(BF)

    def tok(step, target):
        return remote(
            tok_sum.at[target], tok_in.at[step - 1], tok_send.at[step - 1], tok_recv.at[step - 1],
            (dp, seq_of(target, z)),
        )

    def oz_step(i):
        return lax.rem(2 * x + i - z + 8, 8)

    def oz(i):
        step = lax.max(oz_step(i), 1)
        return remote(
            out_z.at[i], out_z_in.at[step - 1], oz_send.at[i], oz_recv.at[step - 1], (dp, seq_of(x, 2 * x + i))
        )

    def oz_in(step):
        return remote(
            out_z.at[0], out_z_in.at[step - 1], oz_send.at[0], oz_recv.at[step - 1], (dp, seq_of(x, z))
        )

    part_rows = D // 16

    def zs(step, half):
        rows = pl.ds(half * part_rows, part_rows)
        at = 7 * half + step - 1
        return remote(
            z_out.at[other_z(step), rows], z_in.at[step - 1, rows], z_send.at[at], z_recv.at[at],
            (dp, seq_of(x, other_z(step))),
        )

    mine = lax.min(dp, PAIRS - 1)

    def fin(step, half):
        part = final.at[mine, pl.ds(half * part_rows, part_rows)]
        return remote(
            part, part, fin_send.at[7 * half + step - 1], fin_recv.at[half, mine], (other_dp(step), sq)
        )

    def out_fin():
        return remote(out_final, final.at[mine], of_send.at[0], of_recv.at[0], (dp, seq_of(3, z)))

    def fin_in(p, half):
        part = final.at[p, pl.ds(half * part_rows, part_rows)]
        return remote(part, part, fin_send.at[0], fin_recv.at[half, p], (p, sq))

    out_core_sum((0, 3))

    for copy in idp_copies:
        copy.wait_recv()

    def hot_of_all():
        return jnp.concatenate([hot_dp[i] for i in range(8)], axis=1)

    @pl.when(dp < PAIRS)
    def _():
        def hot_block(i, carry):
            owner = lax.rem(dp + i, 8)
            hot_dp[owner] = (token == ids_dp[i]).astype(BF)
            return carry

        lax.fori_loop(0, 8, hot_block, 0)

        for i in range(8):
            @pl.when(i != dp)
            def _():
                remote(q_out.at[0], q_in.at[i], q_send.at[0], q_recv.at[i], (mine, sq)).wait_recv()

        tok_sum[0] = nn(hot_of_all(), q_in[...].reshape(8 * B, B)).astype(BF)
        for step in range(1, 4):
            @pl.when(other_x(step) == 0)
            def _():
                tok(step, 0).start()

    for half in range(2):
        relay(3, half).wait_recv()
    gatt[pl.ds(REACH * B, B), :] = nt(cot_all[REACH], wo[...]).astype(BF)
    for d in range(1, REACH + 1):
        stat_copy(0, d).wait_recv()

    def oy(step):
        return remote(
            out_y.at[lax.min(other_y(step), 2)], out_y_in.at[step - 1], oy_send.at[step - 1], oy_recv.at[step - 1],
            (other_y(step) * 2 + c, sq),
        )

    def pass_two(i, slot):
        p = pair_of(i, slot)
        lanes = pl.ds(pl.multiple_of(p * B, B), B)
        k2 = stacked(keys[pl.ds(REACH * B, B), lanes])
        v2 = stacked(values[pl.ds(REACH * B, B), lanes])
        for d in range(REACH + 1):
            q, g = query[pl.ds(d * B, B), lanes], gatt[pl.ds(d * B, B), lanes]
            reach = seeing[:, pl.ds(d * B, B)]
            allowed = jnp.concatenate([reach < window_ref[2 * p], reach < window_ref[2 * p + 1]], axis=0)

            def spread(j):
                first = 8 * j + 2 * (2 * (i % 2) + slot)
                a = jnp.broadcast_to(stats[i // 2, d, pl.ds(first, 1), :], (B, B))
                b = jnp.broadcast_to(stats[i // 2, d, pl.ds(first + 1, 1), :], (B, B))
                return jnp.concatenate([a, b], axis=0)

            probs = jnp.exp(jnp.where(allowed, nt(k2, q) - spread(0), -1e30))
            ds = probs * (nt(v2, g) - spread(1))
            probs_s[slot, :, pl.ds(d * B, B)] = probs.astype(BF)
            ds_s[slot, :, pl.ds(d * B, B)] = ds.astype(BF)
        grad_value = picked(nn(probs_s[slot], gatt[:, lanes])).astype(BF)
        grad_key = unrope(picked(nn(ds_s[slot], query[:, lanes])), own_cos, own_sin).astype(BF)
        gv[:, lanes] = grad_value
        gk[:, lanes] = grad_key

        kv_out[p, 0] = grad_key
        kv_out[p, 1] = grad_value

    def send_kv(p):
        @pl.when(p != dp)
        def _():
            kv_copy(p).start()

        @pl.when(p == dp)
        def _():
            kv_in[dp] = kv_out[p]

    def pass_two_pairs(i, carry):
        @pl.when(i == 2)
        def _():
            for d in range(1, REACH + 1):
                stat_copy(1, d).wait_recv()

        for slot in range(2):
            pass_two(i, slot)
        for slot in range(2):
            send_kv(pair_of(i, slot))
        return carry

    lax.fori_loop(0, PAIRS // 2, pass_two_pairs, 0)

    grad_normed = nt(gq[...], wq[...]) + nt(gk[...], wk[...]) + nt(gv[...], wv[...])
    own = emb[...]
    inv = lax.rsqrt(jnp.mean(own * own, axis=1, keepdims=True) + EPSILON)
    scaled = own * inv
    gin_ref[...] = (
        inv * (grad_normed - scaled * jnp.mean(grad_normed * scaled, axis=1, keepdims=True))
    ).astype(BF)

    for step in range(1, 4):
        ox(step).wait_recv()
    for row in range(3):
        total = out_x[x, row].astype(F32)
        for step in range(3):
            total += out_x_in[step, row].astype(F32)
        out_y[row] = total.astype(BF)
    for step in range(1, 4):
        @pl.when(other_y(step) < 3)
        def _():
            oy(step).start()

    @pl.when(dp < PAIRS)
    def _():
        for i in range(8):
            @pl.when(i != dp)
            def _():
                remote(kv_out.at[0], kv_in.at[i], kv_send.at[0], kv_recv.at[i], (mine, sq)).wait_recv()
        hot_all = hot_of_all()
        tok_sum[1] = nn(hot_all, kv_in[:, 0].reshape(8 * B, B)).astype(BF)
        for step in range(1, 4):
            @pl.when(other_x(step) == 1)
            def _():
                tok(step, 1).start()

        tok_sum[2] = nn(hot_all, kv_in[:, 1].reshape(8 * B, B)).astype(BF)
        for step in range(1, 4):
            @pl.when(other_x(step) == 2)
            def _():
                tok(step, 2).start()

        for step in range(1, 4):
            oy(step).wait_recv()
        total = out_y[lax.min(y, 2)].astype(F32)
        for step in range(3):
            total += out_y_in[step].astype(F32)
        out_z[...] = total.astype(BF).reshape(2, D // 8, B)
        for i in range(2):
            @pl.when(oz_step(i) != 0)
            def _():
                oz(i).start()

        @pl.when(x < 3)
        def _():
            for step in range(1, 4):
                tok(step, lax.min(x, 2)).wait_recv()
            total = tok_sum[lax.min(x, 2)].astype(F32)
            for step in range(3):
                total += tok_in[step].astype(F32)
            z_out[...] = nn(ntab_t[...], total.astype(BF)).astype(BF).reshape(8, D // 8, B)
            for half in range(2):
                for step in (4, 3, 5, 2, 6, 1, 7):
                    zs(step, half).start()

        @pl.when(z // 2 == x)
        def _():
            for step in range(1, 8):
                oz_in(step).wait_recv()
            total = out_z[z % 2].astype(F32)
            for step in range(7):
                total += out_z_in[step].astype(F32)
            out_final[...] = total.astype(BF)

            @pl.when(x < 3)
            def _():
                out_fin().start()

            @pl.when(x == 3)
            def _():
                final[mine] = out_final[...]

        @pl.when(x < 3)
        def _():
            for half in range(2):
                rows = pl.ds(half * part_rows, part_rows)
                for step in range(1, 8):
                    zs(step, half).wait_recv()
                total = z_out[z, rows].astype(F32)
                for step in range(7):
                    total += z_in[step, rows].astype(F32)
                final[mine, rows] = total.astype(BF)
                for step in (4, 3, 5, 2, 6, 1, 7):
                    fin(step, half).start()

        @pl.when(x == 3)
        def _():
            @pl.when(z < 6)
            def _():
                out_fin().wait_recv()

            for half in range(2):
                for step in (4, 3, 5, 2, 6, 1, 7):
                    fin(step, half).start()

    for p in range(PAIRS):
        @pl.when(dp != p)
        def _():
            for half in range(2):
                fin_in(p, half).wait_recv()

    relays = [relay(step, half) for step in range(REACH) for half in range(2)]
    stat_copies = [stat_copy(part, d) for part in range(2) for d in range(1, REACH + 1)]
    for copy in id_copies + idp_copies + relays + stat_copies + [oc(block) for block in range(4)] + [ox(step) for step in range(1, 4)]:
        copy.wait_send()
    for p in range(PAIRS):
        @pl.when(p != dp)
        def _():
            q_copy(p).wait_send()
            kv_copy(p).wait_send()
    for step in range(1, 4):
        @pl.when(other_y(step) < 3)
        def _():
            oy(step).wait_send()

    @pl.when(dp < PAIRS)
    def _():
        for step in range(1, 4):
            @pl.when(other_x(step) < 3)
            def _():
                tok(step, lax.min(other_x(step), 2)).wait_send()
        for i in range(2):
            @pl.when(oz_step(i) != 0)
            def _():
                oz(i).wait_send()

        @pl.when(x < 3)
        def _():
            for half in range(2):
                for step in range(1, 8):
                    zs(step, half).wait_send()

        @pl.when((z // 2 == x) & (x < 3))
        def _():
            out_fin().wait_send()

        for half in range(2):
            for step in range(1, 8):
                fin(step, half).wait_send()


def finish(gin_ref, pieces_ref, gin_out, wg_out):
    gin_out[...] = gin_ref[...]
    for p in range(PAIRS):
        wg_out[:, pl.ds(p * B, B)] = pieces_ref[p].astype(F32)


def on_device(token_ids, cotangent, table, w_query, w_key, w_value, w_out, window):
    tables = [jnp.asarray(part) for part in rope_tables()]
    vmem = pl.BlockSpec(memory_space=pltpu.VMEM)
    hbm = pl.BlockSpec(memory_space=pl.ANY)
    smem = pl.BlockSpec(memory_space=pltpu.SMEM)
    dma = pltpu.SemaphoreType.DMA
    grad_input, pieces = pl.pallas_call(
        kernel,
        out_shape=(
            jax.ShapeDtypeStruct((B, D), BF),
            jax.ShapeDtypeStruct((PAIRS, D // 8, B), BF),
        ),
        in_specs=[vmem] + [hbm] * 6 + [smem] + [vmem] * 4,
        out_specs=(vmem, vmem),
        scratch_shapes=[
            pltpu.VMEM((2 * REACH + 1, 1, B), jnp.int32),
            pltpu.VMEM((8, 1, B), jnp.int32),
            pltpu.VMEM((REACH + 1, B, D), BF),
            pltpu.VMEM((VOCAB, D), BF),
            pltpu.VMEM((D, D), BF),
            pltpu.VMEM((D, D), BF),
            pltpu.VMEM((D, D), BF),
            pltpu.VMEM((D, D), BF),
            pltpu.VMEM((D, VOCAB), BF),
            pltpu.VMEM((VOCAB, D), BF),
            pltpu.VMEM((VOCAB, D), BF),
            pltpu.VMEM((VOCAB, D), BF),
            pltpu.VMEM((VOCAB, D), BF),
            pltpu.VMEM(((2 * REACH + 1) * B, VOCAB), BF),
            pltpu.VMEM((B, D), F32),
            pltpu.VMEM(((2 * REACH + 1) * B, B), F32),
            pltpu.VMEM(((2 * REACH + 1) * B, B), F32),
            pltpu.VMEM((B, SPAN), jnp.int32),
            pltpu.VMEM((B, SPAN), jnp.int32),
            pltpu.VMEM((SPAN, D), BF),
            pltpu.VMEM((SPAN, D), BF),
            pltpu.VMEM((SPAN, D), BF),
            pltpu.VMEM((SPAN, D), BF),
            pltpu.VMEM((B, D), BF),
            pltpu.VMEM((B, D), BF),
            pltpu.VMEM((B, D), BF),
            pltpu.VMEM((B, D), BF),
            pltpu.VMEM((B, B), F32),
            pltpu.VMEM((2, REACH + 1, 16, B), F32),
            pltpu.VMEM((2, 2 * B, SPAN), BF),
            pltpu.VMEM((2, 2 * B, SPAN), BF),
            pltpu.VMEM((8, VOCAB, B), BF),
            pltpu.VMEM((PAIRS, B, B), BF),
            pltpu.VMEM((PAIRS, 2, B, B), BF),
            pltpu.VMEM((8, B, B), BF),
            pltpu.VMEM((8, 2, B, B), BF),
            pltpu.VMEM((3, VOCAB, B), BF),
            pltpu.VMEM((3, VOCAB, B), BF),
            pltpu.VMEM((8, D // 8, B), BF),
            pltpu.VMEM((7, D // 8, B), BF),
            pltpu.VMEM((2, 4, 3, D // 4, B), BF),
            pltpu.VMEM((4, 3, D // 4, B), BF),
            pltpu.VMEM((4, 3, D // 4, B), BF),
            pltpu.VMEM((3, 3, D // 4, B), BF),
            pltpu.VMEM((3, D // 4, B), BF),
            pltpu.VMEM((3, D // 4, B), BF),
            pltpu.VMEM((2, D // 8, B), BF),
            pltpu.VMEM((7, D // 8, B), BF),
            pltpu.VMEM((D // 8, B), BF),
            dma((6,)), dma((8,)), dma((8,)), dma((7,)), dma((7,)), dma((8,)), dma((8,)), dma((8,)), dma((8,)),
            dma((PAIRS,)), dma((8,)), dma((PAIRS,)), dma((8,)), dma((3,)), dma((3,)), dma((14,)), dma((14,)),
            dma((14,)), dma((2, PAIRS)),
            dma((4,)), dma((4,)), dma((3,)), dma((3,)), dma((3,)), dma((3,)), dma((2,)), dma((7,)), dma((1,)), dma((1,)),
        ],
        compiler_params=pltpu.CompilerParams(collective_id=0, has_side_effects=True),
    )(token_ids, cotangent[0], table, w_query, w_key, w_value, w_out, window, *tables)
    grad_input, weight_grads = pl.pallas_call(
        finish,
        out_shape=(
            jax.ShapeDtypeStruct((B, D), BF),
            jax.ShapeDtypeStruct((D // 8, D), F32),
        ),
        in_specs=[vmem, vmem],
        out_specs=(vmem, vmem),
    )(grad_input, pieces)
    return (grad_input[None], weight_grads)


def solution(mesh):
    return jax.shard_map(
        on_device,
        mesh=mesh,
        in_specs=(P("dp", "seq"), P("dp", "seq", None), P(), P(), P(), P(), P(), P()),
        out_specs=(P("dp", "seq", None), P("seq", None)),
        check_vma=False,
    )
```
